32 devices in a mesh: fsdp: 4 (over x, core), ctx: 2 (over y), tp: 4 (over z).
Axes of the slice: x: 2, y: 2, z: 4, core: 2. Of those that a mesh axis runs over, the one named last changes fastest.
Arguments:
- tokens: bfloat16 [4, 1024, 768], P('fsdp', 'ctx'), may hold values from -6 to 6
- parents: int32 [4, 2], P('fsdp'), may hold values from 0 to 0, as said below
- routes: int32 [4, 1024, 2], P('fsdp', 'ctx'), may hold values from 0 to 7, all different within a row; in each aligned block of 512 rows (0 to 511, 512 to 1023, ..., all dimensions but the last counted through in order) at most 192 rows name the same one
- gates: float32 [4, 1024, 2], P('fsdp', 'ctx'), may hold values from 0.2 to 1
- attn_gain: bfloat16 [2, 768], P(None, 'fsdp'), may hold values from 0.5 to 1.5
- ffn_gain: bfloat16 [2, 768], P(None, 'fsdp'), may hold values from 0.5 to 1.5
- qkv_weight: bfloat16 [2, 768, 3, 768], P(None, 'fsdp', None, 'tp'), may hold values from -0.21875 to 0.21875
- out_weight: bfloat16 [2, 768, 768], P(None, 'tp', 'fsdp'), may hold values from -0.875 to 0.875
- shared_in: bfloat16 [2, 768, 2, 2048], P(None, 'fsdp', None, 'tp'), may hold values from -0.21875 to 0.21875
- shared_out: bfloat16 [2, 2048, 768], P(None, 'tp', 'fsdp'), may hold values from -0.125 to 0.125
- expert_in: bfloat16 [2, 8, 768, 2, 2048], P(None, None, 'fsdp', None, 'tp'), may hold values from -0.21875 to 0.21875
- expert_out: bfloat16 [2, 8, 2048, 768], P(None, None, 'tp', 'fsdp'), may hold values from -0.125 to 0.125
- cotangent: bfloat16 [4, 1024, 768], P('fsdp', 'ctx'), may hold values from -6 to 6
Outputs:
- result: bfloat16 [4, 1024, 768], P('fsdp', 'ctx')
- tokens_grad: float32 [4, 1024, 768], P('fsdp', 'ctx')
- attn_gain_grad: float32 [2, 768], P(None, 'fsdp')
- ffn_gain_grad: float32 [2, 768], P(None, 'fsdp')
- qkv_grad: float32 [2, 768, 3, 768], P(None, 'fsdp', None, 'tp')
- out_grad: float32 [2, 768, 768], P(None, 'tp', 'fsdp')
- shared_in_grad: float32 [2, 768, 2, 2048], P(None, 'fsdp', None, 'tp')
- shared_out_grad: float32 [2, 2048, 768], P(None, 'tp', 'fsdp')
- expert_in_grad: float32 [2, 8, 768, 2, 2048], P(None, None, 'fsdp', None, 'tp')
- expert_out_grad: float32 [2, 8, 2048, 768], P(None, None, 'tp', 'fsdp')
The draws below stay inside these ranges and needn't reach their ends.
Inputs may be any that keep to these rules, and one draw needn't show every extreme that they name: parents[g, 0] = 0 marks the root segment; for every segment b >= 1, parents[g, b] < b; the last segment's parent is segment 2 - 2. `routes`: each token names 2 distinct experts; among the 512 rows of one device no expert is named more than 192 times.
All inputs are finite; a program needn't handle non-finite values.
Results may differ from the reference program's by a relative error of at most 0.039.
Values may be sent and summed in bfloat16 or wider, within the bound.
No kernel may reach another device: no remote copies, remote signals or barrier semaphores. Data moves between devices by JAX's collectives and lax.ppermute only.
A program may use at most 320 MiB of HBM per device.

```python
import math
import jax
import jax.numpy as jnp
import numpy as np
from jax import lax

D = 768
HEADS = 12
HEAD_DIM = 64
FF = 2048
EXPERTS = 8
TOP = 2
LAYERS = 2
TOK_DEV = 512
HF = 768
TREE = 1024
NBLK = 2
CAP = 192
GROUPS = 4


def draw_parents(key, part):
    block_ids = jnp.arange(NBLK, dtype=jnp.int32)
    limits = jnp.maximum(block_ids, 1)
    picks = jax.random.randint(key, (GROUPS, NBLK), 0, limits[None, :])
    picks = jnp.where(block_ids[None, :] == NBLK - 1, NBLK - 2, picks)
    return jnp.where(block_ids[None, :] > 0, picks, 0).astype(jnp.int32)


def block_levels(stream_key, shape, split, low, high):
    factor_of, own = 1.0, jax.random.fold_in(stream_key, 6)
    for axis_at, parts in split:
        steps = jnp.exp(jax.random.uniform(jax.random.fold_in(own, axis_at), (parts,), jnp.float32, low / len(split), high / len(split)))
        factor_of = factor_of * jnp.repeat(steps, shape[axis_at] // parts).reshape([-1 if axis == axis_at else 1 for axis in range(len(shape))])
    return factor_of


def routed_block(key, own, number, rows, number_of, top, bound, skew):
    order = jax.random.permutation(key, number_of)
    heavy_load, usual = load_shares(number_of, rows * top, bound, skew, True), load_shares(number_of, rows * top, bound, skew, False)
    places = jnp.arange(number_of)

    def named(lengths, turn):
        used = int((lengths > 0).sum())
        fixed = max(1, used // 4)
        passed = fixed + (places - fixed + turn * (used - fixed)) % max(1, number_of - fixed)
        return jnp.zeros((number_of,), jnp.int32).at[order[jnp.where(places < fixed, places, passed)]].set(jnp.asarray(lengths, jnp.int32))

    lengths = jnp.where(number % 4 == 0, named(heavy_load, number // 4), named(usual, number - number // 4 - 1))
    mixed = jax.random.permutation(jax.random.fold_in(own, 3), number_of)
    source_of, sink = mixed[0:number_of // 2 * 2:2], mixed[1:number_of // 2 * 2:2]
    slack = jnp.minimum(lengths[source_of] - 1, bound - lengths[sink]) // 2
    slack = jnp.where((source_of == order[0]) | (sink == order[0]) | (lengths[sink] == 0), 0, jnp.maximum(slack, 0))
    passed = jax.random.randint(jax.random.fold_in(own, 4), (number_of // 2,), 0, 1 << 20) % (slack + 1)
    lengths = lengths.at[source_of].add(-passed).at[sink].add(passed)
    members = jnp.searchsorted(jnp.cumsum(lengths), jnp.arange(rows * top), side="right").astype(jnp.int32)
    listing = members.reshape(top, rows).T
    listing = listing[jax.random.permutation(jax.random.fold_in(own, 1), rows)]
    turn = jax.random.randint(jax.random.fold_in(own, 2), (rows, 1), 0, top)
    return jnp.take_along_axis(listing, (jnp.arange(top)[None, :] + turn) % top, axis=1)


def load_shares(amount, total, bound, slope, full):
    weights = [(1 << 20) // math.isqrt(rank ** slope) + 1 for rank in range(1, amount + 1)]
    largest = bound if full else min(bound, max(-(-total // amount), total * weights[0] // sum(weights)))
    least = 1 if total - largest >= amount - 1 else 0
    counts, spare = [largest] + [least] * (amount - 1), total - largest - least * (amount - 1)
    while spare > 0:
        candidates = [i for i in range(1, amount) if counts[i] < largest] or [i for i in range(1, amount) if counts[i] < bound]
        whole, budget = sum([weights[i] for i in candidates]), spare
        for i in candidates:
            addition = min(bound - counts[i], max(1, budget * weights[i] // whole), spare)
            counts[i] = counts[i] + addition
            spare = spare - addition
    return np.array(counts)


def normal_values(stream_key, shape, spread, most, pieces=(), held_as=jnp.bfloat16):
    factor_of = block_levels(stream_key, shape, pieces, -0.22, 0.18) if pieces else 1.0
    values = jax.random.normal(stream_key, shape, jnp.float32) * spread * factor_of
    return jnp.minimum(jnp.maximum(values, -most), most).astype(held_as)


def setup_inputs(seed: int = 0) -> dict:
    arg_keys = jax.random.split(jax.random.key(seed), 14)
    tokens = normal_values(arg_keys[0], (GROUPS, TREE, D), 1.0, 6.0, ((0, 4), (1, 2)))
    parents = draw_parents(jax.random.fold_in(arg_keys[13], 71), 0)
    routes_keys = jax.random.split(jax.random.fold_in(arg_keys[2], 1), GROUPS * TREE // TOK_DEV)
    routes_turns = jax.random.permutation(jax.random.fold_in(arg_keys[2], 3), GROUPS * TREE // TOK_DEV)
    routes = jax.vmap(lambda own, number: routed_block(jax.random.fold_in(arg_keys[2], 2), own, number, TOK_DEV, EXPERTS, TOP, CAP, 1))(routes_keys, routes_turns).reshape((GROUPS, TREE, TOP))
    gates = jnp.clip(0.2 + 0.8 * jax.random.uniform(arg_keys[3], (GROUPS, TREE, TOP), jnp.float32) ** block_levels(arg_keys[3], (GROUPS, TREE, TOP), ((0, 4), (1, 2)), -0.2, 0.2), 0.2, 1.0)
    attn_gain = jnp.clip(1.0 + 0.1 * jax.random.normal(arg_keys[4], (LAYERS, D), jnp.float32), 0.5, 1.5).astype(jnp.bfloat16)
    ffn_gain = jnp.clip(1.0 + 0.1 * jax.random.normal(arg_keys[5], (LAYERS, D), jnp.float32), 0.5, 1.5).astype(jnp.bfloat16)
    qkv_weight = normal_values(arg_keys[6], (LAYERS, D, 3, HF), D ** -0.5, 0.21875, ((1, 4), (3, 4)))
    out_weight = normal_values(arg_keys[7], (LAYERS, HF, D), (HF // 16) ** -0.5, 0.875, ((1, 4), (2, 4)))
    shared_in = normal_values(arg_keys[8], (LAYERS, D, 2, FF), D ** -0.5, 0.21875, ((1, 4), (3, 4)))
    shared_out = normal_values(arg_keys[9], (LAYERS, FF, D), FF ** -0.5, 0.125, ((1, 4), (2, 4)))
    expert_in = normal_values(arg_keys[10], (LAYERS, EXPERTS, D, 2, FF), D ** -0.5, 0.21875, ((2, 4), (4, 4)))
    expert_out = normal_values(arg_keys[11], (LAYERS, EXPERTS, FF, D), FF ** -0.5, 0.125, ((2, 4), (3, 4)))
    cotangent = normal_values(arg_keys[12], (GROUPS, TREE, D), 1.0, 6.0, ((0, 4), (1, 2)))
    return dict(tokens=tokens, parents=parents, routes=routes, gates=gates, attn_gain=attn_gain, ffn_gain=ffn_gain, qkv_weight=qkv_weight, out_weight=out_weight, shared_in=shared_in, shared_out=shared_out, expert_in=expert_in, expert_out=expert_out, cotangent=cotangent)


EPS = 1e-06
SCALE = 0.125
MASKED = -1000000000.0
HIGH = lax.Precision.HIGHEST

@jax.custom_vjp
def low(v):
    return lax.optimization_barrier(v.astype(jnp.bfloat16)).astype(jnp.float32)

@jax.custom_vjp
def low_back(v):
    return v

def low_keep(v):
    return (low(v), None)

def low_pass(kept, grad):
    return (grad,)

def back_keep(v):
    return (v, None)

def back_low(kept, grad):
    return (low(grad),)
low.defvjp(low_keep, low_pass)
low_back.defvjp(back_keep, back_low)

def rms_scale(values, gain):
    inverse = lax.rsqrt(lax.optimization_barrier(jnp.mean(values * values, axis=-1, keepdims=True)) + EPS)
    return values * inverse * gain

def ancestry(parent_row):
    count = parent_row.shape[0]
    block_ids = jnp.arange(count, dtype=jnp.int32)
    step_map = ((parent_row[:, None] == block_ids[None, :]) & (block_ids[:, None] > 0)).astype(jnp.float32)
    identity = jnp.eye(count, dtype=jnp.float32)

    def climb(index, state):
        reach_now, on_path = state
        reach_now = jnp.dot(reach_now, step_map, precision=HIGH)
        return (reach_now, on_path + reach_now)
    return lax.fori_loop(0, count, climb, (identity, identity))[1]

def swiglu(normed, w_in, w_out):
    gate_up = low_back(jnp.einsum('gtd,dcf->gtcf', normed, w_in, precision=HIGH))
    hidden = low(jax.nn.silu(gate_up[:, :, 0]) * gate_up[:, :, 1])
    return low_back(jnp.einsum('gtf,fd->gtd', hidden, w_out, precision=HIGH))

def path_attention(queries, keys, values, ancestors):
    tree_len = keys.shape[0]
    count = ancestors.shape[0]
    block = tree_len // count
    key_pos = jnp.arange(tree_len, dtype=jnp.int32)

    def one_block(inputs):
        query_block, anc_row, start = inputs
        query_pos = start + jnp.arange(block, dtype=jnp.int32)
        allowed = (jnp.repeat(anc_row, block)[None, :] > 0.5) & (key_pos[None, :] <= query_pos[:, None])
        scores = jnp.einsum('qhd,khd->hqk', query_block, keys, precision=HIGH) * SCALE
        scores = low_back(jnp.where(allowed[None], scores, MASKED))
        probs = low(jax.nn.softmax(scores, axis=-1))
        return jnp.einsum('hqk,khd->qhd', probs, values, precision=HIGH)
    starts = jnp.arange(count, dtype=jnp.int32) * block
    blocks = queries.reshape(count, block, queries.shape[1], queries.shape[2])
    outputs = lax.map(jax.checkpoint(one_block), (blocks, ancestors, starts))
    return outputs.reshape(queries.shape)

def tree_attention(inputs):
    return path_attention(inputs[0], inputs[1], inputs[2], inputs[3])

def block_layer(stream, ancestors, mixing, attn_gain, ffn_gain, qkv_w, out_w, sh_in, sh_out, ex_in, ex_out):
    groups = stream.shape[0]
    tree_len = stream.shape[1]
    normed = low(rms_scale(stream, attn_gain))
    qkv = low_back(low(jnp.einsum('gtd,dcf->gtcf', normed, qkv_w, precision=HIGH)))
    shaped = qkv.reshape(groups, tree_len, 3, HEADS, HEAD_DIM)
    attended = lax.map(tree_attention, (shaped[:, :, 0], shaped[:, :, 1], shaped[:, :, 2], ancestors))
    heads_out = low_back(low(attended.reshape(groups, tree_len, HEADS * HEAD_DIM)))
    mixed = stream + low_back(jnp.einsum('gtf,fd->gtd', heads_out, out_w, precision=HIGH))
    ffn_in = low(rms_scale(mixed, ffn_gain))
    branch = swiglu(ffn_in, sh_in, sh_out)
    for expert_id in range(EXPERTS):
        routed = jax.checkpoint(swiglu)(ffn_in, ex_in[expert_id], ex_out[expert_id])
        branch = branch + mixing[:, :, expert_id:expert_id + 1] * routed
    return mixed + branch

def reference(tokens, parents, routes, gates, attn_gain, ffn_gain, qkv_weight, out_weight, shared_in, shared_out, expert_in, expert_out, cotangent):
    ancestors = lax.map(ancestry, parents)
    chosen = routes[:, :, :, None] == jnp.arange(EXPERTS, dtype=jnp.int32)[None, None, None, :]
    mixing = lax.optimization_barrier(jnp.sum(jnp.where(chosen, gates[:, :, :, None], 0.0), axis=2))

    def forward(stream, gain_a, gain_b, w_qkv, w_out, w_shin, w_shout, w_exin, w_exout):
        for layer_id in range(LAYERS):
            stream = block_layer(stream, ancestors, mixing, gain_a[layer_id], gain_b[layer_id], w_qkv[layer_id], w_out[layer_id], w_shin[layer_id], w_shout[layer_id], w_exin[layer_id], w_exout[layer_id])
        return stream
    result, pullback = jax.vjp(forward, tokens.astype(jnp.float32), attn_gain.astype(jnp.float32), ffn_gain.astype(jnp.float32), qkv_weight.astype(jnp.float32), out_weight.astype(jnp.float32), shared_in.astype(jnp.float32), shared_out.astype(jnp.float32), expert_in.astype(jnp.float32), expert_out.astype(jnp.float32))
    grads = pullback(cotangent.astype(jnp.float32))
    return (result.astype(jnp.bfloat16), grads[0], grads[1], grads[2], grads[3], grads[4], grads[5], grads[6], grads[7], grads[8])
```

```python
import functools

import jax
import jax.numpy as jnp
from jax import lax
from jax.experimental import pallas as pl
from jax.experimental.pallas import tpu as pltpu
from jax.sharding import PartitionSpec as P

HEAD_DIM = 64
EPS = 1e-06
SCALE = 0.125
MASKED = -1000000000.0
F32 = jnp.float32
BF16 = jnp.bfloat16
VMEM_LIMIT = 56 << 20

NN = (((1,), (0,)), ((), ()))
NT = (((1,), (1,)), ((), ()))
TN = (((0,), (0,)), ((), ()))


def mm(a, b, dims=NN):
    return lax.dot_general(a, b, dims, preferred_element_type=F32)


def swap(values, axis, mask):
    count = lax.axis_size(axis)
    return lax.ppermute(values, axis, [(k, k ^ mask) for k in range(count)])


def gather_blocks(values):
    far = swap(values, "fsdp", 2)
    return [values, swap(values, "fsdp", 1), far, swap(far, "fsdp", 1)]


def swap_blocks(values, axis, block):
    take = lambda r: lax.slice_in_dim(values, r * block, (r + 1) * block, axis=axis)
    return jnp.concatenate([take(1), take(0), take(3), take(2)], axis=axis)


def to_relative(values, block):
    me = lax.axis_index("fsdp")
    cut = lambda v, lo, hi: lax.slice_in_dim(v, lo * block, hi * block, axis=v.ndim - 1)
    far = jnp.concatenate([cut(values, 2, 4), cut(values, 0, 2)], axis=-1)
    values = jnp.where((me & 2) > 0, far, values)
    return jnp.where((me & 1) > 0, swap_blocks(values, values.ndim - 1, block), values)


def tp_sum(part):
    part = part.astype(BF16)
    count = lax.axis_size("tp")
    half = part.shape[0] // 2
    bit = lax.axis_index("tp") & 1
    keep = lax.dynamic_slice_in_dim(part, bit * half, half, 0)
    give = lax.dynamic_slice_in_dim(part, (1 - bit) * half, half, 0)
    total = keep.astype(F32) + swap(give, "tp", 1).astype(F32)
    step = 2
    while step < count:
        sent = total.astype(BF16)
        total = sent.astype(F32) + swap(sent, "tp", step).astype(F32)
        step *= 2
    mine = total.astype(BF16)
    other = swap(mine, "tp", 1)
    first = jnp.where(bit == 0, mine, other)
    last = jnp.where(bit == 0, other, mine)
    return jnp.concatenate([first, last], axis=0).astype(F32)


def ctx_sum(part):
    count = lax.axis_size("ctx")
    total = part
    step = 1
    while step < count:
        sent = total.astype(BF16)
        total = sent.astype(F32) + swap(sent, "ctx", step).astype(F32)
        step *= 2
    return total.astype(F32)


def ctx_scatter(whole):
    count = lax.axis_size("ctx")
    parts = whole.reshape((count, whole.shape[0] // count) + whole.shape[1:])
    parts = lax.all_to_all(parts, "ctx", 0, 0, tiled=True)
    return jnp.sum(parts.astype(F32), axis=0)


def settle_plain(grad, axis):
    block = grad.shape[axis] // 4
    cut = lambda v, lo, hi: lax.slice_in_dim(v, lo * block, hi * block, axis=axis)
    grad = grad.astype(BF16)
    near = cut(grad, 0, 2).astype(F32) + swap(cut(grad, 2, 4), "fsdp", 2).astype(F32)
    near = near.astype(BF16)
    own = cut(near, 0, 1).astype(F32) + swap(cut(near, 1, 2), "fsdp", 1).astype(F32)
    return ctx_sum(own.astype(BF16))


def settle_experts(near, far, axis):
    block = near.shape[axis] // 2
    cut = lambda v, lo, hi: lax.slice_in_dim(v, lo * block, hi * block, axis=axis)
    got = swap(far, "fsdp", 2)
    own = (cut(near, 0, 1).astype(F32) + cut(got, 0, 1).astype(F32)).astype(BF16)
    give = (cut(near, 1, 2).astype(F32) + cut(got, 1, 2).astype(F32)).astype(BF16)
    other = swap(give, "fsdp", 1)
    own, other = ctx_sum(own), ctx_sum(other)
    core = lax.axis_index("fsdp") & 1
    first = jnp.where(core == 0, own, other)
    last = jnp.where(core == 0, other, own)
    return jnp.concatenate([first, last], axis=0)


def allowed_of(base_ref, path_ref, rows, tree_len):
    query_pos = (
        base_ref[0]
        + pl.program_id(0) * rows
        + lax.broadcasted_iota(jnp.int32, (rows, tree_len), 0)
    )
    key_pos = lax.broadcasted_iota(jnp.int32, (rows, tree_len), 1)
    return (key_pos <= query_pos) & (path_ref[...] > 0.5)


def softmax_of(query, key, allowed):
    scores = jnp.where(allowed, mm(query, key, NT) * SCALE, MASKED)
    expo = jnp.exp(scores - jnp.max(scores, axis=-1, keepdims=True))
    return expo * (1.0 / jnp.sum(expo, axis=-1, keepdims=True))


def attend_kernel(base_ref, path_ref, q_ref, k_ref, v_ref, out_ref):
    rows, width = q_ref.shape
    allowed = allowed_of(base_ref, path_ref, rows, k_ref.shape[0])
    outs = []
    for head in range(width // HEAD_DIM):
        cols = slice(head * HEAD_DIM, (head + 1) * HEAD_DIM)
        probs = softmax_of(q_ref[:, cols], k_ref[:, cols], allowed).astype(BF16)
        outs.append(mm(probs, v_ref[:, cols]))
    out_ref[...] = jnp.concatenate(outs, axis=1).astype(BF16)


def attend_back_kernel(
    base_ref, path_ref, q_ref, k_ref, v_ref, do_ref, dq_ref, dk_ref, dv_ref, dk_acc, dv_acc
):
    rows, width = q_ref.shape
    allowed = allowed_of(base_ref, path_ref, rows, k_ref.shape[0])

    @pl.when(pl.program_id(0) == 0)
    def _():
        dk_acc[...] = jnp.zeros_like(dk_acc)
        dv_acc[...] = jnp.zeros_like(dv_acc)

    dqs, dks, dvs = [], [], []
    for head in range(width // HEAD_DIM):
        cols = slice(head * HEAD_DIM, (head + 1) * HEAD_DIM)
        query, key, value, d_out = q_ref[:, cols], k_ref[:, cols], v_ref[:, cols], do_ref[:, cols]
        probs = softmax_of(query, key, allowed)
        d_prob = mm(d_out, value, NT)
        weighted = jnp.sum(probs * d_prob, axis=-1, keepdims=True)
        d_scores = (probs * (d_prob - weighted)).astype(BF16)
        dqs.append(mm(d_scores, key) * SCALE)
        dks.append(mm(d_scores, query, TN))
        dvs.append(mm(probs.astype(BF16), d_out, TN))
    dq_ref[...] = jnp.concatenate(dqs, axis=1).astype(BF16)
    dk_acc[...] += jnp.concatenate(dks, axis=1)
    dv_acc[...] += jnp.concatenate(dvs, axis=1)

    @pl.when(pl.program_id(0) == pl.num_programs(0) - 1)
    def _():
        dk_ref[...] = (dk_acc[...] * SCALE).astype(BF16)
        dv_ref[...] = dv_acc[...].astype(BF16)


def attention_call(kernel, base, path, arrays, outs, scratch, flops):
    rows, width = arrays[0].shape
    tree_len = arrays[1].shape[0]
    tile = rows // 2
    tiled = pl.BlockSpec((tile, width), lambda t, *_: (t, 0))
    whole = pl.BlockSpec((tree_len, width), lambda t, *_: (0, 0))
    spec_of = lambda a: tiled if a.shape[0] == rows and a is not arrays[1] and a is not arrays[2] else whole
    return pl.pallas_call(
        kernel,
        out_shape=[jax.ShapeDtypeStruct((n, width), BF16) for n in outs],
        grid_spec=pltpu.PrefetchScalarGridSpec(
            num_scalar_prefetch=1,
            grid=(rows // tile,),
            in_specs=[pl.BlockSpec((1, tree_len), lambda t, *_: (0, 0))]
            + [spec_of(a) for a in arrays],
            out_specs=[tiled if at == 0 else whole for at in range(len(outs))],
            scratch_shapes=scratch,
        ),
        compiler_params=pltpu.CompilerParams(
            dimension_semantics=("arbitrary",), vmem_limit_bytes=VMEM_LIMIT
        ),
        cost_estimate=pl.CostEstimate(
            flops=flops * rows * tree_len * width,
            transcendentals=rows * tree_len * width // HEAD_DIM,
            bytes_accessed=2 * width * (2 * rows + 4 * tree_len),
        ),
    )(base, path, *arrays)


def one_hot_rows(pos_row, slots):
    hit = lax.broadcasted_iota(jnp.int32, (slots, pos_row.shape[1]), 0) == pos_row
    return jnp.where(hit, 1.0, 0.0).astype(BF16)


def one_hot_cols(pos_col, slots):
    hit = lax.broadcasted_iota(jnp.int32, (pos_col.shape[0], slots), 1) == pos_col
    return jnp.where(hit, 1.0, 0.0).astype(BF16)


def joined(refs, at):
    return jnp.concatenate([ref[at] for ref in refs], axis=0)


def expert_kernel(core_ref, tok_ref, row_ref, col_ref, mix_ref, *refs):
    ins, outs = refs[:4], refs[4:8]
    own_ref, sib_ref, x_ref, gate_ref, up_ref, acc = refs[8:]
    slots = x_ref.shape[1]

    @pl.when(pl.program_id(0) == 0)
    def _():
        acc[...] = jnp.zeros_like(acc)

    chosen = mm(one_hot_rows(row_ref[0], slots), tok_ref[...]).astype(BF16)
    x_ref[0] = chosen
    gate = mm(chosen, joined(ins, (0, 0)))
    up = mm(chosen, joined(ins, (0, 1)))
    gate_ref[0] = gate
    up_ref[0] = up
    hidden = (gate / (1.0 + jnp.exp(-gate)) * up).astype(BF16)
    rows = mm(hidden, joined(outs, 0), NT).astype(BF16)
    acc[...] += mix_ref[0] * mm(one_hot_cols(col_ref[0], slots), rows)

    @pl.when(pl.program_id(0) == pl.num_programs(0) - 1)
    def _():
        half = own_ref.shape[0]
        own_ref[...] = acc[:half, :]
        sib_ref[...] = acc[half:, :].astype(BF16)


def expert_back_kernel(core_ref, d_ref, row_ref, col_ref, mix_ref, x_ref, gate_ref, up_ref, *refs):
    ins, outs = refs[:4], refs[4:8]
    own_ref, sib_ref, gin_near, gin_far, gout_near, gout_far, acc = refs[8:]
    slots = x_ref.shape[1]

    @pl.when(pl.program_id(0) == 0)
    def _():
        acc[...] = jnp.zeros_like(acc)

    hit = lax.broadcasted_iota(jnp.int32, (slots, row_ref.shape[2]), 0) == row_ref[0]
    weight = jnp.sum(jnp.where(hit, mix_ref[0], 0.0), axis=1, keepdims=True)
    d_rows = (mm(jnp.where(hit, 1.0, 0.0).astype(BF16), d_ref[...]) * weight).astype(BF16)
    d_hidden = mm(d_rows, joined(outs, 0))
    gate, up = gate_ref[0], up_ref[0]
    sigmoid = 1.0 / (1.0 + jnp.exp(-gate))
    active = gate * sigmoid
    hidden = (active * up).astype(BF16)
    d_gate = (d_hidden * up * (sigmoid * (1.0 + gate * (1.0 - sigmoid)))).astype(BF16)
    d_up = (d_hidden * active).astype(BF16)
    half = gin_near.shape[2]
    chosen = x_ref[0]
    g_out = mm(d_rows, hidden, TN).astype(BF16)
    gout_near[0] = g_out[:half]
    gout_far[0] = g_out[half:]
    for at, d_part in enumerate((d_gate, d_up)):
        g_in = mm(chosen, d_part, TN).astype(BF16)
        gin_near[0, at] = g_in[:half]
        gin_far[0, at] = g_in[half:]
    d_x = mm(d_gate, joined(ins, (0, 0)), NT) + mm(d_up, joined(ins, (0, 1)), NT)
    acc[...] += mm(one_hot_cols(col_ref[0], slots), d_x.astype(BF16))

    @pl.when(pl.program_id(0) == pl.num_programs(0) - 1)
    def _():
        count = own_ref.shape[0]
        own_ref[...] = acc[:count, :]
        sib_ref[...] = acc[count:, :].astype(BF16)


def experts_call(kernel, core, tok, row, col, mix, kept, w_in, w_out, new, flops):
    count = row.shape[0]
    tokens, width = tok.shape
    _, _, block, hid = w_in[0].shape
    lead = lambda a: pl.BlockSpec((1,) + a.shape[1:], lambda e, c: (e,) + (0,) * (len(a.shape) - 1))
    whole = lambda s: pl.BlockSpec(s, lambda e, c: (0,) * len(s))
    mine = lambda a: pl.BlockSpec(
        (1,) + a.shape[1:], lambda e, c: (c[0] * count + e,) + (0,) * (a.ndim - 1)
    )
    half = (tokens // 2, width)
    shapes = [jax.ShapeDtypeStruct(half, F32), jax.ShapeDtypeStruct(half, BF16)] + new
    moved = 2 * count * 12 * block * hid + sum(
        s.size * s.dtype.itemsize for s in list(kept) + shapes + [tok]
    )
    return pl.pallas_call(
        kernel,
        out_shape=shapes,
        grid_spec=pltpu.PrefetchScalarGridSpec(
            num_scalar_prefetch=1,
            grid=(count,),
            in_specs=[whole(tok.shape), lead(row), lead(col), lead(mix)]
            + [lead(a) for a in kept]
            + [mine(a) for a in list(w_in) + list(w_out)],
            out_specs=[whole(half), whole(half)] + [lead(s) for s in new],
            scratch_shapes=[pltpu.VMEM((tokens, width), F32)],
        ),
        compiler_params=pltpu.CompilerParams(
            dimension_semantics=("arbitrary",), vmem_limit_bytes=VMEM_LIMIT
        ),
        cost_estimate=pl.CostEstimate(
            flops=flops, transcendentals=count * 384 * hid, bytes_accessed=moved
        ),
    )(core, tok, row, col, mix, *kept, *w_in, *w_out)


def norm_forward(values, gain):
    inverse = lax.rsqrt(jnp.mean(values * values, axis=-1, keepdims=True) + EPS)
    scaled = values * inverse
    return (scaled * gain, inverse)


def norm_backward(d_normed, scaled, inverse, gain):
    d_scaled = d_normed * gain
    d_values = inverse * (d_scaled - scaled * jnp.mean(d_scaled * scaled, axis=-1, keepdims=True))
    return (d_values, jnp.sum(d_normed * scaled, axis=0))


def ancestry(parent_row):
    count = parent_row.shape[0]
    block_ids = jnp.arange(count, dtype=jnp.int32)
    step_map = ((parent_row[:, None] == block_ids[None, :]) & (block_ids[:, None] > 0)).astype(F32)
    reach = on_path = jnp.eye(count, dtype=F32)
    for _ in range(count):
        reach = jnp.dot(reach, step_map, precision=lax.Precision.HIGHEST)
        on_path = on_path + reach
    return on_path


def shards(
    tokens,
    parents,
    routes,
    gates,
    attn_gain,
    ffn_gain,
    qkv_weight,
    out_weight,
    shared_in,
    shared_out,
    expert_in,
    expert_out,
    cotangent,
):
    rows_here, width = tokens.shape[1], tokens.shape[2]
    layers, experts = expert_in.shape[0], expert_in.shape[1]
    block = qkv_weight.shape[1]
    heads_width = qkv_weight.shape[3]
    hid = expert_in.shape[4]
    tree_len = rows_here * lax.axis_size("ctx")
    me = lax.axis_index("fsdp")
    core = me & 1
    per_core = experts // 2
    capacity = 2 * (3 * rows_here // 8)

    qkv_t = qkv_weight.transpose(0, 2, 1, 3)
    out_t = out_weight.transpose(0, 2, 1)
    sin_t = shared_in.transpose(0, 2, 1, 3)
    sout_t = shared_out.transpose(0, 2, 1)
    ein_t = expert_in.transpose(0, 1, 3, 2, 4)
    eout_t = expert_out.transpose(0, 1, 3, 2)

    gains = jnp.concatenate(
        gather_blocks(jnp.concatenate([attn_gain, ffn_gain], axis=0)), axis=1
    ).astype(F32)
    weights = []
    for at in range(layers):
        weights.append(
            dict(
                qkv=jnp.concatenate(gather_blocks(qkv_t[at]), axis=1),
                out=jnp.concatenate(gather_blocks(out_t[at]), axis=0),
                sin=jnp.concatenate(gather_blocks(sin_t[at]), axis=1),
                sout=jnp.concatenate(gather_blocks(sout_t[at]), axis=0),
                eout=gather_blocks(eout_t[at]),
                ein=gather_blocks(ein_t[at]),
            )
        )

    ancestors = ancestry(parents[0])
    segment = tree_len // ancestors.shape[0]
    start = lax.axis_index("ctx") * rows_here
    anc_row = lax.dynamic_slice_in_dim(ancestors, start // segment, 1, 0)
    path = jnp.repeat(anc_row, segment, axis=1)
    base = jnp.reshape(start, (1,)).astype(jnp.int32)

    chosen = routes[0][:, :, None] == jnp.arange(experts, dtype=jnp.int32)[None, None, :]
    mixing = jnp.sum(jnp.where(chosen, gates[0][:, :, None], 0.0), axis=1)
    mixing = jnp.concatenate([mixing, swap(mixing, "fsdp", 1)], axis=0)
    mixing = lax.dynamic_slice_in_dim(mixing, core * per_core, per_core, 1)
    named = mixing > 0.0
    pair = mixing.shape[0]
    earlier = (jnp.arange(pair)[:, None] > jnp.arange(pair)[None, :]).astype(BF16)
    slot = mm(earlier, named.astype(BF16)).astype(jnp.int32)
    slot = jnp.where(named, slot, -1).T
    mixing = mixing.T
    slot_row, slot_col = slot[:, None, :], slot[:, :, None]
    mix_row, mix_col = mixing[:, None, :], mixing[:, :, None]
    core_id = jnp.reshape(core, (1,)).astype(jnp.int32)

    with_sibling = lambda v: jnp.concatenate(
        [v, swap_blocks(swap(v, "fsdp", 1), 1, block)], axis=0
    )
    from_sibling = lambda v: swap_blocks(swap(v, "fsdp", 1), 1, block).astype(F32)
    sds = jax.ShapeDtypeStruct
    flops = 2 * per_core * capacity * width * hid

    stream = to_relative(tokens[0], block).astype(F32)
    saved = []
    for at in range(layers):
        w = weights[at]
        normed, inverse_a = norm_forward(stream, gains[at][None])
        normed = normed.astype(BF16)
        query, key, value = (mm(normed, w["qkv"][part]).astype(BF16) for part in range(3))
        both = lax.all_gather(jnp.concatenate([key, value], axis=1), "ctx", axis=0, tiled=True)
        keys, values = both[:, :heads_width], both[:, heads_width:]
        (heads_out,) = attention_call(
            attend_kernel, base, path, (query, keys, values), (rows_here,), [], 4
        )
        mixed = stream + tp_sum(mm(heads_out, w["out"], NT))
        ffn_in, inverse_b = norm_forward(mixed, gains[layers + at][None])
        ffn_in = ffn_in.astype(BF16)
        pair_in = with_sibling(ffn_in)
        gate = mm(ffn_in, w["sin"][0])
        up = mm(ffn_in, w["sin"][1])
        shared_hidden = (gate * jax.nn.sigmoid(gate) * up).astype(BF16)
        branch = mm(shared_hidden, w["sout"], NT)
        own, sib, x, e_gate, e_up = experts_call(
            expert_kernel,
            core_id,
            pair_in,
            slot_row,
            slot_col,
            mix_col,
            (),
            w["ein"],
            w["eout"],
            [
                sds((per_core, capacity, width), BF16),
                sds((per_core, capacity, hid), F32),
                sds((per_core, capacity, hid), F32),
            ],
            5 * flops,
        )
        branch = branch + own + from_sibling(sib)
        saved.append(
            (stream, inverse_a, normed, query, keys, values, heads_out, mixed, inverse_b, ffn_in)
            + (gate, up, shared_hidden, x, e_gate, e_up)
        )
        stream = mixed + tp_sum(branch)
    result = to_relative(stream.astype(BF16), block)

    d_stream = to_relative(cotangent[0], block).astype(F32)
    grads = [None] * layers
    for at in reversed(range(layers)):
        w = weights[at]
        (stream, inverse_a, normed, query, keys, values, heads_out, mixed, inverse_b, ffn_in) = (
            saved[at][:10]
        )
        gate, up, shared_hidden, x, e_gate, e_up = saved[at][10:]
        d_branch = d_stream.astype(BF16)
        pair_d = with_sibling(d_branch)
        d_shared = mm(d_branch, w["sout"])
        sigmoid = jax.nn.sigmoid(gate)
        active = gate * sigmoid
        d_gate = (d_shared * up * (sigmoid * (1.0 + gate * (1.0 - sigmoid)))).astype(BF16)
        d_up = (d_shared * active).astype(BF16)
        d_ffn = mm(d_gate, w["sin"][0], NT) + mm(d_up, w["sin"][1], NT)
        own, sib, gin_near, gin_far, gout_near, gout_far = experts_call(
            expert_back_kernel,
            core_id,
            pair_d,
            slot_row,
            slot_col,
            mix_row,
            (x, e_gate, e_up),
            w["ein"],
            w["eout"],
            [sds((per_core, 2, 2 * block, hid), BF16)] * 2
            + [sds((per_core, 2 * block, hid), BF16)] * 2,
            8 * flops,
        )
        d_ffn = tp_sum(d_ffn + own + from_sibling(sib))
        g_sout = mm(d_branch, shared_hidden, TN)
        g_sin = jnp.stack([mm(ffn_in, d_gate, TN), mm(ffn_in, d_up, TN)])
        d_mixed, g_gain_b = norm_backward(
            d_ffn, mixed * inverse_b, inverse_b, gains[layers + at][None]
        )
        d_mixed = d_mixed + d_stream
        d_attn = d_mixed.astype(BF16)
        g_out = mm(d_attn, heads_out, TN)
        d_heads = mm(d_attn, w["out"]).astype(BF16)
        d_query, d_keys, d_values = attention_call(
            attend_back_kernel,
            base,
            path,
            (query, keys, values, d_heads),
            (rows_here, tree_len, tree_len),
            [pltpu.VMEM((tree_len, heads_width), F32)] * 2,
            10,
        )
        d_both = ctx_scatter(jnp.concatenate([d_keys, d_values], axis=1)).astype(BF16)
        d_parts = (d_query, d_both[:, :heads_width], d_both[:, heads_width:])
        d_normed = tp_sum(sum(mm(d, w["qkv"][part], NT) for part, d in enumerate(d_parts)))
        g_qkv = jnp.stack([mm(normed, d, TN) for d in d_parts])
        d_input, g_gain_a = norm_backward(
            d_normed, stream * inverse_a, inverse_a, gains[at][None]
        )
        d_stream = d_input + d_mixed
        grads[at] = (
            g_gain_a,
            g_gain_b,
            settle_plain(g_qkv, 1),
            settle_plain(g_out, 0),
            settle_plain(g_sin, 1),
            settle_plain(g_sout, 0),
            settle_experts(gin_near, gin_far, 2),
            settle_experts(gout_near, gout_far, 1),
        )
    member = lambda number: jnp.stack([grads[at][number] for at in range(layers)])
    gain_grads = settle_plain(jnp.concatenate([member(0), member(1)], axis=0), 1)
    return (
        result[None],
        to_relative(d_stream, block)[None],
        gain_grads[:layers],
        gain_grads[layers:],
        member(2).transpose(0, 2, 1, 3),
        member(3).transpose(0, 2, 1),
        member(4).transpose(0, 2, 1, 3),
        member(5).transpose(0, 2, 1),
        member(6).transpose(0, 1, 3, 2, 4),
        member(7).transpose(0, 1, 3, 2),
    )


def solution(mesh):
    return jax.shard_map(
        shards,
        mesh=mesh,
        in_specs=(
            P("fsdp", "ctx", None),
            P("fsdp", None),
            P("fsdp", "ctx", None),
            P("fsdp", "ctx", None),
            P(None, "fsdp"),
            P(None, "fsdp"),
            P(None, "fsdp", None, "tp"),
            P(None, "tp", "fsdp"),
            P(None, "fsdp", None, "tp"),
            P(None, "tp", "fsdp"),
            P(None, None, "fsdp", None, "tp"),
            P(None, None, "tp", "fsdp"),
            P("fsdp", "ctx", None),
        ),
        out_specs=(
            P("fsdp", "ctx", None),
            P("fsdp", "ctx", None),
            P(None, "fsdp"),
            P(None, "fsdp"),
            P(None, "fsdp", None, "tp"),
            P(None, "tp", "fsdp"),
            P(None, "fsdp", None, "tp"),
            P(None, "tp", "fsdp"),
            P(None, None, "fsdp", None, "tp"),
            P(None, None, "tp", "fsdp"),
        ),
        check_vma=False,
    )
```

```python
import functools

import jax
import jax.numpy as jnp
from jax import lax
from jax.experimental import pallas as pl
from jax.experimental.pallas import tpu as pltpu
from jax.sharding import PartitionSpec as P

HEAD_DIM = 64
EPS = 1e-06
SCALE = 0.125
MASKED = -1000000000.0
F32 = jnp.float32
BF16 = jnp.bfloat16
MIB = 1 << 20
LIGHT = 1000
KEYS, QUERY, OUT, GAINS, PACK = 0, 384, 640, 832, 896

NN = (((1,), (0,)), ((), ()))
NT = (((1,), (1,)), ((), ()))
TN = (((0,), (0,)), ((), ()))


def mm(a, b, dims=NN):
    return lax.dot_general(a, b, dims, preferred_element_type=F32)


def sds(shape, dtype):
    return jax.ShapeDtypeStruct(tuple(shape), dtype)


def swap(values, axis, mask):
    count = lax.axis_size(axis)
    return lax.ppermute(values, axis, [(k, k ^ mask) for k in range(count)])


def after(value, dep):
    return lax.optimization_barrier((value, dep))[0]


def add(a, b):
    return (a.astype(F32) + b.astype(F32)).astype(BF16)


def gather_blocks(values):
    far = swap(values, "fsdp", 2)
    return [values, swap(values, "fsdp", 1), far, swap(far, "fsdp", 1)]


def tp_sum(halves, between):
    count = lax.axis_size("tp")
    chunks = len(halves) // 2
    totals = [add(k, swap(g, "tp", 1)) for k, g in zip(halves[:chunks], halves[chunks:])]
    totals = between(*totals)
    step = 2
    while step < count:
        totals = [add(total, swap(total, "tp", step)) for total in totals]
        step *= 2
    return list(totals) + [swap(total, "tp", 1) for total in totals]


def ctx_last(part):
    count = lax.axis_size("ctx")
    step = 1
    while step * 2 < count:
        part = add(part, swap(part, "ctx", step))
        step *= 2
    return part, swap(part, "ctx", step)


def call(kernel, scal, grid, ins, outs, scratch=(), flops=0, exps=0, alias=None, limit=32):
    def spec(item):
        shape, block, index = item[0].shape, item[1], item[2]
        if block == "any":
            return pl.BlockSpec(memory_space=pl.ANY)
        if block is None:
            return pl.BlockSpec(shape, lambda *_: (0,) * len(shape))
        return pl.BlockSpec(block, index)

    size = lambda a: a.size * a.dtype.itemsize
    moved = sum(size(i[0]) for i in list(ins) + list(outs) if i[1] != "any" and len(i) < 4)
    moved += sum(i[3] for i in list(ins) + list(outs) if len(i) > 3)
    return pl.pallas_call(
        kernel,
        out_shape=[o[0] for o in outs],
        grid_spec=pltpu.PrefetchScalarGridSpec(
            num_scalar_prefetch=1,
            grid=grid,
            in_specs=[spec(i) for i in ins],
            out_specs=[spec(o) for o in outs],
            scratch_shapes=list(scratch),
        ),
        compiler_params=pltpu.CompilerParams(
            dimension_semantics=("arbitrary",) * len(grid), vmem_limit_bytes=limit * MIB
        ),
        cost_estimate=pl.CostEstimate(flops=flops // LIGHT, transcendentals=0, bytes_accessed=moved // LIGHT),
        input_output_aliases=alias or {},
    )(scal, *[i[0] for i in ins])


def whole(a):
    return (a, None, None)


def tiled(a):
    return (a, (a.shape[0] // 2,) + a.shape[1:], lambda t, *_: (t,) + (0,) * (len(a.shape) - 1))


def joined(refs, *at):
    return jnp.concatenate([ref[at] if at else ref[...] for ref in refs], axis=0)


def gain_row(pack_refs, which):
    cols = jnp.concatenate([ref[:, GAINS - 64 : PACK] for ref in pack_refs], axis=0)
    at = lax.broadcasted_iota(jnp.int32, (8, 128), 1)
    pick = jnp.where(at == 64 + which, 1.0, 0.0).astype(BF16)
    return mm(pick, cols, NT)[:1]


def swap_pairs(values, block):
    two = 2 * block
    return jnp.concatenate(
        [pltpu.roll(values[:, at : at + two], block, 1) for at in (0, two)], axis=1
    )


def relative(values, me, block):
    two = 2 * block
    far = jnp.concatenate([values[:, two:], values[:, :two]], axis=1)
    values = jnp.where((me & 2) > 0, far, values)
    return jnp.where((me & 1) > 0, swap_pairs(values, block), values)


def arrived(bit, refs):
    chunks = len(refs) // 2
    mine, other = joined(refs[:chunks]), joined(refs[chunks:])
    return jnp.where(pl.program_id(0) == bit, mine, other).astype(F32)


def put_halves(tile, bit, values, refs):
    chunks = len(refs) // 2
    rows = values.shape[0] // chunks
    values = values.astype(BF16)

    @pl.when(tile == bit)
    def _():
        for at in range(chunks):
            refs[at][...] = values[at * rows : (at + 1) * rows]

    @pl.when(tile != bit)
    def _():
        for at in range(chunks):
            refs[chunks + at][...] = values[at * rows : (at + 1) * rows]


def half_shapes(rows, width, chunks):
    return [whole(sds((rows // 2 // chunks, width), BF16)) for _ in range(2 * chunks)]


def normed_of(values, gain):
    inverse = lax.rsqrt(jnp.mean(values * values, axis=-1, keepdims=True) + EPS)
    scaled = values * inverse
    return scaled, inverse, scaled * gain


def norm_back(d_normed, values, gain):
    scaled, inverse, _ = normed_of(values, gain)
    d_scaled = d_normed * gain
    mean = jnp.mean(d_scaled * scaled, axis=-1, keepdims=True)
    return inverse * (d_scaled - scaled * mean), jnp.sum(d_normed * scaled, axis=0, keepdims=True)


def order_kernel(scal, tok_ref, cot_ref, tok_out, cot_out, *, block):
    for src, dst in ((tok_ref, tok_out), (cot_ref, cot_out)):
        dst[...] = relative(src[...].astype(F32), scal[0], block).astype(BF16)


def project(stream, packs, normed_ref, q_ref, kv_ref):
    _, _, normed = normed_of(stream, gain_row(packs, 0))
    normed = normed.astype(BF16)
    normed_ref[...] = normed
    weight = joined(packs)
    kv_ref[...] = mm(normed, weight[:, KEYS:QUERY]).astype(BF16)
    q_ref[...] = mm(normed, weight[:, QUERY : QUERY + q_ref.shape[1]]).astype(BF16)


def first_kernel(scal, tok_ref, *refs):
    project(tok_ref[...].astype(F32), refs[:4], *refs[4:])


def next_kernel(scal, mixed_ref, *refs, parts):
    stream = mixed_ref[...] + arrived(scal[1], refs[:parts])
    packs, (stream_ref, *outs) = refs[parts : parts + 4], refs[parts + 4 :]
    stream_ref[...] = stream
    project(stream, packs, *outs)


def last_kernel(scal, mixed_ref, *refs, block):
    result = mixed_ref[...] + arrived(scal[1], refs[:-1])
    refs[-1][...] = relative(result, scal[0], block).astype(BF16)


def allowed_of(scal, path_ref, rows, tree_len):
    first = scal[3] + pl.program_id(0) * rows
    query_pos = first + lax.broadcasted_iota(jnp.int32, (rows, tree_len), 0)
    key_pos = lax.broadcasted_iota(jnp.int32, (rows, tree_len), 1)
    return (key_pos <= query_pos) & (path_ref[...] > 0.5)


def softmax_of(query, key, allowed):
    scores = jnp.where(allowed, mm(query, key, NT) * SCALE, MASKED)
    expo = jnp.exp(scores - jnp.max(scores, axis=-1, keepdims=True))
    return expo * (1.0 / jnp.sum(expo, axis=-1, keepdims=True))


def head_cols(width):
    return [slice(at, at + HEAD_DIM) for at in range(0, width, HEAD_DIM)]


def attend_kernel(scal, path_ref, q_ref, kv_ref, *refs):
    packs, heads_ref, halves = refs[:4], refs[4], refs[5:]
    rows, width = q_ref.shape
    allowed = allowed_of(scal, path_ref, rows, kv_ref.shape[0])
    outs = []
    for cols in head_cols(width):
        vals = slice(width + cols.start, width + cols.stop)
        probs = softmax_of(q_ref[:, cols], kv_ref[:, cols], allowed).astype(BF16)
        outs.append(mm(probs, kv_ref[:, vals]))
    heads = jnp.concatenate(outs, axis=1).astype(BF16)
    heads_ref[...] = heads
    weight = jnp.concatenate([ref[:, OUT : OUT + width] for ref in packs], axis=0)
    put_halves(pl.program_id(0), scal[1], mm(heads, weight, NT), halves)


def attend_back_kernel(scal, path_ref, q_ref, kv_ref, d_ref, heads_ref, *refs):
    packs, (dq_ref, gout_ref), (dkv_refs, scratch) = refs[:4], refs[4:6], (refs[6:-2], refs[-2:])
    dkv_acc, gout_acc = scratch
    rows, width = q_ref.shape
    tile = pl.program_id(0)
    allowed = allowed_of(scal, path_ref, rows, kv_ref.shape[0])

    @pl.when(tile == 0)
    def _():
        dkv_acc[...] = jnp.zeros_like(dkv_acc)
        gout_acc[...] = jnp.zeros_like(gout_acc)

    weight = jnp.concatenate([ref[:, OUT : OUT + width] for ref in packs], axis=0)
    d_heads = mm(d_ref[...], weight).astype(BF16)
    gout_acc[...] += mm(d_ref[...], heads_ref[...], TN)
    dqs, dks, dvs = [], [], []
    for cols in head_cols(width):
        vals = slice(width + cols.start, width + cols.stop)
        query, key, value, d_out = q_ref[:, cols], kv_ref[:, cols], kv_ref[:, vals], d_heads[:, cols]
        probs = softmax_of(query, key, allowed)
        d_prob = mm(d_out, value, NT)
        weighted = jnp.sum(probs * d_prob, axis=-1, keepdims=True)
        d_scores = (probs * (d_prob - weighted)).astype(BF16)
        dqs.append(mm(d_scores, key) * SCALE)
        dks.append(mm(d_scores, query, TN) * SCALE)
        dvs.append(mm(probs.astype(BF16), d_out, TN))
    dq_ref[...] = jnp.concatenate(dqs, axis=1).astype(BF16)
    dkv_acc[...] += jnp.concatenate(dks + dvs, axis=1)

    @pl.when(tile == pl.num_programs(0) - 1)
    def _():
        gout_ref[...] = gout_acc[...].astype(BF16)
        if len(dkv_refs) == 1:
            dkv_refs[0][...] = dkv_acc[...].astype(BF16)
        else:
            half = dkv_refs[0].shape[0]
            for at in range(2):
                part = dkv_acc[at * half : (at + 1) * half, :].astype(BF16)
                mine = scal[3] == at * half

                @pl.when(mine)
                def _():
                    dkv_refs[0][...] = part

                @pl.when(jnp.logical_not(mine))
                def _():
                    dkv_refs[1][...] = part


def project_back_kernel(scal, dq_ref, own_ref, got_ref, normed_ref, gout_ref, *refs, chunks):
    packs, halves, grads = refs[:4], refs[4 : 4 + 2 * chunks], refs[4 + 2 * chunks :]
    d_kv = (own_ref[...].astype(F32) + got_ref[...].astype(F32)).astype(BF16)
    d_q, normed = dq_ref[...], normed_ref[...]
    width = d_q.shape[1]
    weight = joined(packs)
    part = mm(d_kv, weight[:, KEYS:QUERY], NT) + mm(d_q, weight[:, QUERY : QUERY + width], NT)
    half = part.shape[0] // 2
    for at in range(2):
        put_halves(at, scal[1], part[at * half : (at + 1) * half], halves)
    g_kv, g_q, g_out = mm(normed, d_kv, TN), mm(normed, d_q, TN), gout_ref[...]
    rows = grads[0].shape[0]
    for at, ref in enumerate(grads):
        cut = slice(at * rows, (at + 1) * rows)
        ref[...] = jnp.zeros_like(ref)
        ref[:, KEYS:QUERY] = g_kv[cut].astype(BF16)
        ref[:, QUERY : QUERY + width] = g_q[cut].astype(BF16)
        ref[:, OUT : OUT + width] = g_out[cut]


def mix_kernel(scal, stream_ref, *refs, parts):
    mixed = stream_ref[...].astype(F32) + arrived(scal[1], refs[:parts])
    packs, (mixed_ref, in_ref) = refs[parts : parts + 4], refs[parts + 4 :]
    mixed_ref[...] = mixed
    in_ref[...] = normed_of(mixed, gain_row(packs, 1))[2].astype(BF16)


def shared_kernel(scal, in_ref, *refs):
    packs, (branch_ref, gate_ref, up_ref) = refs[:12], refs[12:]
    gate = mm(in_ref[...], joined(packs[:4]))
    up = mm(in_ref[...], joined(packs[4:8]))
    gate_ref[...] = gate
    up_ref[...] = up
    hidden = (gate / (1.0 + jnp.exp(-gate)) * up).astype(BF16)
    branch_ref[...] = mm(hidden, joined(packs[8:]), NT)


def glu_back(gate, up, d_hidden):
    sigmoid = 1.0 / (1.0 + jnp.exp(-gate))
    active = gate * sigmoid
    hidden = (active * up).astype(BF16)
    d_gate = (d_hidden * up * (sigmoid * (1.0 + gate * (1.0 - sigmoid)))).astype(BF16)
    return hidden, d_gate, (d_hidden * active).astype(BF16)


def shared_back_kernel(scal, d_ref, in_ref, gate_ref, up_ref, *refs):
    packs, (out_ref, *grad_refs) = refs[:12], refs[12:]
    hid = gate_ref.shape[1]
    cut = lambda at: joined(packs[4 * at : 4 * at + 4])
    d_branch, ffn_in = d_ref[...], in_ref[...]
    hidden, d_gate, d_up = glu_back(gate_ref[...], up_ref[...], mm(d_branch, cut(2)))
    out_ref[...] = mm(d_gate, cut(0), NT) + mm(d_up, cut(1), NT)
    grads = (mm(ffn_in, d_gate, TN), mm(ffn_in, d_up, TN), mm(d_branch, hidden, TN))
    rows = grad_refs[0].shape[0]
    for at, grad in enumerate(grads):
        for r, ref in enumerate(grad_refs):
            ref[:, at * hid : (at + 1) * hid] = grad[r * rows : (r + 1) * rows].astype(BF16)


def load_pair(own_ref, sib_ref, pair, block):
    half = own_ref.shape[0]
    pair[:half, :] = own_ref[...]
    pair[half:, :] = swap_pairs(sib_ref[...].astype(F32), block).astype(BF16)


def one_hot_cols(pos_col, slots):
    hit = lax.broadcasted_iota(jnp.int32, (pos_col.shape[0], slots), 1) == pos_col
    return jnp.where(hit, 1.0, 0.0).astype(BF16)


def hit_rows(pos_row, slots):
    return lax.broadcasted_iota(jnp.int32, (slots, pos_row.shape[1]), 0) == pos_row


def start_pair(own_ref, sib_ref, init_ref, pair, acc, block):
    @pl.when(pl.program_id(0) == 0)
    def _():
        half = own_ref.shape[0]
        load_pair(own_ref, sib_ref, pair, block)
        acc[:half, :] = init_ref[...]
        acc[half:, :] = jnp.zeros_like(init_ref)


def finish_pair(own_out, sib_out, acc):
    @pl.when(pl.program_id(0) == pl.num_programs(0) - 1)
    def _():
        half = own_out.shape[0]
        own_out[...] = acc[:half, :]
        sib_out[...] = acc[half:, :].astype(BF16)


def pack_kernel(scal, in_ref, out_ref, own_ref, first_ref, last_ref):
    third = first_ref.shape[2]
    own_ref[0, :2] = in_ref[0, 0]
    own_ref[0, 2] = out_ref[0, 0]
    first_ref[0] = own_ref[0, :, pl.ds(pl.multiple_of(scal[4] * third, third), third), :]
    last_ref[0] = own_ref[0, :, 2 * third :, :]


def expert_weights(scal, refs):
    def far(refs, part):
        straight, around, last = [ref[0, part] for ref in refs]
        low = jnp.where(scal[4] == 0, straight, around)
        middle = jnp.where(scal[4] == 0, around, straight)
        return [low, middle, last]

    return [
        jnp.concatenate(
            [refs[0][0, part], refs[1][0, part]] + far(refs[2:5], part) + far(refs[5:8], part), axis=0
        )
        for part in range(3)
    ]


def expert_kernel(scal, own_ref, sib_ref, init_ref, row_ref, col_ref, mix_ref, *refs, block):
    weights, (own_out, sib_out, x_ref, gate_ref, up_ref, acc, pair) = refs[:8], refs[8:]
    slots = x_ref.shape[1]
    start_pair(own_ref, sib_ref, init_ref, pair, acc, block)
    w_gate, w_up, w_out = expert_weights(scal, weights)
    hit = jnp.where(hit_rows(row_ref[0], slots), 1.0, 0.0).astype(BF16)
    chosen = mm(hit, pair[...]).astype(BF16)
    x_ref[0] = chosen
    gate = mm(chosen, w_gate)
    up = mm(chosen, w_up)
    gate_ref[0] = gate
    up_ref[0] = up
    hidden = (gate / (1.0 + jnp.exp(-gate)) * up).astype(BF16)
    rows = mm(hidden, w_out, NT).astype(BF16)
    acc[...] += mix_ref[0] * mm(one_hot_cols(col_ref[0], slots), rows)
    finish_pair(own_out, sib_out, acc)


def expert_back_kernel(
    scal, own_ref, sib_ref, init_ref, row_ref, col_ref, mix_ref, x_ref, gate_ref, up_ref, *refs,
    block, chunks
):
    weights, (own_out, sib_out), grads = refs[:8], refs[8:10], refs[10:-2]
    acc, pair = refs[-2:]
    slots = x_ref.shape[1]
    start_pair(own_ref, sib_ref, init_ref, pair, acc, block)
    w_gate, w_up, w_out = expert_weights(scal, weights)
    hit = hit_rows(row_ref[0], slots)
    weight = jnp.sum(jnp.where(hit, mix_ref[0], 0.0), axis=1, keepdims=True)
    hit = jnp.where(hit, 1.0, 0.0).astype(BF16)
    d_rows = (mm(hit, pair[...]) * weight).astype(BF16)
    hidden, d_gate, d_up = glu_back(gate_ref[0], up_ref[0], mm(d_rows, w_out))
    chosen = x_ref[0]
    step = pl.program_id(0)
    per_chunk = pl.num_programs(0) // chunks
    parts = (mm(chosen, d_gate, TN), mm(chosen, d_up, TN), mm(d_rows, hidden, TN))
    parts = [p.astype(BF16) for p in parts]
    for chunk in range(chunks):

        @pl.when(step // per_chunk == chunk)
        def _():
            for at in range(3):
                grads[2 * chunk][0, at] = parts[at][: 2 * block]
                grads[2 * chunk + 1][0, at] = parts[at][2 * block :]

    d_x = mm(d_gate, w_gate, NT) + mm(d_up, w_up, NT)
    acc[...] += mm(one_hot_cols(col_ref[0], slots), d_x.astype(BF16))
    finish_pair(own_out, sib_out, acc)


def join_kernel(scal, own_ref, got_ref, *halves, block):
    part = own_ref[...] + swap_pairs(got_ref[...].astype(F32), block)
    put_halves(pl.program_id(0), scal[1], part, halves)


def mix_back_kernel(scal, mixed_ref, next_ref, *refs, parts):
    packs, (d_ref, attn_ref, gain_ref) = refs[parts : parts + 4], refs[parts + 4 :]
    back, gain_grad = norm_back(arrived(scal[1], refs[:parts]), mixed_ref[...], gain_row(packs, 1))
    d_mixed = back + next_ref[...].astype(F32)
    d_ref[...] = d_mixed
    attn_ref[...] = d_mixed.astype(BF16)
    sum_tiles(gain_ref, gain_grad)


def sum_tiles(ref, value):
    value = jnp.broadcast_to(value, ref.shape)

    @pl.when(pl.program_id(0) == 0)
    def _():
        ref[...] = value

    @pl.when(pl.program_id(0) > 0)
    def _():
        ref[...] += value


def input_back_kernel(scal, stream_ref, mixed_ref, *refs, parts, block, final):
    packs, outs = refs[parts : parts + 4], refs[parts + 4 :]
    stream = stream_ref[...].astype(F32)
    back, gain_grad = norm_back(arrived(scal[1], refs[:parts]), stream, gain_row(packs, 0))
    d_stream = back + mixed_ref[...]
    if final:
        outs[0][...] = relative(d_stream, scal[0], block)
    else:
        outs[0][...] = d_stream
        outs[1][...] = d_stream.astype(BF16)
    sum_tiles(outs[-1], gain_grad)


def store_expert(in_ref, out_ref, gate, up, out):
    blocks = gate.shape[1] // 128
    for at, part in enumerate((gate, up)):
        for col in range(blocks):
            rows = pl.ds(col * 2 + at, part.shape[0], stride=2 * blocks)
            in_ref[0, 0, rows, :] = part[:, col * 128 : (col + 1) * 128]
    out_ref[0, 0] = out


def own_kernel(scal, part_ref, got_ref, *refs):
    give_ref, in_ref, out_ref = refs[-3:]
    half = give_ref.shape[2]
    total = [part_ref[0, at].astype(F32) + got_ref[0, at].astype(F32) for at in range(3)]
    for at in range(3):
        give_ref[0, at] = total[at][half:].astype(BF16)
    store_expert(in_ref, out_ref, *[t[:half] for t in total])


def other_kernel(scal, got_ref, *refs):
    store_expert(*refs[-2:], *[got_ref[0, at].astype(F32) for at in range(3)])

CHUNKS, PARTS = 2, (2, 1)
SLOTS = {
    "start": ["pack 0", ("experts", 0)],
    ("attend", 0): ["slots"],
    ("attend half", 0): [("experts", 0), "pack 1"],
    ("mixed", 0): [("experts", 0), "pack 1", ("experts", 1), "pack 2"],
    ("branch half", 0): [("experts", 1), "pack 2"],
    ("attend sum", 1): [("experts", 1)],
    (1, "experts"): [(1, 0)],
    (1, "project"): [(1, "packs")],
    (1, "attention sum"): [(1, 0), (1, "packs")],
    (0, "experts"): [(1, "packs"), (0, 0)],
    (0, "ffn sum"): [(0, "shared")],
    (0, "attention"): [(0, 0), (0, 1)],
    (0, "project"): [(1, 0), (1, "packs"), (0, "shared"), (0, "attention")],
    (0, "attention sum"): [(1, 0), (0, "shared"), (0, "attention")],
    (0, "input"): [(0, 0), (0, 1)],
}
TAIL = (
    ["gains", (0, "shared"), (0, "attention")],
    ["gains", (0, 0), (0, "attention")],
    ["gains", (0, 1)],
    [(0, 1)],
)


class Outs:
    def __init__(self, scal, layers, experts, block, hid):
        self.scal, self.per_core = scal, experts // 2
        self.shapes = (
            sds((layers, experts, block * 2 * hid // 128, 128), F32),
            sds((layers, experts, block, hid), F32),
        )
        self.held = None

    def put(self, kernel, ins, extra, layer, first, other):
        count = ins[0].shape[0]
        lead = lambda a: (a, (1,) + a.shape[1:], lambda e, s: (e, 0, 0, 0))
        place = lambda e, s: (layer, (s[2] ^ other) * self.per_core + first + e, 0, 0)
        moved = lambda s: count * s.size * 4 // (s.shape[0] * s.shape[1])
        slot = lambda s: (s, (1, 1) + s.shape[2:], place, moved(s))
        held = [] if self.held is None else [(h, "any", None) for h in self.held]
        base = 1 + len(ins)
        *rest, gin, gout = call(
            kernel,
            self.scal,
            (count,),
            [lead(i) for i in ins] + held,
            [lead(x) for x in extra] + [slot(s) for s in self.shapes],
            alias={base + at: len(extra) + at for at in range(len(held))},
            limit=16,
        )
        self.held = (gin, gout)
        return rest


def expert_flow(outs, near, far, layer, first):
    near, far = yield [near, far]
    near, got = yield [near, swap(far, "fsdp", 2)]
    part, got = yield list(ctx_last(add(near, got)))
    block = near.shape[2] // 2
    give = sds(near.shape[:2] + (block,) + near.shape[3:], BF16)
    (give,) = outs.put(own_kernel, (part, got), (give,), layer, first, 0)
    (got,) = yield [swap(give, "fsdp", 1)]
    outs.put(other_kernel, (got,), (), layer, first, 1)
    yield []


def pack_flow(place, name, parts):
    parts = yield list(parts)
    own, far, got, far_got = yield [parts[0], parts[2], swap(parts[1], "fsdp", 1), swap(parts[3], "fsdp", 1)]
    own, far = add(own, got), add(far, far_got)
    own, got = yield [own, swap(far, "fsdp", 2)]
    part, got = yield list(ctx_last(add(own, got)))
    place[name] = part.astype(F32) + got.astype(F32)
    yield []


def weight_flow(place, at, own, first, last):
    own, first, last = yield [own, first, last]
    own, sib, straight, last = yield [own, swap(own, "fsdp", 1), swap(first, "fsdp", 2), last]
    around, last = swap(straight, "ctx", 1), swap(last, "fsdp", 2)
    held = yield [straight, around, last, swap(straight, "fsdp", 1)]
    straight, around, last, cross = held
    place[at] = [own, sib, straight, around, last]
    place[at] += [cross, swap(around, "fsdp", 1), swap(last, "fsdp", 1)]
    yield []


def block_flow(place, at, own):
    (own,) = yield [own]
    own, far = yield [own, swap(own, "fsdp", 2)]
    place[at] = [own, swap(own, "fsdp", 1), far, swap(far, "fsdp", 1)]
    yield []


def ancestry(parent_row):
    count = parent_row.shape[0]
    block_ids = jnp.arange(count, dtype=jnp.int32)
    step_map = ((parent_row[:, None] == block_ids[None, :]) & (block_ids[:, None] > 0)).astype(F32)
    reach = on_path = jnp.eye(count, dtype=F32)
    for _ in range(count):
        reach = jnp.dot(reach, step_map, precision=lax.Precision.HIGHEST)
        on_path = on_path + reach
    return on_path


def shards(
    tokens,
    parents,
    routes,
    gates,
    attn_gain,
    ffn_gain,
    qkv_weight,
    out_weight,
    shared_in,
    shared_out,
    expert_in,
    expert_out,
    cotangent,
):
    rows, width = tokens.shape[1], tokens.shape[2]
    layers, experts = expert_in.shape[0], expert_in.shape[1]
    block, heads_width = qkv_weight.shape[1], qkv_weight.shape[3]
    hid = expert_in.shape[4]
    ctx = lax.axis_size("ctx")
    tree_len = rows * ctx
    me, here = lax.axis_index("fsdp"), lax.axis_index("ctx")
    core, bit = me & 1, lax.axis_index("tp") & 1
    half_at = here & 1
    per_core = experts // 2
    capacity = 2 * (3 * rows // 8)
    scal = jnp.stack([me, bit, core, here * rows, half_at]).astype(jnp.int32)

    def pack_attention(at):
        cols = [qkv_weight[at][:, part] for part in (1, 2, 0)]
        pad = jnp.zeros((block, OUT - QUERY - heads_width), BF16)
        gains = jnp.stack([attn_gain[at], ffn_gain[at]], axis=1)
        tail = jnp.zeros((block, PACK - GAINS - 2), BF16)
        return jnp.concatenate(cols + [pad, out_weight[at].T, gains, tail], axis=1)

    def pack_shared(at):
        return [shared_in[at].reshape(block, 2 * hid), shared_out[at].T]

    ein = lax.optimization_barrier(expert_in.transpose(0, 1, 3, 2, 4))
    eout = expert_out.transpose(0, 1, 3, 2)

    def pack_experts(at):
        third = block // 3
        whole_pack = sds((experts, 3, block, hid), BF16)
        part = sds((experts, 3, third, hid), BF16)
        lead = lambda a: (a, (1,) + a.shape[1:], lambda e, s: (e, 0, 0, 0))
        return call(
            pack_kernel,
            scal,
            (experts,),
            [
                (ein, (1, 1) + ein.shape[2:], lambda e, s: (at, e, 0, 0, 0)),
                (eout, (1, 1) + eout.shape[2:], lambda e, s: (at, e, 0, 0)),
            ],
            [lead(whole_pack), lead(part), lead(part)],
            limit=16,
        )

    ancestors = ancestry(parents[0])
    segment = tree_len // ancestors.shape[0]
    anc_row = lax.dynamic_slice_in_dim(ancestors, here * rows // segment, 1, 0)
    path = jnp.repeat(anc_row, segment, axis=1)

    chosen = routes[0][:, :, None] == jnp.arange(experts, dtype=jnp.int32)[None, None, :]
    mixing = jnp.sum(jnp.where(chosen, gates[0][:, :, None], 0.0), axis=1)
    mixing = jnp.concatenate([mixing, swap(mixing, "fsdp", 1)], axis=0)
    mixing = lax.dynamic_slice_in_dim(mixing, core * per_core, per_core, 1)
    named = mixing > 0.0
    pair = mixing.shape[0]
    earlier = (jnp.arange(pair)[:, None] > jnp.arange(pair)[None, :]).astype(BF16)
    slot = mm(earlier, named.astype(BF16)).astype(jnp.int32)
    slot = jnp.where(named, slot, -1).T
    mixing = mixing.T
    slot_row, slot_col = slot[:, None, :], slot[:, :, None]
    mix_row, mix_col = mixing[:, None, :], mixing[:, :, None]

    lead = lambda a: (
        a,
        (1,) + tuple(a.shape[1:]),
        lambda e, s: (e,) + (0,) * (len(a.shape) - 1),
    )

    matrix = 2 * rows * width
    expert_flops = 2 * per_core * capacity * width * hid
    pair_scratch = [pltpu.VMEM((2 * rows, width), F32), pltpu.VMEM((2 * rows, width), BF16)]
    halves = half_shapes(rows, width, CHUNKS)
    row_f32, row_bf16 = sds((rows, width), F32), sds((rows, width), BF16)

    flows, held = {}, {}

    def open_flow(name, flow):
        flows[name] = flow
        held[name] = next(flow)

    def slot(name, *values):
        names = SLOTS.get(name, ())
        values, arrays = lax.optimization_barrier((list(values), [held[n] for n in names]))
        for n, a in zip(names, arrays):
            if n == "slots":
                tables.extend(a)
            else:
                held[n] = flows[n].send(a)
        return values

    tables = []

    def finish(*names):
        for name in names:
            held[name] = flows[name].send(held[name])

    small, routed = {}, {}
    open_flow("pack 0", block_flow(small, 0, pack_attention(0)))
    for at in range(layers):
        open_flow(("experts", at), weight_flow(routed, at, *pack_experts(at)))
    open_flow("pack 1", block_flow(small, 1, jnp.concatenate(pack_shared(0), axis=1)))
    rest = [pack_attention(at) for at in range(1, layers)]
    rest = [v for pack in rest for v in (pack, jnp.zeros((block, 128), BF16))]
    rest += [v for at in range(1, layers) for v in pack_shared(at)]
    open_flow("pack 2", block_flow(small, 2, jnp.concatenate(rest, axis=1)))

    held["slots"] = [slot_row, slot_col, mix_row, mix_col]

    def attention_ins(at):
        if at == 0:
            return [whole(p) for p in small[0]]
        return [(p, (block, 1024), lambda *_: (0, at - 1)) for p in small[2]]

    def shared_ins(at):
        packs, first = (small[1], 0) if at == 0 else (small[2], 1024 * (layers - 1) // hid + 3 * at - 3)
        index = lambda which: lambda *_: (0, first + which)
        return [(p, (block, hid), index(which)) for which in range(3) for p in packs]

    def expert_ins(at):
        index = lambda e, s: (s[2] * per_core + e, 0, 0, 0)
        return [(a, (1,) + a.shape[1:], index) for a in routed[at]]

    stream, cot = call(
        functools.partial(order_kernel, block=block),
        scal,
        (2,),
        [tiled(tokens[0]), tiled(cotangent[0])],
        [tiled(row_bf16)] * 2,
    )
    finish("pack 0")
    slot("start")

    saved = []
    mixed = arrivals = None
    for at in range(layers):
        outs = [
            tiled(row_bf16),
            tiled(sds((rows, heads_width), BF16)),
            tiled(sds((rows, 2 * heads_width), BF16)),
        ]
        weights = attention_ins(at)
        if at == 0:
            normed, query, kv = call(
                first_kernel, scal, (2,), [tiled(stream)] + weights, outs, flops=matrix * 576
            )
        else:
            stream, normed, query, kv = call(
                functools.partial(next_kernel, parts=len(arrivals)),
                scal,
                (2,),
                [tiled(mixed)] + [whole(a) for a in arrivals] + weights,
                [tiled(row_f32)] + outs,
                flops=matrix * 576,
            )
        (kv,) = slot(("project", at), kv)
        kv = lax.all_gather(kv, "ctx", axis=0, tiled=True)
        heads, *part = call(
            attend_kernel,
            scal,
            (2,),
            [whole(path), tiled(query), whole(kv)] + weights,
            [tiled(sds((rows, heads_width), BF16))] + halves,
            flops=4 * rows * tree_len * heads_width + matrix * heads_width,
            exps=rows * tree_len * heads_width // HEAD_DIM,
            limit=40,
        )
        part = slot(("attend", at), *part)
        arrivals = tp_sum(part, functools.partial(slot, ("attend half", at)))
        arrivals = slot(("attend sum", at), *arrivals)
        mixed, ffn_in = call(
            functools.partial(mix_kernel, parts=len(arrivals)),
            scal,
            (2,),
            [tiled(stream)] + [whole(a) for a in arrivals] + weights,
            [tiled(row_f32), tiled(row_bf16)],
        )
        sib_in = swap(ffn_in, "fsdp", 1)
        ffn_in, sib_in = slot(("mixed", at), ffn_in, sib_in)
        branch, gate, up = call(
            shared_kernel,
            scal,
            (2,),
            [tiled(ffn_in)] + shared_ins(at),
            [tiled(row_f32)] + [tiled(sds((rows, hid), F32))] * 2,
            flops=3 * matrix * hid,
            exps=rows * hid,
        )
        own, sib, x, e_gate, e_up = call(
            functools.partial(expert_kernel, block=block),
            scal,
            (per_core,),
            [whole(ffn_in), whole(sib_in), whole(branch)]
            + [lead(tables[at]) for at in (0, 1, 3)]
            + expert_ins(at),
            [whole(row_f32), whole(row_bf16), lead(sds((per_core, capacity, width), BF16))]
            + [lead(sds((per_core, capacity, hid), F32))] * 2,
            scratch=pair_scratch,
            flops=5 * expert_flops,
            exps=per_core * capacity * hid,
            limit=48,
        )
        own, sib = slot(("experts", at), own, sib)
        part = call(
            functools.partial(join_kernel, block=block),
            scal,
            (2,),
            [tiled(own), tiled(swap(sib, "fsdp", 1))],
            halves,
        )
        saved.append(
            (stream, normed, query, kv, heads, mixed, ffn_in, gate, up, x, e_gate, e_up)
        )
        part = slot(("join", at), *part)
        arrivals = tp_sum(part, functools.partial(slot, ("branch half", at)))
        arrivals = slot(("branch sum", at), *arrivals)
    (result,) = call(
        functools.partial(last_kernel, block=block),
        scal,
        (2,),
        [tiled(mixed)] + [whole(a) for a in arrivals],
        [tiled(row_bf16)],
    )

    outs = Outs(scal, layers, experts, block, hid)
    packed = {}
    gain_grads = [None] * (2 * layers)
    d_next, d_branch = cot, cot
    for at in reversed(range(layers)):
        stream, normed, query, kv, heads, mixed, ffn_in, gate, up, x, e_gate, e_up = saved[at]
        weights = attention_ins(at)
        sib_d = swap(d_branch, "fsdp", 1)
        d_ffn, *g_shared = call(
            shared_back_kernel,
            scal,
            (1,),
            [whole(a) for a in (d_branch, ffn_in, gate, up)] + shared_ins(at),
            [whole(row_f32)] + [whole(sds((block, 3 * hid), BF16))] * 4,
            flops=6 * matrix * hid,
            exps=rows * hid,
        )
        chunks = PARTS[at]
        size = per_core // chunks
        part_of = lambda chunk: (
            sds((size, 3, 2 * block, hid), BF16),
            (1, 3, 2 * block, hid),
            lambda e, s: (jnp.clip(e - chunk * size, 0, size - 1), 0, 0, 0),
        )
        own, sib, *grads = call(
            functools.partial(expert_back_kernel, block=block, chunks=chunks),
            scal,
            (per_core,),
            [whole(d_branch), whole(sib_d), whole(d_ffn)]
            + [lead(a) for a in (*tables[:3], x, e_gate, e_up)]
            + expert_ins(at),
            [whole(row_f32), whole(row_bf16)]
            + [part_of(chunk) for chunk in range(chunks) for _ in range(2)],
            scratch=pair_scratch,
            flops=8 * expert_flops,
            exps=per_core * capacity * hid,
            limit=56,
        )
        for chunk in range(chunks):
            near, far = grads[2 * chunk : 2 * chunk + 2]
            open_flow((at, chunk), expert_flow(outs, near, far, at, chunk * size))
        if at == 0:
            open_flow((0, "shared"), pack_flow(packed, (0, "shared"), g_shared))
        own, sib = slot((at, "experts"), own, sib)
        part = call(
            functools.partial(join_kernel, block=block),
            scal,
            (2,),
            [tiled(own), tiled(swap(sib, "fsdp", 1))],
            halves,
        )
        part = slot((at, "join"), *part)
        arrivals = tp_sum(part, functools.partial(slot, (at, "ffn half")))
        arrivals = slot((at, "ffn sum"), *arrivals)
        d_mixed, d_attn, gain = call(
            functools.partial(mix_back_kernel, parts=len(arrivals)),
            scal,
            (2,),
            [tiled(mixed), tiled(d_next)] + [whole(a) for a in arrivals] + weights,
            [tiled(row_f32), tiled(row_bf16), whole(sds((8, width), F32))],
        )
        gain_grads[layers + at] = gain[:1]
        kv_shape = sds((rows, 2 * heads_width), BF16)
        kv_outs = [kv_shape] * 2 if ctx == 2 else [sds((tree_len, 2 * heads_width), BF16)]
        dq, g_out, *dkv = call(
            attend_back_kernel,
            scal,
            (2,),
            [whole(path), tiled(query), whole(kv), tiled(d_attn), tiled(heads)] + weights,
            [tiled(sds((rows, heads_width), BF16)), whole(sds((width, heads_width), BF16))]
            + [whole(k) for k in kv_outs],
            scratch=[
                pltpu.VMEM((tree_len, 2 * heads_width), F32),
                pltpu.VMEM((width, heads_width), F32),
            ],
            flops=10 * rows * tree_len * heads_width + 2 * matrix * heads_width,
            exps=rows * tree_len * heads_width // HEAD_DIM,
            limit=56,
        )
        dq, *dkv = slot((at, "attention"), dq, *dkv)
        if ctx == 2:
            kv_own, kv_got = dkv[0], swap(dkv[1], "ctx", 1)
        else:
            parts = dkv[0].reshape((ctx, rows) + dkv[0].shape[1:])
            parts = lax.all_to_all(parts, "ctx", 0, 0, tiled=True)
            kv_own, kv_got = jnp.sum(parts.astype(F32), axis=0), jnp.zeros(kv_shape.shape, F32)
        *part, g0, g1, g2, g3 = call(
            functools.partial(project_back_kernel, chunks=CHUNKS),
            scal,
            (1,),
            [whole(a) for a in (dq, kv_own, kv_got, normed, g_out)] + weights,
            halves + [whole(sds((block, PACK), BF16))] * 4,
            flops=2 * matrix * 576,
        )
        g_attention = [g0, g1, g2, g3]
        if at == 0:
            open_flow((0, "attention"), pack_flow(packed, (0, "attention"), g_attention))
        else:
            both = [jnp.concatenate(g, axis=1) for g in zip(g_shared, g_attention)]
            open_flow((at, "packs"), pack_flow(packed, at, both))
        part = slot((at, "project"), *part)
        arrivals = tp_sum(part, functools.partial(slot, (at, "attention half")))
        arrivals = slot((at, "attention sum"), *arrivals)
        final = at == 0
        *rest, gain = call(
            functools.partial(
                input_back_kernel, parts=len(arrivals), block=block, final=final
            ),
            scal,
            (2,),
            [tiled(stream), tiled(d_mixed)] + [whole(a) for a in arrivals] + weights,
            [tiled(row_f32)] + ([] if final else [tiled(row_bf16)]) + [whole(sds((8, width), F32))],
        )
        gain_grads[at] = gain[:1]
        d_next, *rest = slot((at, "input"), *rest)
        if not final:
            (d_branch,) = rest
    gains = jnp.concatenate(gain_grads, axis=0).astype(BF16)
    cuts = [gains[:, r * block : (r + 1) * block] for r in range(4)]
    open_flow("gains", pack_flow(packed, "gains", cuts))
    finish("gains")
    for step in TAIL:
        finish(*step)
    gains = packed["gains"]
    later = [packed[at] for at in range(1, layers)]
    g_shared = jnp.stack([packed[0, "shared"]] + [p[:, : 3 * hid] for p in later])
    g_attention = jnp.stack([packed[0, "attention"]] + [p[:, 3 * hid :] for p in later])
    cut = lambda first: g_attention[:, :, first : first + heads_width]
    g_in, g_out = outs.held
    blocks = hid // 128
    g_in = g_in.reshape(layers * experts * block, blocks, 2, 128).transpose(0, 2, 1, 3)
    return (
        result[None],
        d_next[None],
        gains[:layers],
        gains[layers:],
        jnp.stack([cut(QUERY), cut(KEYS), cut(KEYS + heads_width)], axis=2),
        cut(OUT).transpose(0, 2, 1),
        g_shared[:, :, : 2 * hid].reshape(layers, block, 2, hid),
        g_shared[:, :, 2 * hid :].transpose(0, 2, 1),
        g_in.reshape(layers, experts, block, 2, hid),
        g_out.transpose(0, 1, 3, 2),
    )


def solution(mesh):
    return jax.shard_map(
        shards,
        mesh=mesh,
        in_specs=(
            P("fsdp", "ctx", None),
            P("fsdp", None),
            P("fsdp", "ctx", None),
            P("fsdp", "ctx", None),
            P(None, "fsdp"),
            P(None, "fsdp"),
            P(None, "fsdp", None, "tp"),
            P(None, "tp", "fsdp"),
            P(None, "fsdp", None, "tp"),
            P(None, "tp", "fsdp"),
            P(None, None, "fsdp", None, "tp"),
            P(None, None, "tp", "fsdp"),
            P("fsdp", "ctx", None),
        ),
        out_specs=(
            P("fsdp", "ctx", None),
            P("fsdp", "ctx", None),
            P(None, "fsdp"),
            P(None, "fsdp"),
            P(None, "fsdp", None, "tp"),
            P(None, "tp", "fsdp"),
            P(None, "fsdp", None, "tp"),
            P(None, "tp", "fsdp"),
            P(None, None, "fsdp", None, "tp"),
            P(None, None, "tp", "fsdp"),
        ),
        check_vma=False,
    )
```

```python
import functools

import jax
import jax.numpy as jnp
from jax import lax
from jax.experimental import pallas as pl
from jax.experimental.pallas import tpu as pltpu
from jax.sharding import PartitionSpec as P

HEAD_DIM = 64
EPS = 1e-06
SCALE = 0.125
MASKED = -1000000000.0
F32 = jnp.float32
BF16 = jnp.bfloat16
MIB = 1 << 20
LIGHT = 1000
KEYS, QUERY, OUT, GAINS, PACK = 0, 384, 640, 832, 896

NN = (((1,), (0,)), ((), ()))
NT = (((1,), (1,)), ((), ()))
TN = (((0,), (0,)), ((), ()))


def mm(a, b, dims=NN):
    return lax.dot_general(a, b, dims, preferred_element_type=F32)


def sds(shape, dtype):
    return jax.ShapeDtypeStruct(tuple(shape), dtype)


def swap(values, axis, mask):
    count = lax.axis_size(axis)
    return lax.ppermute(values, axis, [(k, k ^ mask) for k in range(count)])


def after(value, dep):
    return lax.optimization_barrier((value, dep))[0]


def add(a, b):
    return (a.astype(F32) + b.astype(F32)).astype(BF16)


def gather_blocks(values):
    far = swap(values, "fsdp", 2)
    return [values, swap(values, "fsdp", 1), far, swap(far, "fsdp", 1)]


def tp_sum(halves, between):
    count = lax.axis_size("tp")
    chunks = len(halves) // 2
    totals = [add(k, swap(g, "tp", 1)) for k, g in zip(halves[:chunks], halves[chunks:])]
    totals[0] = between(totals[0])[0]
    step = 2
    while step < count:
        totals = [add(total, swap(total, "tp", step)) for total in totals]
        step *= 2
    return list(totals) + [swap(total, "tp", 1) for total in totals]


def ctx_last(part):
    count = lax.axis_size("ctx")
    step = 1
    while step * 2 < count:
        part = add(part, swap(part, "ctx", step))
        step *= 2
    return part, swap(part, "ctx", step)


def call(
    kernel, scal, grid, ins, outs, scratch=(), flops=0, exps=0, alias=None, limit=32, light=LIGHT
):
    def spec(item):
        shape, block, index = item[0].shape, item[1], item[2]
        if block == "any":
            return pl.BlockSpec(memory_space=pl.ANY)
        if block is None:
            return pl.BlockSpec(shape, lambda *_: (0,) * len(shape))
        return pl.BlockSpec(block, index)

    size = lambda a: a.size * a.dtype.itemsize
    moved = sum(size(i[0]) for i in list(ins) + list(outs) if i[1] != "any" and len(i) < 4)
    moved += sum(i[3] for i in list(ins) + list(outs) if len(i) > 3)
    return pl.pallas_call(
        kernel,
        out_shape=[o[0] for o in outs],
        grid_spec=pltpu.PrefetchScalarGridSpec(
            num_scalar_prefetch=1,
            grid=grid,
            in_specs=[spec(i) for i in ins],
            out_specs=[spec(o) for o in outs],
            scratch_shapes=list(scratch),
        ),
        compiler_params=pltpu.CompilerParams(
            dimension_semantics=("arbitrary",) * len(grid), vmem_limit_bytes=limit * MIB
        ),
        cost_estimate=pl.CostEstimate(flops=flops // light, transcendentals=0, bytes_accessed=moved // light),
        input_output_aliases=alias or {},
    )(scal, *[i[0] for i in ins])


def whole(a):
    return (a, None, None)


def tiled(a):
    return (a, (a.shape[0] // 2,) + a.shape[1:], lambda t, *_: (t,) + (0,) * (len(a.shape) - 1))


def joined(refs, *at):
    return jnp.concatenate([ref[at] if at else ref[...] for ref in refs], axis=0)


def gain_row(pack_refs, which):
    cols = jnp.concatenate([ref[:, GAINS - 64 : PACK] for ref in pack_refs], axis=0)
    at = lax.broadcasted_iota(jnp.int32, (8, 128), 1)
    pick = jnp.where(at == 64 + which, 1.0, 0.0).astype(BF16)
    return mm(pick, cols, NT)[:1]


def swap_pairs(values, block):
    two = 2 * block
    return jnp.concatenate(
        [pltpu.roll(values[:, at : at + two], block, 1) for at in (0, two)], axis=1
    )


def relative(values, me, block):
    two = 2 * block
    far = jnp.concatenate([values[:, two:], values[:, :two]], axis=1)
    values = jnp.where((me & 2) > 0, far, values)
    return jnp.where((me & 1) > 0, swap_pairs(values, block), values)


def arrived(bit, refs):
    chunks = len(refs) // 2
    mine, other = joined(refs[:chunks]), joined(refs[chunks:])
    return jnp.where(pl.program_id(0) == bit, mine, other).astype(F32)


def put_halves(tile, bit, values, refs):
    chunks = len(refs) // 2
    rows = values.shape[0] // chunks
    values = values.astype(BF16)

    @pl.when(tile == bit)
    def _():
        for at in range(chunks):
            refs[at][...] = values[at * rows : (at + 1) * rows]

    @pl.when(tile != bit)
    def _():
        for at in range(chunks):
            refs[chunks + at][...] = values[at * rows : (at + 1) * rows]


def half_shapes(rows, width, chunks):
    return [whole(sds((rows // 2 // chunks, width), BF16)) for _ in range(2 * chunks)]


def normed_of(values, gain):
    inverse = lax.rsqrt(jnp.mean(values * values, axis=-1, keepdims=True) + EPS)
    scaled = values * inverse
    return scaled, inverse, scaled * gain


def norm_back(d_normed, values, gain):
    scaled, inverse, _ = normed_of(values, gain)
    d_scaled = d_normed * gain
    mean = jnp.mean(d_scaled * scaled, axis=-1, keepdims=True)
    return inverse * (d_scaled - scaled * mean), jnp.sum(d_normed * scaled, axis=0, keepdims=True)


def order_kernel(scal, tok_ref, cot_ref, tok_out, cot_out, *, block):
    for src, dst in ((tok_ref, tok_out), (cot_ref, cot_out)):
        dst[...] = relative(src[...].astype(F32), scal[0], block).astype(BF16)


def project(stream, packs, normed_ref, q_ref, kv_ref):
    _, _, normed = normed_of(stream, gain_row(packs, 0))
    normed = normed.astype(BF16)
    normed_ref[...] = normed
    weight = joined(packs)
    kv_ref[...] = mm(normed, weight[:, KEYS:QUERY]).astype(BF16)
    q_ref[...] = mm(normed, weight[:, QUERY : QUERY + q_ref.shape[1]]).astype(BF16)


def first_kernel(scal, tok_ref, *refs):
    project(tok_ref[...].astype(F32), refs[:4], *refs[4:])


def next_kernel(scal, mixed_ref, *refs, parts):
    stream = mixed_ref[...] + arrived(scal[1], refs[:parts])
    packs, (stream_ref, *outs) = refs[parts : parts + 4], refs[parts + 4 :]
    stream_ref[...] = stream
    project(stream, packs, *outs)


def last_kernel(scal, mixed_ref, *refs, block):
    result = mixed_ref[...] + arrived(scal[1], refs[:-1])
    refs[-1][...] = relative(result, scal[0], block).astype(BF16)


def allowed_of(scal, path_ref, rows, tree_len):
    first = scal[3] + pl.program_id(0) * rows
    query_pos = first + lax.broadcasted_iota(jnp.int32, (rows, tree_len), 0)
    key_pos = lax.broadcasted_iota(jnp.int32, (rows, tree_len), 1)
    return (key_pos <= query_pos) & (path_ref[...] > 0.5)


def softmax_of(query, key, allowed):
    scores = jnp.where(allowed, mm(query, key, NT) * SCALE, MASKED)
    expo = jnp.exp(scores - jnp.max(scores, axis=-1, keepdims=True))
    return expo * (1.0 / jnp.sum(expo, axis=-1, keepdims=True))


def head_cols(width):
    return [slice(at, at + HEAD_DIM) for at in range(0, width, HEAD_DIM)]


def all_keys(scal, refs):
    if len(refs) == 1:
        return refs[0][...]
    own, got = refs[0][...], refs[1][...]
    first = scal[4] == 0
    return jnp.concatenate([jnp.where(first, own, got), jnp.where(first, got, own)], axis=0)


def attend_kernel(scal, path_ref, q_ref, *refs, parts):
    kv_ref, refs = all_keys(scal, refs[:parts]), refs[parts:]
    packs, heads_ref, halves = refs[:4], refs[4], refs[5:]
    rows, width = q_ref.shape
    allowed = allowed_of(scal, path_ref, rows, kv_ref.shape[0])
    outs = []
    for cols in head_cols(width):
        vals = slice(width + cols.start, width + cols.stop)
        probs = softmax_of(q_ref[:, cols], kv_ref[:, cols], allowed).astype(BF16)
        outs.append(mm(probs, kv_ref[:, vals]))
    heads = jnp.concatenate(outs, axis=1).astype(BF16)
    heads_ref[...] = heads
    weight = jnp.concatenate([ref[:, OUT : OUT + width] for ref in packs], axis=0)
    put_halves(pl.program_id(0), scal[1], mm(heads, weight, NT), halves)


def attend_back_kernel(scal, path_ref, q_ref, d_ref, heads_ref, *refs, parts):
    kv_ref, refs = all_keys(scal, refs[:parts]), refs[parts:]
    packs, (dq_ref, gout_ref), (dkv_refs, scratch) = refs[:4], refs[4:6], (refs[6:-2], refs[-2:])
    dkv_acc, gout_acc = scratch
    rows, width = q_ref.shape
    tile = pl.program_id(0)
    allowed = allowed_of(scal, path_ref, rows, kv_ref.shape[0])

    @pl.when(tile == 0)
    def _():
        dkv_acc[...] = jnp.zeros_like(dkv_acc)
        gout_acc[...] = jnp.zeros_like(gout_acc)

    weight = jnp.concatenate([ref[:, OUT : OUT + width] for ref in packs], axis=0)
    d_heads = mm(d_ref[...], weight).astype(BF16)
    gout_acc[...] += mm(d_ref[...], heads_ref[...], TN)
    dqs, dks, dvs = [], [], []
    for cols in head_cols(width):
        vals = slice(width + cols.start, width + cols.stop)
        query, key, value, d_out = q_ref[:, cols], kv_ref[:, cols], kv_ref[:, vals], d_heads[:, cols]
        probs = softmax_of(query, key, allowed)
        d_prob = mm(d_out, value, NT)
        weighted = jnp.sum(probs * d_prob, axis=-1, keepdims=True)
        d_scores = (probs * (d_prob - weighted)).astype(BF16)
        dqs.append(mm(d_scores, key) * SCALE)
        dks.append(mm(d_scores, query, TN) * SCALE)
        dvs.append(mm(probs.astype(BF16), d_out, TN))
    dq_ref[...] = jnp.concatenate(dqs, axis=1).astype(BF16)
    dkv_acc[...] += jnp.concatenate(dks + dvs, axis=1)

    @pl.when(tile == pl.num_programs(0) - 1)
    def _():
        gout_ref[...] = gout_acc[...].astype(BF16)
        if len(dkv_refs) == 1:
            dkv_refs[0][...] = dkv_acc[...].astype(BF16)
        else:
            half = dkv_refs[0].shape[0]
            for at in range(2):
                part = dkv_acc[at * half : (at + 1) * half, :].astype(BF16)
                mine = scal[3] == at * half

                @pl.when(mine)
                def _():
                    dkv_refs[0][...] = part

                @pl.when(jnp.logical_not(mine))
                def _():
                    dkv_refs[1][...] = part


def project_back_kernel(scal, dq_ref, own_ref, got_ref, normed_ref, gout_ref, *refs, chunks):
    packs, halves, grads = refs[:4], refs[4 : 4 + 2 * chunks], refs[4 + 2 * chunks :]
    d_kv = (own_ref[...].astype(F32) + got_ref[...].astype(F32)).astype(BF16)
    d_q, normed = dq_ref[...], normed_ref[...]
    width = d_q.shape[1]
    weight = joined(packs)
    part = mm(d_kv, weight[:, KEYS:QUERY], NT) + mm(d_q, weight[:, QUERY : QUERY + width], NT)
    half = part.shape[0] // 2
    for at in range(2):
        put_halves(at, scal[1], part[at * half : (at + 1) * half], halves)
    g_kv, g_q, g_out = mm(normed, d_kv, TN), mm(normed, d_q, TN), gout_ref[...]
    rows = grads[0].shape[0]
    for at, ref in enumerate(grads):
        cut = slice(at * rows, (at + 1) * rows)
        ref[...] = jnp.zeros_like(ref)
        ref[:, KEYS:QUERY] = g_kv[cut].astype(BF16)
        ref[:, QUERY : QUERY + width] = g_q[cut].astype(BF16)
        ref[:, OUT : OUT + width] = g_out[cut]


def mix_kernel(scal, stream_ref, *refs, parts):
    mixed = stream_ref[...].astype(F32) + arrived(scal[1], refs[:parts])
    packs, (mixed_ref, in_ref) = refs[parts : parts + 4], refs[parts + 4 :]
    mixed_ref[...] = mixed
    in_ref[...] = normed_of(mixed, gain_row(packs, 1))[2].astype(BF16)


def shared_kernel(scal, in_ref, *refs):
    packs, (branch_ref, gate_ref, up_ref) = refs[:12], refs[12:]
    gate = mm(in_ref[...], joined(packs[:4]))
    up = mm(in_ref[...], joined(packs[4:8]))
    gate_ref[...] = gate
    up_ref[...] = up
    hidden = (gate / (1.0 + jnp.exp(-gate)) * up).astype(BF16)
    branch_ref[...] = mm(hidden, joined(packs[8:]), NT)


def glu_back(gate, up, d_hidden):
    sigmoid = 1.0 / (1.0 + jnp.exp(-gate))
    active = gate * sigmoid
    hidden = (active * up).astype(BF16)
    d_gate = (d_hidden * up * (sigmoid * (1.0 + gate * (1.0 - sigmoid)))).astype(BF16)
    return hidden, d_gate, (d_hidden * active).astype(BF16)


def shared_back_kernel(scal, d_ref, in_ref, gate_ref, up_ref, *refs):
    packs, (out_ref, *grad_refs) = refs[:12], refs[12:]
    hid = gate_ref.shape[1]
    cut = lambda at: joined(packs[4 * at : 4 * at + 4])
    d_branch, ffn_in = d_ref[...], in_ref[...]
    hidden, d_gate, d_up = glu_back(gate_ref[...], up_ref[...], mm(d_branch, cut(2)))
    out_ref[...] = mm(d_gate, cut(0), NT) + mm(d_up, cut(1), NT)
    grads = (mm(ffn_in, d_gate, TN), mm(ffn_in, d_up, TN), mm(d_branch, hidden, TN))
    rows = grad_refs[0].shape[0]
    for at, grad in enumerate(grads):
        for r, ref in enumerate(grad_refs):
            ref[:, at * hid : (at + 1) * hid] = grad[r * rows : (r + 1) * rows].astype(BF16)


def column(table_ref, rows, at):
    values = table_ref[rows, :]
    lane = lax.broadcasted_iota(jnp.int32, values.shape, 1)
    return jnp.sum(jnp.where(lane == at, values, 0.0), axis=1, keepdims=True)


def spread(first, second, places, weights):
    one, two = weights
    return jnp.where(places == first, one, jnp.where(places == second, two, 0.0)).astype(BF16)


def rows_of(lists_ref, half, tokens, slots, weighted):
    cut = slice(half * tokens, (half + 1) * tokens)
    first, second, one, two = [lists_ref[at : at + 1, cut] for at in range(4)]
    places = lax.broadcasted_iota(jnp.int32, (slots, tokens), 0)
    weights = (one, two) if weighted else (1.0, 1.0)
    return spread(first.astype(jnp.int32), second.astype(jnp.int32), places, weights)


def cols_of(table_ref, half, tokens, slots, weighted):
    cut = slice(half * tokens, (half + 1) * tokens)
    first, second = [column(table_ref, cut, at).astype(jnp.int32) for at in range(2)]
    weights = [column(table_ref, cut, at) for at in (2, 3)] if weighted else (1.0, 1.0)
    places = lax.broadcasted_iota(jnp.int32, (tokens, slots), 1)
    return spread(first, second, places, weights)


def to_slots(own_ref, sib_ref, lists_ref, slot_ref, block, weighted):
    @pl.when(pl.program_id(0) == 0)
    def _():
        tokens, slots = own_ref.shape[0], slot_ref.shape[1]
        sib = swap_pairs(sib_ref[...].astype(F32), block).astype(BF16)
        for half, values in enumerate((own_ref[...], sib)):
            picks = rows_of(lists_ref, half, tokens, slots, weighted)
            slot_ref[half] = mm(picks, values).astype(BF16)


def from_slots(slot_ref, table_ref, own_out, sib_out, weighted):
    @pl.when(pl.program_id(0) == pl.num_programs(0) - 1)
    def _():
        tokens, slots = own_out.shape[0], slot_ref.shape[1]
        for half, ref in enumerate((own_out, sib_out)):
            picks = cols_of(table_ref, half, tokens, slots, weighted)
            ref[...] = mm(picks, slot_ref[half]).astype(ref.dtype)


def of_expert(slot_ref):
    count = slot_ref.shape[1] // pl.num_programs(0)
    rows = pl.ds(pl.multiple_of(pl.program_id(0) * count, count), count)
    return jnp.concatenate([slot_ref[0, rows, :], slot_ref[1, rows, :]], axis=0)


def put_expert(slot_ref, values):
    count = slot_ref.shape[1] // pl.num_programs(0)
    rows = pl.ds(pl.multiple_of(pl.program_id(0) * count, count), count)
    slot_ref[0, rows, :] = values[:count]
    slot_ref[1, rows, :] = values[count:]


def pack_kernel(scal, in_ref, out_ref, own_ref, first_ref, last_ref):
    third = first_ref.shape[2]
    own_ref[0, :2] = in_ref[0, 0]
    own_ref[0, 2] = out_ref[0, 0]
    first_ref[0] = own_ref[0, :, pl.ds(pl.multiple_of(scal[4] * third, third), third), :]
    last_ref[0] = own_ref[0, :, 2 * third :, :]


def expert_weights(scal, refs):
    if len(refs) == 4:
        return [joined(refs, 0, part) for part in range(3)]

    def far(refs, part):
        straight, around, last = [ref[0, part] for ref in refs]
        low = jnp.where(scal[4] == 0, straight, around)
        middle = jnp.where(scal[4] == 0, around, straight)
        return [low, middle, last]

    return [
        jnp.concatenate(
            [refs[0][0, part], refs[1][0, part]] + far(refs[2:5], part) + far(refs[5:8], part), axis=0
        )
        for part in range(3)
    ]


def expert_kernel(scal, own_ref, sib_ref, lists_ref, table_ref, *refs, block, sources):
    weights, (own_out, sib_out, x_ref, gate_ref, up_ref, x_all, y_all) = refs[:sources], refs[sources:]
    to_slots(own_ref, sib_ref, lists_ref, x_all, block, False)
    w_gate, w_up, w_out = expert_weights(scal, weights)
    chosen = of_expert(x_all)
    gate = mm(chosen, w_gate)
    up = mm(chosen, w_up)
    x_ref[0], gate_ref[0], up_ref[0] = chosen, gate.astype(BF16), up.astype(BF16)
    hidden = (gate / (1.0 + jnp.exp(-gate)) * up).astype(BF16)
    put_expert(y_all, mm(hidden, w_out, NT).astype(BF16))
    from_slots(y_all, table_ref, own_out, sib_out, True)


def expert_back_kernel(
    scal, own_ref, sib_ref, lists_ref, table_ref, a_ref, b_ref, *refs, block, sizes, sources, fresh
):
    given, refs = ((), refs) if fresh else (refs[:1], refs[1:])
    weights, refs = refs[:sources], refs[sources:]
    (own_out, sib_out), grads, refs = refs[:2], refs[2 : 2 + 2 * len(sizes)], refs[2 + 2 * len(sizes) :]
    to_slots(own_ref, sib_ref, lists_ref, refs[-1], block, True)
    w_gate, w_up, w_out = expert_weights(scal, weights)
    d_rows = of_expert(refs[-1])
    if fresh:
        own_next, sib_next, x_all, y_all = refs[:4]
        to_slots(a_ref, b_ref, lists_ref, x_all, block, False)
        chosen = of_expert(x_all)
        gate, up = mm(chosen, w_gate), mm(chosen, w_up)
    else:
        chosen, gate, up = a_ref[0], b_ref[0].astype(F32), given[0][0].astype(F32)
    hidden, d_gate, d_up = glu_back(gate, up, mm(d_rows, w_out))
    if fresh:
        put_expert(y_all, mm(hidden, w_out, NT).astype(BF16))
        from_slots(y_all, table_ref, own_next, sib_next, True)
    step = pl.program_id(0)
    parts = (mm(chosen, d_gate, TN), mm(chosen, d_up, TN), mm(d_rows, hidden, TN))
    parts = [p.astype(BF16) for p in parts]
    for chunk, size in enumerate(sizes):
        first = sum(sizes[:chunk])

        @pl.when((step >= first) & (step < first + size))
        def _():
            for at in range(3):
                grads[2 * chunk][0, at] = parts[at][: 2 * block]
                grads[2 * chunk + 1][0, at] = parts[at][2 * block :]

    d_x = mm(d_gate, w_gate, NT) + mm(d_up, w_up, NT)
    put_expert(refs[-1], d_x.astype(BF16))
    from_slots(refs[-1], table_ref, own_out, sib_out, False)


def join_kernel(scal, own_ref, got_ref, shared_ref, *halves, block):
    part = own_ref[...] + shared_ref[...] + swap_pairs(got_ref[...].astype(F32), block)
    put_halves(pl.program_id(0), scal[1], part, halves)


def mix_back_kernel(scal, mixed_ref, next_ref, *refs, parts):
    packs, (d_ref, attn_ref, gain_ref) = refs[parts : parts + 4], refs[parts + 4 :]
    back, gain_grad = norm_back(arrived(scal[1], refs[:parts]), mixed_ref[...], gain_row(packs, 1))
    d_mixed = back + next_ref[...].astype(F32)
    d_ref[...] = d_mixed
    attn_ref[...] = d_mixed.astype(BF16)
    sum_tiles(gain_ref, gain_grad)


def sum_tiles(ref, value):
    value = jnp.broadcast_to(value, ref.shape)

    @pl.when(pl.program_id(0) == 0)
    def _():
        ref[...] = value

    @pl.when(pl.program_id(0) > 0)
    def _():
        ref[...] += value


def input_back_kernel(scal, stream_ref, mixed_ref, *refs, parts, block, final):
    packs, outs = refs[parts : parts + 4], refs[parts + 4 :]
    stream = stream_ref[...].astype(F32)
    back, gain_grad = norm_back(arrived(scal[1], refs[:parts]), stream, gain_row(packs, 0))
    d_stream = back + mixed_ref[...]
    if final:
        outs[0][...] = relative(d_stream, scal[0], block)
    else:
        outs[0][...] = d_stream
        outs[1][...] = d_stream.astype(BF16)
    sum_tiles(outs[-1], gain_grad)


def store_expert(in_ref, out_ref, gate, up, out):
    blocks = gate.shape[1] // 128
    for at, part in enumerate((gate, up)):
        for col in range(blocks):
            rows = pl.ds(col * 2 + at, part.shape[0], stride=2 * blocks)
            in_ref[0, 0, rows, :] = part[:, col * 128 : (col + 1) * 128]
    out_ref[0, 0] = out


def own_kernel(scal, part_ref, got_ref, *refs):
    give_ref, in_ref, out_ref = refs[-3:]
    half = give_ref.shape[2]
    total = [part_ref[0, at].astype(F32) + got_ref[0, at].astype(F32) for at in range(3)]
    for at in range(3):
        give_ref[0, at] = total[at][half:].astype(BF16)
    store_expert(in_ref, out_ref, *[t[:half] for t in total])


def other_kernel(scal, got_ref, *refs):
    store_expert(*refs[-2:], *[got_ref[0, at].astype(F32) for at in range(3)])


def packed_kernel(scal, part_ref, got_ref, *refs, first, shared, blocks):
    total = part_ref[...].astype(F32) + got_ref[...].astype(F32)
    if first is not None:
        refs, (qkv_ref, out_ref) = refs[:-2], refs[-2:]
        width = qkv_ref.shape[3]
        for at, col in enumerate((QUERY, KEYS, KEYS + width)):
            qkv_ref[0, at] = total[:, first + col : first + col + width]
        out_ref[0] = total[:, first + OUT : first + OUT + width].T
    if shared:
        sin_ref, sout_ref = refs[-2:]
        hid = sout_ref.shape[2]
        for at in range(2):
            for col in range(blocks):
                rows = pl.ds(col * 2 + at, total.shape[0], stride=2 * blocks)
                lanes = at * hid + col * 128
                sin_ref[0, rows, :] = total[:, lanes : lanes + 128]
        sout_ref[0] = total[:, 2 * hid : 3 * hid]

CHUNKS, PARTS = 2, ((1, 1, 1, 1), (2, 1, 1))
SLOTS = {
    "start": ["pack 0", ("experts", 0)],
    ("attend", 0): ["slots"],
    ("attend half", 0): [("experts", 0), "pack 1"],
    ("attend sum", 0): ["pack 2", ("experts", 1)],
    ("mixed", 0): [("experts", 0), "pack 1", "pack 2"],
    ("experts", 0): ["pack 1", "pack 2", ("experts", 1)],
    ("attend sum", 1): [("experts", 1)],
    ("mixed", 1): [("experts", 1)],
    (1, "experts"): [(1, 0)],
    (1, "attention"): [(1, 0), (1, 1)],
    (1, "project"): [(1, "packs")],
    (1, "attention half"): [(1, 1), (1, 2)],
    (1, "input"): [(1, 0), (1, 2), (1, "packs")],
    (0, "experts"): [(1, 1), (1, "packs"), (0, 0)],
    (0, "ffn half"): [(1, 0), (1, 2), (0, 0), (0, 1)],
    (0, "ffn sum"): [(1, 1), (0, 1), (0, 2), (0, "shared")],
    (0, "attention"): [(1, "packs"), (0, 0), (0, 2), (0, 3)],
    (0, "project"): [(0, "attention"), "result"],
    (0, "attention half"): [(1, 2), (0, 1), (0, 3), (0, "shared")],
    (0, "attention sum"): [(0, 0), (0, 2), (0, "shared"), (0, "attention"), "result"],
    (0, "input"): [(0, 1), (0, "attention")],
}
TAIL = (
    ["gains", (0, "shared"), (0, "attention"), (0, 3), (0, 2)],
    ["gains", "result"],
    ["gains", (0, 3)],
)


class Packs:
    def __init__(self, scal, layers, block, hid, width):
        self.scal, self.blocks = scal, hid // 128
        self.shapes = (
            sds((layers, block * 2 * self.blocks, 128), F32),
            sds((layers, block, hid), F32),
            sds((layers, 3, block, width), F32),
            sds((layers, width, block), F32),
        )
        self.held = [None] * 4

    def put(self, layer, first, shared, part, got):
        used = [0, 1] * shared + [2, 3] * (first is not None)
        before = [at for at in used if self.held[at] is not None]
        slot = lambda s: (s, (1,) + s.shape[1:], lambda *_: (layer,) + (0,) * (len(s.shape) - 1))
        results = call(
            functools.partial(packed_kernel, first=first, shared=shared, blocks=self.blocks),
            self.scal,
            (1,),
            [whole(part), whole(got)] + [(self.held[at], "any", None) for at in before],
            [slot(self.shapes[at]) for at in used],
            alias={3 + n: used.index(at) for n, at in enumerate(before)},
            limit=16,
        )
        for at, result in zip(used, results):
            self.held[at] = result


class Outs:
    def __init__(self, scal, layers, experts, block, hid):
        self.scal, self.per_core = scal, experts // 2
        self.shapes = (
            sds((layers, experts, block * 2 * hid // 128, 128), F32),
            sds((layers, experts, block, hid), F32),
        )
        self.held = None

    def put(self, kernel, ins, extra, layer, first, other):
        count = ins[0].shape[0]
        lead = lambda a: (a, (1,) + a.shape[1:], lambda e, s: (e, 0, 0, 0))
        place = lambda e, s: (layer, (s[2] ^ other) * self.per_core + first + e, 0, 0)
        moved = lambda s: count * s.size * 4 // (s.shape[0] * s.shape[1])
        slot = lambda s: (s, (1, 1) + s.shape[2:], place, moved(s))
        held = [] if self.held is None else [(h, "any", None) for h in self.held]
        base = 1 + len(ins)
        *rest, gin, gout = call(
            kernel,
            self.scal,
            (count,),
            [lead(i) for i in ins] + held,
            [lead(x) for x in extra] + [slot(s) for s in self.shapes],
            alias={base + at: len(extra) + at for at in range(len(held))},
            limit=16,
        )
        self.held = (gin, gout)
        return rest


def expert_flow(outs, near, far, layer, first):
    near, far = yield [near, far]
    near, got = yield [near, swap(far, "fsdp", 2)]
    part, got = yield list(ctx_last(add(near, got)))
    block = near.shape[2] // 2
    give = sds(near.shape[:2] + (block,) + near.shape[3:], BF16)
    (give,) = outs.put(own_kernel, (part, got), (give,), layer, first, 0)
    (got,) = yield [swap(give, "fsdp", 1)]
    outs.put(other_kernel, (got,), (), layer, first, 1)
    yield []


def pack_flow(done, parts):
    parts = yield list(parts)
    own, far, got, far_got = yield [parts[0], parts[2], swap(parts[1], "fsdp", 1), swap(parts[3], "fsdp", 1)]
    own, far = add(own, got), add(far, far_got)
    own, got = yield [own, swap(far, "fsdp", 2)]
    part, got = yield list(ctx_last(add(own, got)))
    done(part, got)
    yield []


def weight_flow(place, at, own, first, last):
    own, first, last = yield [own, first, last]
    own, sib, straight, last = yield [own, swap(own, "fsdp", 1), swap(first, "fsdp", 2), last]
    around, last = swap(straight, "ctx", 1), swap(last, "fsdp", 2)
    held = yield [straight, around, last, swap(straight, "fsdp", 1)]
    straight, around, last, cross = held
    place[at] = [own, sib, straight, around, last]
    place[at] += [cross, swap(around, "fsdp", 1), swap(last, "fsdp", 1)]
    yield []


def plain_flow(place, at, own, first, last):
    (own,) = yield [own]
    (own,) = yield [own]
    own, far = yield [own, swap(own, "fsdp", 2)]
    near = swap(own, "fsdp", 1)
    near, far, cross = yield [near, far, swap(far, "fsdp", 1)]
    place[at] = [own, near, far, cross]
    yield []


def block_flow(place, at, own):
    (own,) = yield [own]
    (own,) = yield [own]
    own, far = yield [own, swap(own, "fsdp", 2)]
    place[at] = [own, swap(own, "fsdp", 1), far, swap(far, "fsdp", 1)]
    yield []


def ancestry(parent_row):
    count = parent_row.shape[0]
    block_ids = jnp.arange(count, dtype=jnp.int32)
    step_map = ((parent_row[:, None] == block_ids[None, :]) & (block_ids[:, None] > 0)).astype(F32)
    reach = on_path = jnp.eye(count, dtype=F32)
    for _ in range(count):
        reach = jnp.dot(reach, step_map, precision=lax.Precision.HIGHEST)
        on_path = on_path + reach
    return on_path


def shards(
    tokens,
    parents,
    routes,
    gates,
    attn_gain,
    ffn_gain,
    qkv_weight,
    out_weight,
    shared_in,
    shared_out,
    expert_in,
    expert_out,
    cotangent,
):
    rows, width = tokens.shape[1], tokens.shape[2]
    layers, experts = expert_in.shape[0], expert_in.shape[1]
    block, heads_width = qkv_weight.shape[1], qkv_weight.shape[3]
    hid = expert_in.shape[4]
    ctx = lax.axis_size("ctx")
    tree_len = rows * ctx
    me, here = lax.axis_index("fsdp"), lax.axis_index("ctx")
    core, bit = me & 1, lax.axis_index("tp") & 1
    half_at = here & 1
    per_core = experts // 2
    capacity = 2 * (3 * rows // 8)
    scal = jnp.stack([me, bit, core, here * rows, half_at]).astype(jnp.int32)

    def pack_attention(at):
        cols = [qkv_weight[at][:, part] for part in (1, 2, 0)]
        pad = jnp.zeros((block, OUT - QUERY - heads_width), BF16)
        gains = jnp.stack([attn_gain[at], ffn_gain[at]], axis=1)
        tail = jnp.zeros((block, PACK - GAINS - 2), BF16)
        return jnp.concatenate(cols + [pad, out_weight[at].T, gains, tail], axis=1)

    def pack_shared(at):
        return [shared_in[at].reshape(block, 2 * hid), shared_out[at].T]

    ein = lax.optimization_barrier(expert_in.transpose(0, 1, 3, 2, 4))
    eout = expert_out.transpose(0, 1, 3, 2)

    def pack_experts(at):
        third = block // 3
        whole_pack = sds((experts, 3, block, hid), BF16)
        part = sds((experts, 3, third, hid), BF16)
        lead = lambda a: (a, (1,) + a.shape[1:], lambda e, s: (e, 0, 0, 0))
        return call(
            pack_kernel,
            scal,
            (experts,),
            [
                (ein, (1, 1) + ein.shape[2:], lambda e, s: (at, e, 0, 0, 0)),
                (eout, (1, 1) + eout.shape[2:], lambda e, s: (at, e, 0, 0)),
            ],
            [lead(whole_pack), lead(part), lead(part)],
            limit=16,
        )

    ancestors = ancestry(parents[0])
    segment = tree_len // ancestors.shape[0]
    anc_row = lax.dynamic_slice_in_dim(ancestors, here * rows // segment, 1, 0)
    path = jnp.repeat(anc_row, segment, axis=1)

    places = 3 * rows // 8
    info = jnp.concatenate([routes[0].astype(F32), gates[0]], axis=1)
    info = jnp.concatenate([info, swap(info, "fsdp", 1)], axis=0)
    local = info[:, :2].astype(jnp.int32) - core * per_core
    hits = local[:, :, None] == jnp.arange(per_core, dtype=jnp.int32)
    at = jnp.arange(2 * rows)
    earlier = (at[:, None] > at[None, :]) & (at[:, None] // rows == at[None, :] // rows)
    before = mm(earlier.astype(BF16), jnp.any(hits, axis=1).astype(BF16))
    slot = before[:, None, :] + places * jnp.arange(per_core, dtype=F32)
    slot = jnp.sum(jnp.where(hits, slot + 1.0, 0.0), axis=2) - 1.0
    table = jnp.concatenate([slot, info[:, 2:]], axis=1)

    lead = lambda a: (
        a,
        (1,) + tuple(a.shape[1:]),
        lambda e, s: (e,) + (0,) * (len(a.shape) - 1),
    )

    matrix = 2 * rows * width
    expert_flops = 2 * per_core * capacity * width * hid
    slot_scratch = [pltpu.VMEM((2, per_core * places, width), BF16)]
    halves = half_shapes(rows, width, CHUNKS)
    row_f32, row_bf16 = sds((rows, width), F32), sds((rows, width), BF16)

    flows, held = {}, {}

    def open_flow(name, flow):
        flows[name] = flow
        held[name] = next(flow)

    def slot(name, *values):
        names = SLOTS.get(name, ())
        if not names:
            return list(values)
        values, arrays = lax.optimization_barrier((list(values), [held[n] for n in names]))
        for n, a in zip(names, arrays):
            if n == "slots":
                tables.extend(a)
            else:
                held[n] = flows[n].send(a)
        return values

    tables = []

    def finish(*names):
        for name in names:
            held[name] = flows[name].send(held[name])

    small, routed = {}, {}
    open_flow("pack 0", block_flow(small, 0, pack_attention(0)))
    for at in range(layers):
        kind = weight_flow if at == 0 else plain_flow
        open_flow(("experts", at), kind(routed, at, *pack_experts(at)))
    open_flow("pack 1", block_flow(small, 1, jnp.concatenate(pack_shared(0), axis=1)))
    rest = [pack_attention(at) for at in range(1, layers)]
    rest = [v for pack in rest for v in (pack, jnp.zeros((block, 128), BF16))]
    rest += [v for at in range(1, layers) for v in pack_shared(at)]
    open_flow("pack 2", block_flow(small, 2, jnp.concatenate(rest, axis=1)))

    held["slots"] = [table.T, table]

    def attention_ins(at):
        if at == 0:
            return [whole(p) for p in small[0]]
        return [(p, (block, 1024), lambda *_: (0, at - 1)) for p in small[2]]

    def shared_ins(at):
        packs, first = (small[1], 0) if at == 0 else (small[2], 1024 * (layers - 1) // hid + 3 * at - 3)
        index = lambda which: lambda *_: (0, first + which)
        return [(p, (block, hid), index(which)) for which in range(3) for p in packs]

    def expert_ins(at):
        index = lambda e, s: (s[2] * per_core + e, 0, 0, 0)
        return [(a, (1,) + a.shape[1:], index) for a in routed[at]]

    stream, cot = call(
        functools.partial(order_kernel, block=block),
        scal,
        (2,),
        [tiled(tokens[0]), tiled(cotangent[0])],
        [tiled(row_bf16)] * 2,
    )
    finish("pack 0")
    finish("pack 0")
    slot("start")

    def experts_forward(at, own_in, sib_in):
        kept = [lead(sds((per_core, capacity, width), BF16))]
        kept += [lead(sds((per_core, capacity, hid), BF16))] * 2
        return call(
            functools.partial(
                expert_kernel, block=block, sources=len(routed[at])
            ),
            scal,
            (per_core,),
            [whole(own_in), whole(sib_in), whole(tables[0]), whole(tables[1])] + expert_ins(at),
            [whole(row_f32), whole(row_bf16)] + kept,
            scratch=slot_scratch * 2,
            flops=5 * expert_flops,
            limit=48,
        )

    def join(own, sib, shared_part):
        return call(
            functools.partial(join_kernel, block=block),
            scal,
            (2,),
            [tiled(own), tiled(swap(sib, "fsdp", 1)), tiled(shared_part)],
            halves,
        )

    def result_flow(mixed, own, sib, branch):
        own, sib = yield [own, sib]
        part = yield list(join(own, sib, branch))
        arrivals = yield tp_sum(part, lambda *values: values)
        (result[0],) = call(
            functools.partial(last_kernel, block=block),
            scal,
            (2,),
            [tiled(mixed)] + [whole(a) for a in arrivals],
            [tiled(row_bf16)],
        )
        yield []

    result = [None]
    saved = []
    mixed = arrivals = None
    for at in range(layers):
        outs = [
            tiled(row_bf16),
            tiled(sds((rows, heads_width), BF16)),
            tiled(sds((rows, 2 * heads_width), BF16)),
        ]
        weights = attention_ins(at)
        if at == 0:
            normed, query, kv = call(
                first_kernel, scal, (2,), [tiled(stream)] + weights, outs, flops=matrix * 576
            )
        else:
            stream, normed, query, kv = call(
                functools.partial(next_kernel, parts=len(arrivals)),
                scal,
                (2,),
                [tiled(mixed)] + [whole(a) for a in arrivals] + weights,
                [tiled(row_f32)] + outs,
                flops=matrix * 576,
            )
        (kv,) = slot(("project", at), kv)
        if ctx == 2:
            kv = [kv, swap(kv, "ctx", 1)]
        else:
            kv = [lax.all_gather(kv, "ctx", axis=0, tiled=True)]
        heads, *part = call(
            functools.partial(attend_kernel, parts=len(kv)),
            scal,
            (2,),
            [whole(path), tiled(query)] + [whole(k) for k in kv] + weights,
            [tiled(sds((rows, heads_width), BF16))] + halves,
            flops=4 * rows * tree_len * heads_width + matrix * heads_width,
            exps=rows * tree_len * heads_width // HEAD_DIM,
            limit=40,
        )
        part = slot(("attend", at), *part)
        arrivals = tp_sum(part, functools.partial(slot, ("attend half", at)))
        arrivals = slot(("attend sum", at), *arrivals)
        mixed, ffn_in = call(
            functools.partial(mix_kernel, parts=len(arrivals)),
            scal,
            (2,),
            [tiled(stream)] + [whole(a) for a in arrivals] + weights,
            [tiled(row_f32), tiled(row_bf16)],
        )
        sib_in = swap(ffn_in, "fsdp", 1)
        ffn_in, sib_in = slot(("mixed", at), ffn_in, sib_in)
        if at + 1 < layers:
            own, sib, *hidden = experts_forward(at, ffn_in, sib_in)
            own, sib = slot(("experts", at), own, sib)
        branch, gate, up = call(
            shared_kernel,
            scal,
            (2,),
            [tiled(ffn_in)] + shared_ins(at),
            [tiled(row_f32)] + [tiled(sds((rows, hid), F32))] * 2,
            flops=3 * matrix * hid,
            exps=rows * hid,
        )
        if at + 1 < layers:
            part = join(own, sib, branch)
            part = slot(("join", at), *part)
            arrivals = tp_sum(part, functools.partial(slot, ("branch half", at)))
            arrivals = slot(("branch sum", at), *arrivals)
        else:
            hidden = [ffn_in, sib_in]
        saved.append((stream, normed, query, kv, heads, mixed, ffn_in, gate, up, hidden))

    outs = Outs(scal, layers, experts, block, hid)
    packed = Packs(scal, layers, block, hid, heads_width)
    gain_sums = []
    gain_grads = [None] * (2 * layers)
    d_next, d_branch = cot, cot
    for at in reversed(range(layers)):
        stream, normed, query, kv, heads, mixed, ffn_in, gate, up, hidden = saved[at]
        weights = attention_ins(at)
        sib_d = swap(d_branch, "fsdp", 1)
        d_ffn, *g_shared = call(
            shared_back_kernel,
            scal,
            (1,),
            [whole(a) for a in (d_branch, ffn_in, gate, up)] + shared_ins(at),
            [whole(row_f32)] + [whole(sds((block, 3 * hid), BF16))] * 4,
            flops=6 * matrix * hid,
            exps=rows * hid,
        )
        sizes = PARTS[at]
        fresh = len(hidden) == 2
        part_of = lambda first, size: (
            sds((size, 3, 2 * block, hid), BF16),
            (1, 3, 2 * block, hid),
            lambda e, s: (jnp.clip(e - first, 0, size - 1), 0, 0, 0),
        )
        own, sib, *grads = call(
            functools.partial(
                expert_back_kernel, block=block, sizes=sizes, fresh=fresh,
                sources=len(routed[at])
            ),
            scal,
            (per_core,),
            [whole(d_branch), whole(sib_d), whole(tables[0]), whole(tables[1])]
            + [whole(a) if fresh else lead(a) for a in hidden]
            + expert_ins(at),
            [whole(row_f32), whole(row_bf16)]
            + [part_of(sum(sizes[:n]), size) for n, size in enumerate(sizes) for _ in range(2)]
            + [whole(row_f32), whole(row_bf16)] * fresh,
            scratch=slot_scratch * (3 if fresh else 1),
            flops=8 * expert_flops,
            exps=per_core * capacity * hid,
            limit=56,
        )
        for chunk in range(len(sizes)):
            near, far = grads[2 * chunk : 2 * chunk + 2]
            open_flow((at, chunk), expert_flow(outs, near, far, at, sum(sizes[:chunk])))
        if fresh:
            open_flow("result", result_flow(mixed, *grads[-2:], branch))
        if at == 0:
            open_flow((0, "shared"), pack_flow(functools.partial(packed.put, 0, None, True), g_shared))
        own, sib = slot((at, "experts"), own, sib)
        part = join(own, sib, d_ffn)
        part = slot((at, "join"), *part)
        arrivals = tp_sum(part, functools.partial(slot, (at, "ffn half")))
        arrivals = slot((at, "ffn sum"), *arrivals)
        d_mixed, d_attn, gain = call(
            functools.partial(mix_back_kernel, parts=len(arrivals)),
            scal,
            (2,),
            [tiled(mixed), tiled(d_next)] + [whole(a) for a in arrivals] + weights,
            [tiled(row_f32), tiled(row_bf16), whole(sds((8, width), F32))],
        )
        gain_grads[layers + at] = gain[:1]
        kv_shape = sds((rows, 2 * heads_width), BF16)
        kv_outs = [kv_shape] * 2 if ctx == 2 else [sds((tree_len, 2 * heads_width), BF16)]
        dq, g_out, *dkv = call(
            functools.partial(attend_back_kernel, parts=len(kv)),
            scal,
            (2,),
            [whole(path), tiled(query), tiled(d_attn), tiled(heads)]
            + [whole(k) for k in kv]
            + weights,
            [tiled(sds((rows, heads_width), BF16)), whole(sds((width, heads_width), BF16))]
            + [whole(k) for k in kv_outs],
            scratch=[
                pltpu.VMEM((tree_len, 2 * heads_width), F32),
                pltpu.VMEM((width, heads_width), F32),
            ],
            flops=10 * rows * tree_len * heads_width + 2 * matrix * heads_width,
            exps=rows * tree_len * heads_width // HEAD_DIM,
            limit=56,
        )
        dq, *dkv = slot((at, "attention"), dq, *dkv)
        if ctx == 2:
            kv_own, kv_got = dkv[0], swap(dkv[1], "ctx", 1)
        else:
            parts = dkv[0].reshape((ctx, rows) + dkv[0].shape[1:])
            parts = lax.all_to_all(parts, "ctx", 0, 0, tiled=True)
            kv_own, kv_got = jnp.sum(parts.astype(F32), axis=0), jnp.zeros(kv_shape.shape, F32)
        *part, g0, g1, g2, g3 = call(
            functools.partial(project_back_kernel, chunks=CHUNKS),
            scal,
            (1,),
            [whole(a) for a in (dq, kv_own, kv_got, normed, g_out)] + weights,
            halves + [whole(sds((block, PACK), BF16))] * 4,
            flops=2 * matrix * 576,
        )
        g_attention = [g0, g1, g2, g3]
        if at == 0:
            open_flow((0, "attention"), pack_flow(functools.partial(packed.put, 0, 0, False), g_attention))
        else:
            both = [jnp.concatenate(g, axis=1) for g in zip(g_shared, g_attention)]
            open_flow((at, "packs"), pack_flow(functools.partial(packed.put, at, 3 * hid, True), both))
        part = slot((at, "project"), *part)
        arrivals = tp_sum(part, functools.partial(slot, (at, "attention half")))
        arrivals = slot((at, "attention sum"), *arrivals)
        final = at == 0
        *rest, gain = call(
            functools.partial(
                input_back_kernel, parts=len(arrivals), block=block, final=final
            ),
            scal,
            (2,),
            [tiled(stream), tiled(d_mixed)] + [whole(a) for a in arrivals] + weights,
            [tiled(row_f32)] + ([] if final else [tiled(row_bf16)]) + [whole(sds((8, width), F32))],
        )
        gain_grads[at] = gain[:1]
        d_next, *rest = slot((at, "input"), *rest)
        if not final:
            (d_branch,) = rest
    gains = jnp.concatenate(gain_grads, axis=0).astype(BF16)
    cuts = [gains[:, r * block : (r + 1) * block] for r in range(4)]
    open_flow("gains", pack_flow(lambda *v: gain_sums.extend(v), cuts))
    finish("gains")
    for step in TAIL:
        finish(*step)
    gains = gain_sums[0].astype(F32) + gain_sums[1].astype(F32)
    g_sin, g_sout, g_qkv, g_attention_out = packed.held
    g_in, g_out = outs.held
    blocks = hid // 128
    g_in = g_in.reshape(layers * experts * block, blocks, 2, 128).transpose(0, 2, 1, 3)
    g_sin = g_sin.reshape(layers * block, blocks, 2, 128).transpose(0, 2, 1, 3)
    return (
        result[0][None],
        d_next[None],
        gains[:layers],
        gains[layers:],
        g_qkv.transpose(0, 2, 1, 3),
        g_attention_out,
        g_sin.reshape(layers, block, 2, hid),
        g_sout.transpose(0, 2, 1),
        g_in.reshape(layers, experts, block, 2, hid),
        g_out.transpose(0, 1, 3, 2),
    )


def solution(mesh):
    return jax.shard_map(
        shards,
        mesh=mesh,
        in_specs=(
            P("fsdp", "ctx", None),
            P("fsdp", None),
            P("fsdp", "ctx", None),
            P("fsdp", "ctx", None),
            P(None, "fsdp"),
            P(None, "fsdp"),
            P(None, "fsdp", None, "tp"),
            P(None, "tp", "fsdp"),
            P(None, "fsdp", None, "tp"),
            P(None, "tp", "fsdp"),
            P(None, None, "fsdp", None, "tp"),
            P(None, None, "tp", "fsdp"),
            P("fsdp", "ctx", None),
        ),
        out_specs=(
            P("fsdp", "ctx", None),
            P("fsdp", "ctx", None),
            P(None, "fsdp"),
            P(None, "fsdp"),
            P(None, "fsdp", None, "tp"),
            P(None, "tp", "fsdp"),
            P(None, "fsdp", None, "tp"),
            P(None, "tp", "fsdp"),
            P(None, None, "fsdp", None, "tp"),
            P(None, None, "tp", "fsdp"),
        ),
        check_vma=False,
    )
```

```python
import functools

import jax
import jax.numpy as jnp
from jax import lax
from jax.experimental import pallas as pl
from jax.experimental.pallas import tpu as pltpu
from jax.sharding import PartitionSpec as P

HEAD_DIM = 64
EPS = 1e-06
SCALE = 0.125
MASKED = -1000000000.0
F32 = jnp.float32
BF16 = jnp.bfloat16
MIB = 1 << 20
LIGHT = 1000
KEYS, QUERY, OUT, GAINS, PACK = 0, 384, 640, 832, 896

NN = (((1,), (0,)), ((), ()))
NT = (((1,), (1,)), ((), ()))
TN = (((0,), (0,)), ((), ()))


def mm(a, b, dims=NN):
    return lax.dot_general(a, b, dims, preferred_element_type=F32)


def sds(shape, dtype):
    return jax.ShapeDtypeStruct(tuple(shape), dtype)


def swap(values, axis, mask):
    count = lax.axis_size(axis)
    return lax.ppermute(values, axis, [(k, k ^ mask) for k in range(count)])


def after(value, dep):
    return lax.optimization_barrier((value, dep))[0]


def add(a, b):
    return (a.astype(F32) + b.astype(F32)).astype(BF16)


def gather_blocks(values):
    far = swap(values, "fsdp", 2)
    return [values, swap(values, "fsdp", 1), far, swap(far, "fsdp", 1)]


def tp_sum(halves, between):
    count = lax.axis_size("tp")
    chunks = len(halves) // 2
    totals = [add(k, swap(g, "tp", 1)) for k, g in zip(halves[:chunks], halves[chunks:])]
    totals[0] = between(totals[0])[0]
    step = 2
    while step < count:
        totals = [add(total, swap(total, "tp", step)) for total in totals]
        step *= 2
    return list(totals) + [swap(total, "tp", 1) for total in totals]


def ctx_last(part):
    count = lax.axis_size("ctx")
    step = 1
    while step * 2 < count:
        part = add(part, swap(part, "ctx", step))
        step *= 2
    return part, swap(part, "ctx", step)


def call(
    kernel, scal, grid, ins, outs, scratch=(), flops=0, exps=0, alias=None, limit=20, light=LIGHT
):
    def spec(item):
        shape, block, index = item[0].shape, item[1], item[2]
        if block == "any":
            return pl.BlockSpec(memory_space=pl.ANY)
        if block is None:
            return pl.BlockSpec(shape, lambda *_: (0,) * len(shape))
        return pl.BlockSpec(block, index)

    size = lambda a: a.size * a.dtype.itemsize
    moved = sum(size(i[0]) for i in list(ins) + list(outs) if i[1] != "any" and len(i) < 4)
    moved += sum(i[3] for i in list(ins) + list(outs) if len(i) > 3)
    return pl.pallas_call(
        kernel,
        out_shape=[o[0] for o in outs],
        grid_spec=pltpu.PrefetchScalarGridSpec(
            num_scalar_prefetch=1,
            grid=grid,
            in_specs=[spec(i) for i in ins],
            out_specs=[spec(o) for o in outs],
            scratch_shapes=list(scratch),
        ),
        compiler_params=pltpu.CompilerParams(
            dimension_semantics=("arbitrary",) * len(grid), vmem_limit_bytes=limit * MIB
        ),
        cost_estimate=pl.CostEstimate(flops=flops // light, transcendentals=0, bytes_accessed=moved // light),
        input_output_aliases=alias or {},
    )(scal, *[i[0] for i in ins])


def whole(a):
    return (a, None, None)


def tiled(a):
    return (a, (a.shape[0] // 2,) + a.shape[1:], lambda t, *_: (t,) + (0,) * (len(a.shape) - 1))


def joined(refs, *at):
    return jnp.concatenate([ref[at] if at else ref[...] for ref in refs], axis=0)


def gain_row(pack_refs, which):
    cols = jnp.concatenate([ref[:, GAINS - 64 : PACK] for ref in pack_refs], axis=0)
    at = lax.broadcasted_iota(jnp.int32, (8, 128), 1)
    pick = jnp.where(at == 64 + which, 1.0, 0.0).astype(BF16)
    return mm(pick, cols, NT)[:1]


def swap_pairs(values, block):
    two = 2 * block
    return jnp.concatenate(
        [pltpu.roll(values[:, at : at + two], block, 1) for at in (0, two)], axis=1
    )


def relative(values, me, block):
    two = 2 * block
    far = jnp.concatenate([values[:, two:], values[:, :two]], axis=1)
    values = jnp.where((me & 2) > 0, far, values)
    return jnp.where((me & 1) > 0, swap_pairs(values, block), values)


def arrived(bit, refs):
    chunks = len(refs) // 2
    mine, other = joined(refs[:chunks]), joined(refs[chunks:])
    return jnp.where(pl.program_id(0) == bit, mine, other).astype(F32)


def put_halves(tile, bit, values, refs):
    chunks = len(refs) // 2
    rows = values.shape[0] // chunks
    values = values.astype(BF16)

    @pl.when(tile == bit)
    def _():
        for at in range(chunks):
            refs[at][...] = values[at * rows : (at + 1) * rows]

    @pl.when(tile != bit)
    def _():
        for at in range(chunks):
            refs[chunks + at][...] = values[at * rows : (at + 1) * rows]


def half_shapes(rows, width, chunks):
    return [whole(sds((rows // 2 // chunks, width), BF16)) for _ in range(2 * chunks)]


def normed_of(values, gain):
    inverse = lax.rsqrt(jnp.mean(values * values, axis=-1, keepdims=True) + EPS)
    scaled = values * inverse
    return scaled, inverse, scaled * gain


def norm_back(d_normed, values, gain):
    scaled, inverse, _ = normed_of(values, gain)
    d_scaled = d_normed * gain
    mean = jnp.mean(d_scaled * scaled, axis=-1, keepdims=True)
    return inverse * (d_scaled - scaled * mean), jnp.sum(d_normed * scaled, axis=0, keepdims=True)


def order_kernel(scal, tok_ref, cot_ref, tok_out, cot_out, *, block):
    for src, dst in ((tok_ref, tok_out), (cot_ref, cot_out)):
        dst[...] = relative(src[...].astype(F32), scal[0], block).astype(BF16)


def project(stream, packs, normed_ref, q_ref, kv_ref):
    _, _, normed = normed_of(stream, gain_row(packs, 0))
    normed = normed.astype(BF16)
    normed_ref[...] = normed
    weight = joined(packs)
    kv_ref[...] = mm(normed, weight[:, KEYS:QUERY]).astype(BF16)
    q_ref[...] = mm(normed, weight[:, QUERY : QUERY + q_ref.shape[1]]).astype(BF16)


def first_kernel(scal, tok_ref, *refs):
    project(tok_ref[...].astype(F32), refs[:4], *refs[4:])


def next_kernel(scal, mixed_ref, *refs, parts):
    stream = mixed_ref[...] + arrived(scal[1], refs[:parts])
    packs, (stream_ref, *outs) = refs[parts : parts + 4], refs[parts + 4 :]
    stream_ref[...] = stream
    project(stream, packs, *outs)


def last_kernel(scal, mixed_ref, *refs, block):
    result = mixed_ref[...] + arrived(scal[1], refs[:-1])
    refs[-1][...] = relative(result, scal[0], block).astype(BF16)


def allowed_of(scal, path_ref, rows, tree_len):
    first = scal[3] + pl.program_id(0) * rows
    query_pos = first + lax.broadcasted_iota(jnp.int32, (rows, tree_len), 0)
    key_pos = lax.broadcasted_iota(jnp.int32, (rows, tree_len), 1)
    return (key_pos <= query_pos) & (path_ref[...] > 0.5)


def softmax_of(query, key, allowed):
    scores = jnp.where(allowed, mm(query, key, NT) * SCALE, MASKED)
    expo = jnp.exp(scores - jnp.max(scores, axis=-1, keepdims=True))
    return expo * (1.0 / jnp.sum(expo, axis=-1, keepdims=True))


def head_cols(width):
    return [slice(at, at + HEAD_DIM) for at in range(0, width, HEAD_DIM)]


def all_keys(scal, refs):
    if len(refs) == 1:
        return refs[0][...]
    own, got = refs[0][...], refs[1][...]
    first = scal[4] == 0
    return jnp.concatenate([jnp.where(first, own, got), jnp.where(first, got, own)], axis=0)


def attend_kernel(scal, path_ref, q_ref, *refs, parts):
    kv_ref, refs = all_keys(scal, refs[:parts]), refs[parts:]
    packs, heads_ref, halves = refs[:4], refs[4], refs[5:]
    rows, width = q_ref.shape
    allowed = allowed_of(scal, path_ref, rows, kv_ref.shape[0])
    outs = []
    for cols in head_cols(width):
        vals = slice(width + cols.start, width + cols.stop)
        probs = softmax_of(q_ref[:, cols], kv_ref[:, cols], allowed).astype(BF16)
        outs.append(mm(probs, kv_ref[:, vals]))
    heads = jnp.concatenate(outs, axis=1).astype(BF16)
    heads_ref[...] = heads
    weight = jnp.concatenate([ref[:, OUT : OUT + width] for ref in packs], axis=0)
    put_halves(pl.program_id(0), scal[1], mm(heads, weight, NT), halves)


def attend_back_kernel(scal, path_ref, q_ref, d_ref, heads_ref, *refs, parts):
    kv_ref, refs = all_keys(scal, refs[:parts]), refs[parts:]
    packs, (dq_ref, gout_ref), (dkv_refs, scratch) = refs[:4], refs[4:6], (refs[6:-2], refs[-2:])
    dkv_acc, gout_acc = scratch
    rows, width = q_ref.shape
    tile = pl.program_id(0)
    allowed = allowed_of(scal, path_ref, rows, kv_ref.shape[0])

    @pl.when(tile == 0)
    def _():
        dkv_acc[...] = jnp.zeros_like(dkv_acc)
        gout_acc[...] = jnp.zeros_like(gout_acc)

    weight = jnp.concatenate([ref[:, OUT : OUT + width] for ref in packs], axis=0)
    d_heads = mm(d_ref[...], weight).astype(BF16)
    gout_acc[...] += mm(d_ref[...], heads_ref[...], TN)
    dqs, dks, dvs = [], [], []
    for cols in head_cols(width):
        vals = slice(width + cols.start, width + cols.stop)
        query, key, value, d_out = q_ref[:, cols], kv_ref[:, cols], kv_ref[:, vals], d_heads[:, cols]
        probs = softmax_of(query, key, allowed)
        d_prob = mm(d_out, value, NT)
        weighted = jnp.sum(probs * d_prob, axis=-1, keepdims=True)
        d_scores = (probs * (d_prob - weighted)).astype(BF16)
        dqs.append(mm(d_scores, key) * SCALE)
        dks.append(mm(d_scores, query, TN) * SCALE)
        dvs.append(mm(probs.astype(BF16), d_out, TN))
    dq_ref[...] = jnp.concatenate(dqs, axis=1).astype(BF16)
    dkv_acc[...] += jnp.concatenate(dks + dvs, axis=1)

    @pl.when(tile == pl.num_programs(0) - 1)
    def _():
        gout_ref[...] = gout_acc[...].astype(BF16)
        if len(dkv_refs) == 1:
            dkv_refs[0][...] = dkv_acc[...].astype(BF16)
        else:
            half = dkv_refs[0].shape[0]
            for at in range(2):
                part = dkv_acc[at * half : (at + 1) * half, :].astype(BF16)
                mine = scal[3] == at * half

                @pl.when(mine)
                def _():
                    dkv_refs[0][...] = part

                @pl.when(jnp.logical_not(mine))
                def _():
                    dkv_refs[1][...] = part


def project_back_kernel(scal, dq_ref, own_ref, got_ref, normed_ref, gout_ref, *refs, chunks):
    packs, halves, grads = refs[:4], refs[4 : 4 + 2 * chunks], refs[4 + 2 * chunks :]
    d_kv = (own_ref[...].astype(F32) + got_ref[...].astype(F32)).astype(BF16)
    d_q, normed = dq_ref[...], normed_ref[...]
    width = d_q.shape[1]
    weight = joined(packs)
    part = mm(d_kv, weight[:, KEYS:QUERY], NT) + mm(d_q, weight[:, QUERY : QUERY + width], NT)
    half = part.shape[0] // 2
    for at in range(2):
        put_halves(at, scal[1], part[at * half : (at + 1) * half], halves)
    g_kv, g_q, g_out = mm(normed, d_kv, TN), mm(normed, d_q, TN), gout_ref[...]
    rows = grads[0].shape[0]
    for at, ref in enumerate(grads):
        cut = slice(at * rows, (at + 1) * rows)
        ref[...] = jnp.zeros_like(ref)
        ref[:, KEYS:QUERY] = g_kv[cut].astype(BF16)
        ref[:, QUERY : QUERY + width] = g_q[cut].astype(BF16)
        ref[:, OUT : OUT + width] = g_out[cut]


def mix_kernel(scal, stream_ref, *refs, parts):
    mixed = stream_ref[...].astype(F32) + arrived(scal[1], refs[:parts])
    packs, (mixed_ref, in_ref) = refs[parts : parts + 4], refs[parts + 4 :]
    mixed_ref[...] = mixed
    in_ref[...] = normed_of(mixed, gain_row(packs, 1))[2].astype(BF16)


def shared_kernel(scal, in_ref, *refs):
    packs, (branch_ref, gate_ref, up_ref) = refs[:12], refs[12:]
    gate = mm(in_ref[...], joined(packs[:4]))
    up = mm(in_ref[...], joined(packs[4:8]))
    gate_ref[...] = gate
    up_ref[...] = up
    hidden = (gate / (1.0 + jnp.exp(-gate)) * up).astype(BF16)
    branch_ref[...] = mm(hidden, joined(packs[8:]), NT)


def glu_back(gate, up, d_hidden):
    sigmoid = 1.0 / (1.0 + jnp.exp(-gate))
    active = gate * sigmoid
    hidden = (active * up).astype(BF16)
    d_gate = (d_hidden * up * (sigmoid * (1.0 + gate * (1.0 - sigmoid)))).astype(BF16)
    return hidden, d_gate, (d_hidden * active).astype(BF16)


def shared_back_kernel(scal, d_ref, in_ref, gate_ref, up_ref, *refs):
    packs, (out_ref, *grad_refs) = refs[:12], refs[12:]
    hid = gate_ref.shape[1]
    cut = lambda at: joined(packs[4 * at : 4 * at + 4])
    d_branch, ffn_in = d_ref[...], in_ref[...]
    hidden, d_gate, d_up = glu_back(gate_ref[...], up_ref[...], mm(d_branch, cut(2)))
    out_ref[...] = mm(d_gate, cut(0), NT) + mm(d_up, cut(1), NT)
    grads = (mm(ffn_in, d_gate, TN), mm(ffn_in, d_up, TN), mm(d_branch, hidden, TN))
    rows = grad_refs[0].shape[0]
    for at, grad in enumerate(grads):
        for r, ref in enumerate(grad_refs):
            ref[:, at * hid : (at + 1) * hid] = grad[r * rows : (r + 1) * rows].astype(BF16)


def column(table_ref, rows, at):
    values = table_ref[rows, :]
    lane = lax.broadcasted_iota(jnp.int32, values.shape, 1)
    return jnp.sum(jnp.where(lane == at, values, 0.0), axis=1, keepdims=True)


def spread(first, second, places, weights):
    one, two = weights
    return jnp.where(places == first, one, jnp.where(places == second, two, 0.0)).astype(BF16)


def rows_of(lists_ref, half, tokens, slots, weighted):
    cut = slice(half * tokens, (half + 1) * tokens)
    first, second, one, two = [lists_ref[at : at + 1, cut] for at in range(4)]
    places = lax.broadcasted_iota(jnp.int32, (slots, tokens), 0)
    weights = (one, two) if weighted else (1.0, 1.0)
    return spread(first.astype(jnp.int32), second.astype(jnp.int32), places, weights)


def cols_of(table_ref, half, tokens, slots, weighted):
    cut = slice(half * tokens, (half + 1) * tokens)
    first, second = [column(table_ref, cut, at).astype(jnp.int32) for at in range(2)]
    weights = [column(table_ref, cut, at) for at in (2, 3)] if weighted else (1.0, 1.0)
    places = lax.broadcasted_iota(jnp.int32, (tokens, slots), 1)
    return spread(first, second, places, weights)


def to_slots(own_ref, sib_ref, lists_ref, slot_ref, block, weighted):
    @pl.when(pl.program_id(0) == 0)
    def _():
        tokens, slots = own_ref.shape[0], slot_ref.shape[1]
        sib = swap_pairs(sib_ref[...].astype(F32), block).astype(BF16)
        for half, values in enumerate((own_ref[...], sib)):
            picks = rows_of(lists_ref, half, tokens, slots, weighted)
            slot_ref[half] = mm(picks, values).astype(BF16)


def from_slots(slot_ref, table_ref, own_out, sib_out, weighted):
    @pl.when(pl.program_id(0) == pl.num_programs(0) - 1)
    def _():
        tokens, slots = own_out.shape[0], slot_ref.shape[1]
        for half, ref in enumerate((own_out, sib_out)):
            picks = cols_of(table_ref, half, tokens, slots, weighted)
            ref[...] = mm(picks, slot_ref[half]).astype(ref.dtype)


def of_expert(slot_ref):
    count = slot_ref.shape[1] // pl.num_programs(0)
    rows = pl.ds(pl.multiple_of(pl.program_id(0) * count, count), count)
    return jnp.concatenate([slot_ref[0, rows, :], slot_ref[1, rows, :]], axis=0)


def put_expert(slot_ref, values):
    count = slot_ref.shape[1] // pl.num_programs(0)
    rows = pl.ds(pl.multiple_of(pl.program_id(0) * count, count), count)
    slot_ref[0, rows, :] = values[:count]
    slot_ref[1, rows, :] = values[count:]


def pack_kernel(scal, in_ref, out_ref, own_ref, first_ref, last_ref):
    third = first_ref.shape[2]
    own_ref[0, :2] = pltpu.einshape("dkf->kdf", in_ref[0, 0])
    own_ref[0, 2] = out_ref[0, 0]
    first_ref[0] = own_ref[0, :, pl.ds(pl.multiple_of(scal[4] * third, third), third), :]
    last_ref[0] = own_ref[0, :, 2 * third :, :]


def expert_weights(scal, refs):
    def far(refs, part):
        straight, around, last = [ref[0, part] for ref in refs]
        low = jnp.where(scal[4] == 0, straight, around)
        middle = jnp.where(scal[4] == 0, around, straight)
        return [low, middle, last]

    return [
        jnp.concatenate(
            [refs[0][0, part], refs[1][0, part]] + far(refs[2:5], part) + far(refs[5:8], part), axis=0
        )
        for part in range(3)
    ]


def expert_kernel(scal, own_ref, sib_ref, lists_ref, table_ref, *refs, block, sources):
    weights, (own_out, sib_out, x_ref, gate_ref, up_ref, x_all, y_all) = refs[:sources], refs[sources:]
    to_slots(own_ref, sib_ref, lists_ref, x_all, block, False)
    w_gate, w_up, w_out = expert_weights(scal, weights)
    chosen = of_expert(x_all)
    gate = mm(chosen, w_gate)
    up = mm(chosen, w_up)
    x_ref[0], gate_ref[0], up_ref[0] = chosen, gate.astype(BF16), up.astype(BF16)
    hidden = (gate / (1.0 + jnp.exp(-gate)) * up).astype(BF16)
    put_expert(y_all, mm(hidden, w_out, NT).astype(BF16))
    from_slots(y_all, table_ref, own_out, sib_out, True)


def expert_back_kernel(
    scal, own_ref, sib_ref, lists_ref, table_ref, a_ref, b_ref, *refs, block, sizes, sources, fresh
):
    given, refs = ((), refs) if fresh else (refs[:1], refs[1:])
    weights, refs = refs[:sources], refs[sources:]
    (own_out, sib_out), grads, refs = refs[:2], refs[2 : 2 + 2 * len(sizes)], refs[2 + 2 * len(sizes) :]
    to_slots(own_ref, sib_ref, lists_ref, refs[-1], block, True)
    w_gate, w_up, w_out = expert_weights(scal, weights)
    d_rows = of_expert(refs[-1])
    if fresh:
        own_next, sib_next, x_all, y_all = refs[:4]
        to_slots(a_ref, b_ref, lists_ref, x_all, block, False)
        chosen = of_expert(x_all)
        gate, up = mm(chosen, w_gate), mm(chosen, w_up)
    else:
        chosen, gate, up = a_ref[0], b_ref[0].astype(F32), given[0][0].astype(F32)
    hidden, d_gate, d_up = glu_back(gate, up, mm(d_rows, w_out))
    if fresh:
        put_expert(y_all, mm(hidden, w_out, NT).astype(BF16))
        from_slots(y_all, table_ref, own_next, sib_next, True)
    step = pl.program_id(0)
    parts = (mm(chosen, d_gate, TN), mm(chosen, d_up, TN), mm(d_rows, hidden, TN))
    parts = [p.astype(BF16) for p in parts]
    for chunk, size in enumerate(sizes):
        first = sum(sizes[:chunk])

        @pl.when((step >= first) & (step < first + size))
        def _():
            for at in range(3):
                grads[2 * chunk][0, at] = parts[at][: 2 * block]
                grads[2 * chunk + 1][0, at] = parts[at][2 * block :]

    d_x = mm(d_gate, w_gate, NT) + mm(d_up, w_up, NT)
    put_expert(refs[-1], d_x.astype(BF16))
    from_slots(refs[-1], table_ref, own_out, sib_out, False)


def join_kernel(scal, own_ref, got_ref, shared_ref, *halves, block):
    part = own_ref[...] + shared_ref[...] + swap_pairs(got_ref[...].astype(F32), block)
    put_halves(pl.program_id(0), scal[1], part, halves)


def mix_back_kernel(scal, mixed_ref, next_ref, *refs, parts):
    packs, (d_ref, attn_ref, gain_ref) = refs[parts : parts + 4], refs[parts + 4 :]
    back, gain_grad = norm_back(arrived(scal[1], refs[:parts]), mixed_ref[...], gain_row(packs, 1))
    d_mixed = back + next_ref[...].astype(F32)
    d_ref[...] = d_mixed
    attn_ref[...] = d_mixed.astype(BF16)
    sum_tiles(gain_ref, gain_grad)


def sum_tiles(ref, value):
    value = jnp.broadcast_to(value, ref.shape)

    @pl.when(pl.program_id(0) == 0)
    def _():
        ref[...] = value

    @pl.when(pl.program_id(0) > 0)
    def _():
        ref[...] += value


def input_back_kernel(scal, stream_ref, mixed_ref, *refs, parts, block, final):
    packs, outs = refs[parts : parts + 4], refs[parts + 4 :]
    stream = stream_ref[...].astype(F32)
    back, gain_grad = norm_back(arrived(scal[1], refs[:parts]), stream, gain_row(packs, 0))
    d_stream = back + mixed_ref[...]
    if final:
        outs[0][...] = relative(d_stream, scal[0], block)
    else:
        outs[0][...] = d_stream
        outs[1][...] = d_stream.astype(BF16)
    sum_tiles(outs[-1], gain_grad)


def store_expert(in_ref, out_ref, gate, up, out):
    blocks = gate.shape[1] // 128
    for at, part in enumerate((gate, up)):
        for col in range(blocks):
            rows = pl.ds(col * 2 + at, part.shape[0], stride=2 * blocks)
            in_ref[0, 0, rows, :] = part[:, col * 128 : (col + 1) * 128]
    out_ref[0, 0] = out


def own_kernel(scal, part_ref, got_ref, *refs):
    give_ref, in_ref, out_ref = refs[-3:]
    half = give_ref.shape[2]
    total = [part_ref[0, at].astype(F32) + got_ref[0, at].astype(F32) for at in range(3)]
    for at in range(3):
        give_ref[0, at] = total[at][half:].astype(BF16)
    store_expert(in_ref, out_ref, *[t[:half] for t in total])


def other_kernel(scal, got_ref, *refs):
    store_expert(*refs[-2:], *[got_ref[0, at].astype(F32) for at in range(3)])


def packed_kernel(scal, part_ref, got_ref, *refs, first, shared, blocks):
    total = part_ref[...].astype(F32) + got_ref[...].astype(F32)
    if first is not None:
        refs, (qkv_ref, out_ref) = refs[:-2], refs[-2:]
        width = qkv_ref.shape[3]
        for at, col in enumerate((QUERY, KEYS, KEYS + width)):
            qkv_ref[0, at] = total[:, first + col : first + col + width]
        out_ref[0] = total[:, first + OUT : first + OUT + width].T
    if shared:
        sin_ref, sout_ref = refs[-2:]
        hid = sout_ref.shape[2]
        for at in range(2):
            for col in range(blocks):
                rows = pl.ds(col * 2 + at, total.shape[0], stride=2 * blocks)
                lanes = at * hid + col * 128
                sin_ref[0, rows, :] = total[:, lanes : lanes + 128]
        sout_ref[0] = total[:, 2 * hid : 3 * hid]

CHUNKS, PARTS = 2, ((2, 2), (1, 1, 2))
SLOTS = {
    "start": ["pack 0", ("experts", 0)],
    ("attend", 0): ["slots"],
    ("attend half", 0): [("experts", 0), "pack 1"],
    ("attend sum", 0): ["pack 2", ("experts", 1)],
    ("mixed", 0): [("experts", 0), "pack 1"],
    ("experts", 0): ["pack 1", "pack 2", ("experts", 1)],
    ("branch sum", 0): ["pack 2", ("experts", 1)],
    ("attend", 1): [("experts", 1)],
    ("mixed", 1): [("experts", 1)],
    (1, "experts"): [(1, 0)],
    (1, "ffn half"): [(1, 1)],
    (1, "ffn sum"): [(1, 0), (1, 2)],
    (1, "attention"): [(1, 1)],
    (1, "project"): [(1, "packs")],
    (1, "attention half"): [(1, 0), (1, 2)],
    (1, "attention sum"): [(1, "packs")],
    (1, "input"): [(1, 0), (1, 1)],
    (0, "experts"): [(1, 2), (1, "packs"), (0, 0)],
    (0, "ffn half"): [(1, 1), "result"],
    (0, "ffn sum"): [(1, 2), "result", (0, 0), (0, 1), (0, "shared")],
    (0, "attention"): [(1, "packs")],
    (0, "project"): [(0, "attention"), "result"],
    (0, "attention half"): [(0, 0), (0, 1), (0, "shared")],
    (0, "attention sum"): [(0, 0)],
    (0, "input"): [(0, 1), (0, "shared"), (0, "attention")],
}
TAIL = (
    ["gains", (0, 1), (0, "shared"), (0, "attention")],
    ["gains", (0, "attention")],
    ["gains"],
)


class Packs:
    def __init__(self, scal, layers, block, hid, width):
        self.scal, self.blocks = scal, hid // 128
        self.shapes = (
            sds((layers, block * 2 * self.blocks, 128), F32),
            sds((layers, block, hid), F32),
            sds((layers, 3, block, width), F32),
            sds((layers, width, block), F32),
        )
        self.held = [None] * 4

    def put(self, layer, first, shared, part, got):
        used = [0, 1] * shared + [2, 3] * (first is not None)
        before = [at for at in used if self.held[at] is not None]
        slot = lambda s: (s, (1,) + s.shape[1:], lambda *_: (layer,) + (0,) * (len(s.shape) - 1))
        results = call(
            functools.partial(packed_kernel, first=first, shared=shared, blocks=self.blocks),
            self.scal,
            (1,),
            [whole(part), whole(got)] + [(self.held[at], "any", None) for at in before],
            [slot(self.shapes[at]) for at in used],
            alias={3 + n: used.index(at) for n, at in enumerate(before)},
            limit=10,
        )
        for at, result in zip(used, results):
            self.held[at] = result


class Outs:
    def __init__(self, scal, layers, experts, block, hid):
        self.scal, self.per_core = scal, experts // 2
        self.shapes = (
            sds((layers, experts, block * 2 * hid // 128, 128), F32),
            sds((layers, experts, block, hid), F32),
        )
        self.held = None

    def put(self, kernel, ins, extra, layer, first, other):
        count = ins[0].shape[0]
        lead = lambda a: (a, (1,) + a.shape[1:], lambda e, s: (e, 0, 0, 0))
        place = lambda e, s: (layer, (s[2] ^ other) * self.per_core + first + e, 0, 0)
        moved = lambda s: count * s.size * 4 // (s.shape[0] * s.shape[1])
        slot = lambda s: (s, (1, 1) + s.shape[2:], place, moved(s))
        held = [] if self.held is None else [(h, "any", None) for h in self.held]
        base = 1 + len(ins)
        *rest, gin, gout = call(
            kernel,
            self.scal,
            (count,),
            [lead(i) for i in ins] + held,
            [lead(x) for x in extra] + [slot(s) for s in self.shapes],
            alias={base + at: len(extra) + at for at in range(len(held))},
            limit=10,
        )
        self.held = (gin, gout)
        return rest


def expert_flow(outs, near, far, layer, first):
    near, far = yield [near, far]
    near, got = yield [near, swap(far, "fsdp", 2)]
    part, got = yield list(ctx_last(add(near, got)))
    block = near.shape[2] // 2
    give = sds(near.shape[:2] + (block,) + near.shape[3:], BF16)
    (give,) = outs.put(own_kernel, (part, got), (give,), layer, first, 0)
    (got,) = yield [swap(give, "fsdp", 1)]
    outs.put(other_kernel, (got,), (), layer, first, 1)
    yield []


def pack_flow(done, parts):
    parts = yield list(parts)
    own, far, got, far_got = yield [parts[0], parts[2], swap(parts[1], "fsdp", 1), swap(parts[3], "fsdp", 1)]
    own, far = add(own, got), add(far, far_got)
    own, got = yield [own, swap(far, "fsdp", 2)]
    part, got = yield list(ctx_last(add(own, got)))
    done(part, got)
    yield []


def weight_flow(place, at, own, first, last):
    own, first, last = yield [own, first, last]
    if at > 0:
        own, first, last = yield [own, first, last]
    own, sib, straight, last = yield [own, swap(own, "fsdp", 1), swap(first, "fsdp", 2), last]
    last = swap(last, "fsdp", 2)
    if at > 0:
        (straight,) = yield [straight]
    around, cross = swap(straight, "ctx", 1), swap(straight, "fsdp", 1)
    straight, around, last, cross = yield [straight, around, last, cross]
    place[at] = [own, sib, straight, around, last]
    place[at] += [cross, swap(around, "fsdp", 1), swap(last, "fsdp", 1)]
    yield []


def block_flow(place, at, own):
    (own,) = yield [own]
    (own,) = yield [own]
    own, far = yield [own, swap(own, "fsdp", 2)]
    place[at] = [own, swap(own, "fsdp", 1), far, swap(far, "fsdp", 1)]
    yield []


def ancestry(parent_row):
    count = parent_row.shape[0]
    block_ids = jnp.arange(count, dtype=jnp.int32)
    step_map = ((parent_row[:, None] == block_ids[None, :]) & (block_ids[:, None] > 0)).astype(F32)
    reach = on_path = jnp.eye(count, dtype=F32)
    for _ in range(count):
        reach = jnp.dot(reach, step_map, precision=lax.Precision.HIGHEST)
        on_path = on_path + reach
    return on_path


def shards(
    tokens,
    parents,
    routes,
    gates,
    attn_gain,
    ffn_gain,
    qkv_weight,
    out_weight,
    shared_in,
    shared_out,
    expert_in,
    expert_out,
    cotangent,
):
    rows, width = tokens.shape[1], tokens.shape[2]
    layers, experts = expert_in.shape[0], expert_in.shape[1]
    block, heads_width = qkv_weight.shape[1], qkv_weight.shape[3]
    hid = expert_in.shape[4]
    ctx = lax.axis_size("ctx")
    tree_len = rows * ctx
    me, here = lax.axis_index("fsdp"), lax.axis_index("ctx")
    core, bit = me & 1, lax.axis_index("tp") & 1
    half_at = here & 1
    per_core = experts // 2
    capacity = 2 * (3 * rows // 8)
    scal = jnp.stack([me, bit, core, here * rows, half_at]).astype(jnp.int32)

    def pack_attention(at):
        cols = [qkv_weight[at][:, part] for part in (1, 2, 0)]
        pad = jnp.zeros((block, OUT - QUERY - heads_width), BF16)
        gains = jnp.stack([attn_gain[at], ffn_gain[at]], axis=1)
        tail = jnp.zeros((block, PACK - GAINS - 2), BF16)
        return jnp.concatenate(cols + [pad, out_weight[at].T, gains, tail], axis=1)

    def pack_shared(at):
        return [shared_in[at].reshape(block, 2 * hid), shared_out[at].T]

    eout = expert_out.transpose(0, 1, 3, 2)

    def pack_experts(at):
        third = block // 3
        whole_pack = sds((experts, 3, block, hid), BF16)
        part = sds((experts, 3, third, hid), BF16)
        lead = lambda a: (a, (1,) + a.shape[1:], lambda e, s: (e, 0, 0, 0))
        return call(
            pack_kernel,
            scal,
            (experts,),
            [
                (expert_in, (1, 1) + expert_in.shape[2:], lambda e, s: (at, e, 0, 0, 0)),
                (eout, (1, 1) + eout.shape[2:], lambda e, s: (at, e, 0, 0)),
            ],
            [lead(whole_pack), lead(part), lead(part)],
            limit=10,
        )

    ancestors = ancestry(parents[0])
    segment = tree_len // ancestors.shape[0]
    anc_row = lax.dynamic_slice_in_dim(ancestors, here * rows // segment, 1, 0)
    path = jnp.repeat(anc_row, segment, axis=1)

    places = 3 * rows // 8
    info = jnp.concatenate([routes[0].astype(F32), gates[0]], axis=1)
    info = jnp.concatenate([info, swap(info, "fsdp", 1)], axis=0)
    local = info[:, :2].astype(jnp.int32) - core * per_core
    hits = local[:, :, None] == jnp.arange(per_core, dtype=jnp.int32)
    at = jnp.arange(2 * rows)
    earlier = (at[:, None] > at[None, :]) & (at[:, None] // rows == at[None, :] // rows)
    before = mm(earlier.astype(BF16), jnp.any(hits, axis=1).astype(BF16))
    slot = before[:, None, :] + places * jnp.arange(per_core, dtype=F32)
    slot = jnp.sum(jnp.where(hits, slot + 1.0, 0.0), axis=2) - 1.0
    table = jnp.concatenate([slot, info[:, 2:]], axis=1)

    lead = lambda a: (
        a,
        (1,) + tuple(a.shape[1:]),
        lambda e, s: (e,) + (0,) * (len(a.shape) - 1),
    )

    matrix = 2 * rows * width
    expert_flops = 2 * per_core * capacity * width * hid
    slot_scratch = [pltpu.VMEM((2, per_core * places, width), BF16)]
    halves = half_shapes(rows, width, CHUNKS)
    row_f32, row_bf16 = sds((rows, width), F32), sds((rows, width), BF16)

    flows, held = {}, {}

    def open_flow(name, flow):
        flows[name] = flow
        held[name] = next(flow)

    def slot(name, *values):
        names = SLOTS.get(name, ())
        if not names:
            return list(values)
        values, arrays = lax.optimization_barrier((list(values), [held[n] for n in names]))
        for n, a in zip(names, arrays):
            if n == "slots":
                tables.extend(a)
            else:
                held[n] = flows[n].send(a)
        return values

    tables = []

    def finish(*names):
        for name in names:
            held[name] = flows[name].send(held[name])

    small, routed = {}, {}
    open_flow("pack 0", block_flow(small, 0, pack_attention(0)))
    for at in range(layers):
        open_flow(("experts", at), weight_flow(routed, at, *pack_experts(at)))
    open_flow("pack 1", block_flow(small, 1, jnp.concatenate(pack_shared(0), axis=1)))
    rest = [pack_attention(at) for at in range(1, layers)]
    rest = [v for pack in rest for v in (pack, jnp.zeros((block, 128), BF16))]
    rest += [v for at in range(1, layers) for v in pack_shared(at)]
    open_flow("pack 2", block_flow(small, 2, jnp.concatenate(rest, axis=1)))

    held["slots"] = [table.T, table]

    def attention_ins(at):
        if at == 0:
            return [whole(p) for p in small[0]]
        return [(p, (block, 1024), lambda *_: (0, at - 1)) for p in small[2]]

    def shared_ins(at):
        packs, first = (small[1], 0) if at == 0 else (small[2], 1024 * (layers - 1) // hid + 3 * at - 3)
        index = lambda which: lambda *_: (0, first + which)
        return [(p, (block, hid), index(which)) for which in range(3) for p in packs]

    def expert_ins(at):
        index = lambda e, s: (s[2] * per_core + e, 0, 0, 0)
        return [(a, (1,) + a.shape[1:], index) for a in routed[at]]

    stream, cot = call(
        functools.partial(order_kernel, block=block),
        scal,
        (2,),
        [tiled(tokens[0]), tiled(cotangent[0])],
        [tiled(row_bf16)] * 2,
    )
    finish("pack 0")
    finish("pack 0")
    slot("start")

    def experts_forward(at, own_in, sib_in):
        kept = [lead(sds((per_core, capacity, width), BF16))]
        kept += [lead(sds((per_core, capacity, hid), BF16))] * 2
        return call(
            functools.partial(
                expert_kernel, block=block, sources=len(routed[at])
            ),
            scal,
            (per_core,),
            [whole(own_in), whole(sib_in), whole(tables[0]), whole(tables[1])] + expert_ins(at),
            [whole(row_f32), whole(row_bf16)] + kept,
            scratch=slot_scratch * 2,
            flops=5 * expert_flops,
            limit=32,
        )

    def join(own, sib, shared_part):
        return call(
            functools.partial(join_kernel, block=block),
            scal,
            (2,),
            [tiled(own), tiled(swap(sib, "fsdp", 1)), tiled(shared_part)],
            halves,
        )

    def result_flow(mixed, own, sib, branch):
        own, sib = yield [own, sib]
        part = yield list(join(own, sib, branch))
        arrivals = yield tp_sum(part, lambda *values: values)
        (result[0],) = call(
            functools.partial(last_kernel, block=block),
            scal,
            (2,),
            [tiled(mixed)] + [whole(a) for a in arrivals],
            [tiled(row_bf16)],
        )
        yield []

    result = [None]
    saved = []
    mixed = arrivals = None
    for at in range(layers):
        outs = [
            tiled(row_bf16),
            tiled(sds((rows, heads_width), BF16)),
            tiled(sds((rows, 2 * heads_width), BF16)),
        ]
        weights = attention_ins(at)
        if at == 0:
            normed, query, kv = call(
                first_kernel, scal, (2,), [tiled(stream)] + weights, outs, flops=matrix * 576
            )
        else:
            stream, normed, query, kv = call(
                functools.partial(next_kernel, parts=len(arrivals)),
                scal,
                (2,),
                [tiled(mixed)] + [whole(a) for a in arrivals] + weights,
                [tiled(row_f32)] + outs,
                flops=matrix * 576,
            )
        (kv,) = slot(("project", at), kv)
        if ctx == 2:
            kv = [kv, swap(kv, "ctx", 1)]
        else:
            kv = [lax.all_gather(kv, "ctx", axis=0, tiled=True)]
        heads, *part = call(
            functools.partial(attend_kernel, parts=len(kv)),
            scal,
            (2,),
            [whole(path), tiled(query)] + [whole(k) for k in kv] + weights,
            [tiled(sds((rows, heads_width), BF16))] + halves,
            flops=4 * rows * tree_len * heads_width + matrix * heads_width,
            exps=rows * tree_len * heads_width // HEAD_DIM,
            limit=24,
        )
        part = slot(("attend", at), *part)
        arrivals = tp_sum(part, functools.partial(slot, ("attend half", at)))
        arrivals = slot(("attend sum", at), *arrivals)
        mixed, ffn_in = call(
            functools.partial(mix_kernel, parts=len(arrivals)),
            scal,
            (2,),
            [tiled(stream)] + [whole(a) for a in arrivals] + weights,
            [tiled(row_f32), tiled(row_bf16)],
        )
        sib_in = swap(ffn_in, "fsdp", 1)
        ffn_in, sib_in = slot(("mixed", at), ffn_in, sib_in)
        if at + 1 < layers:
            own, sib, *hidden = experts_forward(at, ffn_in, sib_in)
            own, sib = slot(("experts", at), own, sib)
        branch, gate, up = call(
            shared_kernel,
            scal,
            (2,),
            [tiled(ffn_in)] + shared_ins(at),
            [tiled(row_f32)] + [tiled(sds((rows, hid), F32))] * 2,
            flops=3 * matrix * hid,
            exps=rows * hid,
        )
        if at + 1 < layers:
            part = join(own, sib, branch)
            part = slot(("join", at), *part)
            arrivals = tp_sum(part, functools.partial(slot, ("branch half", at)))
            arrivals = slot(("branch sum", at), *arrivals)
        else:
            hidden = [ffn_in, sib_in]
        saved.append((stream, normed, query, kv, heads, mixed, ffn_in, gate, up, hidden))

    outs = Outs(scal, layers, experts, block, hid)
    packed = Packs(scal, layers, block, hid, heads_width)
    gain_sums = []
    gain_grads = [None] * (2 * layers)
    d_next, d_branch = cot, cot
    for at in reversed(range(layers)):
        stream, normed, query, kv, heads, mixed, ffn_in, gate, up, hidden = saved[at]
        weights = attention_ins(at)
        sib_d = swap(d_branch, "fsdp", 1)
        d_ffn, *g_shared = call(
            shared_back_kernel,
            scal,
            (1,),
            [whole(a) for a in (d_branch, ffn_in, gate, up)] + shared_ins(at),
            [whole(row_f32)] + [whole(sds((block, 3 * hid), BF16))] * 4,
            flops=6 * matrix * hid,
            exps=rows * hid,
        )
        sizes = PARTS[at]
        fresh = len(hidden) == 2
        part_of = lambda first, size: (
            sds((size, 3, 2 * block, hid), BF16),
            (1, 3, 2 * block, hid),
            lambda e, s: (jnp.clip(e - first, 0, size - 1), 0, 0, 0),
        )
        own, sib, *grads = call(
            functools.partial(
                expert_back_kernel, block=block, sizes=sizes, fresh=fresh,
                sources=len(routed[at])
            ),
            scal,
            (per_core,),
            [whole(d_branch), whole(sib_d), whole(tables[0]), whole(tables[1])]
            + [whole(a) if fresh else lead(a) for a in hidden]
            + expert_ins(at),
            [whole(row_f32), whole(row_bf16)]
            + [part_of(sum(sizes[:n]), size) for n, size in enumerate(sizes) for _ in range(2)]
            + [whole(row_f32), whole(row_bf16)] * fresh,
            scratch=slot_scratch * (3 if fresh else 1),
            flops=8 * expert_flops,
            exps=per_core * capacity * hid,
            limit=44,
        )
        for chunk in range(len(sizes)):
            near, far = grads[2 * chunk : 2 * chunk + 2]
            open_flow((at, chunk), expert_flow(outs, near, far, at, sum(sizes[:chunk])))
        if fresh:
            open_flow("result", result_flow(mixed, *grads[-2:], branch))
        if at == 0:
            open_flow((0, "shared"), pack_flow(functools.partial(packed.put, 0, None, True), g_shared))
        own, sib = slot((at, "experts"), own, sib)
        part = join(own, sib, d_ffn)
        part = slot((at, "join"), *part)
        arrivals = tp_sum(part, functools.partial(slot, (at, "ffn half")))
        arrivals = slot((at, "ffn sum"), *arrivals)
        d_mixed, d_attn, gain = call(
            functools.partial(mix_back_kernel, parts=len(arrivals)),
            scal,
            (2,),
            [tiled(mixed), tiled(d_next)] + [whole(a) for a in arrivals] + weights,
            [tiled(row_f32), tiled(row_bf16), whole(sds((8, width), F32))],
        )
        gain_grads[layers + at] = gain[:1]
        kv_shape = sds((rows, 2 * heads_width), BF16)
        kv_outs = [kv_shape] * 2 if ctx == 2 else [sds((tree_len, 2 * heads_width), BF16)]
        dq, g_out, *dkv = call(
            functools.partial(attend_back_kernel, parts=len(kv)),
            scal,
            (2,),
            [whole(path), tiled(query), tiled(d_attn), tiled(heads)]
            + [whole(k) for k in kv]
            + weights,
            [tiled(sds((rows, heads_width), BF16)), whole(sds((width, heads_width), BF16))]
            + [whole(k) for k in kv_outs],
            scratch=[
                pltpu.VMEM((tree_len, 2 * heads_width), F32),
                pltpu.VMEM((width, heads_width), F32),
            ],
            flops=10 * rows * tree_len * heads_width + 2 * matrix * heads_width,
            exps=rows * tree_len * heads_width // HEAD_DIM,
            limit=34,
        )
        dq, *dkv = slot((at, "attention"), dq, *dkv)
        if ctx == 2:
            kv_own, kv_got = dkv[0], swap(dkv[1], "ctx", 1)
        else:
            parts = dkv[0].reshape((ctx, rows) + dkv[0].shape[1:])
            parts = lax.all_to_all(parts, "ctx", 0, 0, tiled=True)
            kv_own, kv_got = jnp.sum(parts.astype(F32), axis=0), jnp.zeros(kv_shape.shape, F32)
        *part, g0, g1, g2, g3 = call(
            functools.partial(project_back_kernel, chunks=CHUNKS),
            scal,
            (1,),
            [whole(a) for a in (dq, kv_own, kv_got, normed, g_out)] + weights,
            halves + [whole(sds((block, PACK), BF16))] * 4,
            flops=2 * matrix * 576,
        )
        g_attention = [g0, g1, g2, g3]
        if at == 0:
            open_flow((0, "attention"), pack_flow(functools.partial(packed.put, 0, 0, False), g_attention))
        else:
            both = [jnp.concatenate(g, axis=1) for g in zip(g_shared, g_attention)]
            open_flow((at, "packs"), pack_flow(functools.partial(packed.put, at, 3 * hid, True), both))
        part = slot((at, "project"), *part)
        arrivals = tp_sum(part, functools.partial(slot, (at, "attention half")))
        arrivals = slot((at, "attention sum"), *arrivals)
        final = at == 0
        *rest, gain = call(
            functools.partial(
                input_back_kernel, parts=len(arrivals), block=block, final=final
            ),
            scal,
            (2,),
            [tiled(stream), tiled(d_mixed)] + [whole(a) for a in arrivals] + weights,
            [tiled(row_f32)] + ([] if final else [tiled(row_bf16)]) + [whole(sds((8, width), F32))],
        )
        gain_grads[at] = gain[:1]
        d_next, *rest = slot((at, "input"), *rest)
        if not final:
            (d_branch,) = rest
    gains = jnp.concatenate(gain_grads, axis=0).astype(BF16)
    cuts = [gains[:, r * block : (r + 1) * block] for r in range(4)]
    open_flow("gains", pack_flow(lambda *v: gain_sums.extend(v), cuts))
    finish("gains")
    for step in TAIL:
        finish(*step)
    gains = gain_sums[0].astype(F32) + gain_sums[1].astype(F32)
    g_sin, g_sout, g_qkv, g_attention_out = packed.held
    g_in, g_out = outs.held
    blocks = hid // 128
    g_in = g_in.reshape(layers * experts * block, blocks, 2, 128).transpose(0, 2, 1, 3)
    g_sin = g_sin.reshape(layers * block, blocks, 2, 128).transpose(0, 2, 1, 3)
    return (
        result[0][None],
        d_next[None],
        gains[:layers],
        gains[layers:],
        g_qkv.transpose(0, 2, 1, 3),
        g_attention_out,
        g_sin.reshape(layers, block, 2, hid),
        g_sout.transpose(0, 2, 1),
        g_in.reshape(layers, experts, block, 2, hid),
        g_out.transpose(0, 1, 3, 2),
    )


def solution(mesh):
    return jax.shard_map(
        shards,
        mesh=mesh,
        in_specs=(
            P("fsdp", "ctx", None),
            P("fsdp", None),
            P("fsdp", "ctx", None),
            P("fsdp", "ctx", None),
            P(None, "fsdp"),
            P(None, "fsdp"),
            P(None, "fsdp", None, "tp"),
            P(None, "tp", "fsdp"),
            P(None, "fsdp", None, "tp"),
            P(None, "tp", "fsdp"),
            P(None, None, "fsdp", None, "tp"),
            P(None, None, "tp", "fsdp"),
            P("fsdp", "ctx", None),
        ),
        out_specs=(
            P("fsdp", "ctx", None),
            P("fsdp", "ctx", None),
            P(None, "fsdp"),
            P(None, "fsdp"),
            P(None, "fsdp", None, "tp"),
            P(None, "tp", "fsdp"),
            P(None, "fsdp", None, "tp"),
            P(None, "tp", "fsdp"),
            P(None, None, "fsdp", None, "tp"),
            P(None, None, "tp", "fsdp"),
        ),
        check_vma=False,
    )
```

```python
import functools

import jax
import jax.numpy as jnp
from jax import lax
from jax.experimental import pallas as pl
from jax.experimental.pallas import tpu as pltpu
from jax.sharding import PartitionSpec as P

HEAD_DIM = 64
EPS = 1e-06
SCALE = 0.125
MASKED = -1000000000.0
F32 = jnp.float32
BF16 = jnp.bfloat16
MIB = 1 << 20
LIGHT = 1000
KEYS, QUERY, OUT, GAINS, PACK = 0, 384, 640, 832, 896

NN = (((1,), (0,)), ((), ()))
NT = (((1,), (1,)), ((), ()))
TN = (((0,), (0,)), ((), ()))


def mm(a, b, dims=NN):
    return lax.dot_general(a, b, dims, preferred_element_type=F32)


def sds(shape, dtype):
    return jax.ShapeDtypeStruct(tuple(shape), dtype)


def swap(values, axis, mask):
    count = lax.axis_size(axis)
    return lax.ppermute(values, axis, [(k, k ^ mask) for k in range(count)])


def after(value, dep):
    return lax.optimization_barrier((value, dep))[0]


def add(a, b):
    return (a.astype(F32) + b.astype(F32)).astype(BF16)


def gather_blocks(values):
    far = swap(values, "fsdp", 2)
    return [values, swap(values, "fsdp", 1), far, swap(far, "fsdp", 1)]


def tp_sum(halves, between):
    count = lax.axis_size("tp")
    chunks = len(halves) // 2
    totals = [add(k, swap(g, "tp", 1)) for k, g in zip(halves[:chunks], halves[chunks:])]
    totals[0] = between(totals[0])[0]
    step = 2
    while step < count:
        totals = [add(total, swap(total, "tp", step)) for total in totals]
        step *= 2
    return list(totals) + [swap(total, "tp", 1) for total in totals]


def ctx_last(part):
    count = lax.axis_size("ctx")
    step = 1
    while step * 2 < count:
        part = add(part, swap(part, "ctx", step))
        step *= 2
    return part, swap(part, "ctx", step)


def call(
    kernel, scal, grid, ins, outs, scratch=(), flops=0, exps=0, alias=None, limit=20, light=LIGHT
):
    def spec(item):
        shape, block, index = item[0].shape, item[1], item[2]
        if block == "any":
            return pl.BlockSpec(memory_space=pl.ANY)
        if block is None:
            return pl.BlockSpec(shape, lambda *_: (0,) * len(shape))
        return pl.BlockSpec(block, index)

    size = lambda a: a.size * a.dtype.itemsize
    moved = sum(size(i[0]) for i in list(ins) + list(outs) if i[1] != "any" and len(i) < 4)
    moved += sum(i[3] for i in list(ins) + list(outs) if len(i) > 3)
    return pl.pallas_call(
        kernel,
        out_shape=[o[0] for o in outs],
        grid_spec=pltpu.PrefetchScalarGridSpec(
            num_scalar_prefetch=1,
            grid=grid,
            in_specs=[spec(i) for i in ins],
            out_specs=[spec(o) for o in outs],
            scratch_shapes=list(scratch),
        ),
        compiler_params=pltpu.CompilerParams(
            dimension_semantics=("arbitrary",) * len(grid), vmem_limit_bytes=limit * MIB
        ),
        cost_estimate=pl.CostEstimate(flops=flops // light, transcendentals=0, bytes_accessed=moved // light),
        input_output_aliases=alias or {},
    )(scal, *[i[0] for i in ins])


def whole(a):
    return (a, None, None)


def tiled(a):
    return (a, (a.shape[0] // 2,) + a.shape[1:], lambda t, *_: (t,) + (0,) * (len(a.shape) - 1))


def joined(refs, *at):
    return jnp.concatenate([ref[at] if at else ref[...] for ref in refs], axis=0)


def gain_row(pack_refs, which):
    cols = jnp.concatenate([ref[:, GAINS - 64 : PACK] for ref in pack_refs], axis=0)
    at = lax.broadcasted_iota(jnp.int32, (8, 128), 1)
    pick = jnp.where(at == 64 + which, 1.0, 0.0).astype(BF16)
    return mm(pick, cols, NT)[:1]


def swap_pairs(values, block):
    two = 2 * block
    return jnp.concatenate(
        [pltpu.roll(values[:, at : at + two], block, 1) for at in (0, two)], axis=1
    )


def relative(values, me, block):
    two = 2 * block
    far = jnp.concatenate([values[:, two:], values[:, :two]], axis=1)
    values = jnp.where((me & 2) > 0, far, values)
    return jnp.where((me & 1) > 0, swap_pairs(values, block), values)


def arrived(bit, refs):
    chunks = len(refs) // 2
    mine, other = joined(refs[:chunks]), joined(refs[chunks:])
    return jnp.where(pl.program_id(0) == bit, mine, other).astype(F32)


def put_halves(tile, bit, values, refs):
    chunks = len(refs) // 2
    rows = values.shape[0] // chunks
    values = values.astype(BF16)

    @pl.when(tile == bit)
    def _():
        for at in range(chunks):
            refs[at][...] = values[at * rows : (at + 1) * rows]

    @pl.when(tile != bit)
    def _():
        for at in range(chunks):
            refs[chunks + at][...] = values[at * rows : (at + 1) * rows]


def half_shapes(rows, width, chunks):
    return [whole(sds((rows // 2 // chunks, width), BF16)) for _ in range(2 * chunks)]


def normed_of(values, gain):
    inverse = lax.rsqrt(jnp.mean(values * values, axis=-1, keepdims=True) + EPS)
    scaled = values * inverse
    return scaled, inverse, scaled * gain


def norm_back(d_normed, values, gain):
    scaled, inverse, _ = normed_of(values, gain)
    d_scaled = d_normed * gain
    mean = jnp.mean(d_scaled * scaled, axis=-1, keepdims=True)
    return inverse * (d_scaled - scaled * mean), jnp.sum(d_normed * scaled, axis=0, keepdims=True)


def order_kernel(scal, tok_ref, cot_ref, tok_out, cot_out, *, block):
    for src, dst in ((tok_ref, tok_out), (cot_ref, cot_out)):
        dst[...] = relative(src[...].astype(F32), scal[0], block).astype(BF16)


def project(stream, packs, normed_ref, q_ref, kv_ref):
    _, _, normed = normed_of(stream, gain_row(packs, 0))
    normed = normed.astype(BF16)
    normed_ref[...] = normed
    weight = joined(packs)
    kv_ref[...] = mm(normed, weight[:, KEYS:QUERY]).astype(BF16)
    q_ref[...] = mm(normed, weight[:, QUERY : QUERY + q_ref.shape[1]]).astype(BF16)


def first_kernel(scal, tok_ref, *refs):
    project(tok_ref[...].astype(F32), refs[:4], *refs[4:])


def next_kernel(scal, mixed_ref, *refs, parts):
    stream = mixed_ref[...] + arrived(scal[1], refs[:parts])
    packs, (stream_ref, *outs) = refs[parts : parts + 4], refs[parts + 4 :]
    stream_ref[...] = stream
    project(stream, packs, *outs)


def last_kernel(scal, mixed_ref, *refs, block):
    result = mixed_ref[...] + arrived(scal[1], refs[:-1])
    refs[-1][...] = relative(result, scal[0], block).astype(BF16)


def allowed_of(scal, path_ref, rows, tree_len):
    first = scal[3] + pl.program_id(0) * rows
    query_pos = first + lax.broadcasted_iota(jnp.int32, (rows, tree_len), 0)
    key_pos = lax.broadcasted_iota(jnp.int32, (rows, tree_len), 1)
    return (key_pos <= query_pos) & (path_ref[...] > 0.5)


def softmax_of(query, key, allowed):
    scores = jnp.where(allowed, mm(query, key, NT) * SCALE, MASKED)
    expo = jnp.exp(scores - jnp.max(scores, axis=-1, keepdims=True))
    return expo * (1.0 / jnp.sum(expo, axis=-1, keepdims=True))


def head_cols(width):
    return [slice(at, at + HEAD_DIM) for at in range(0, width, HEAD_DIM)]


def all_keys(scal, refs):
    if len(refs) == 1:
        return refs[0][...]
    own, got = refs[0][...], refs[1][...]
    first = scal[4] == 0
    return jnp.concatenate([jnp.where(first, own, got), jnp.where(first, got, own)], axis=0)


def attend_kernel(scal, path_ref, q_ref, *refs, parts):
    kv_ref, refs = all_keys(scal, refs[:parts]), refs[parts:]
    packs, heads_ref, halves = refs[:4], refs[4], refs[5:]
    rows, width = q_ref.shape
    allowed = allowed_of(scal, path_ref, rows, kv_ref.shape[0])
    outs = []
    for cols in head_cols(width):
        vals = slice(width + cols.start, width + cols.stop)
        probs = softmax_of(q_ref[:, cols], kv_ref[:, cols], allowed).astype(BF16)
        outs.append(mm(probs, kv_ref[:, vals]))
    heads = jnp.concatenate(outs, axis=1).astype(BF16)
    heads_ref[...] = heads
    weight = jnp.concatenate([ref[:, OUT : OUT + width] for ref in packs], axis=0)
    put_halves(pl.program_id(0), scal[1], mm(heads, weight, NT), halves)


def attend_back_kernel(scal, path_ref, q_ref, d_ref, heads_ref, *refs, parts):
    kv_ref, refs = all_keys(scal, refs[:parts]), refs[parts:]
    packs, (dq_ref, gout_ref), (dkv_refs, scratch) = refs[:4], refs[4:6], (refs[6:-2], refs[-2:])
    dkv_acc, gout_acc = scratch
    rows, width = q_ref.shape
    tile = pl.program_id(0)
    allowed = allowed_of(scal, path_ref, rows, kv_ref.shape[0])

    @pl.when(tile == 0)
    def _():
        dkv_acc[...] = jnp.zeros_like(dkv_acc)
        gout_acc[...] = jnp.zeros_like(gout_acc)

    weight = jnp.concatenate([ref[:, OUT : OUT + width] for ref in packs], axis=0)
    d_heads = mm(d_ref[...], weight).astype(BF16)
    gout_acc[...] += mm(d_ref[...], heads_ref[...], TN)
    dqs, dks, dvs = [], [], []
    for cols in head_cols(width):
        vals = slice(width + cols.start, width + cols.stop)
        query, key, value, d_out = q_ref[:, cols], kv_ref[:, cols], kv_ref[:, vals], d_heads[:, cols]
        probs = softmax_of(query, key, allowed)
        d_prob = mm(d_out, value, NT)
        weighted = jnp.sum(probs * d_prob, axis=-1, keepdims=True)
        d_scores = (probs * (d_prob - weighted)).astype(BF16)
        dqs.append(mm(d_scores, key) * SCALE)
        dks.append(mm(d_scores, query, TN) * SCALE)
        dvs.append(mm(probs.astype(BF16), d_out, TN))
    dq_ref[...] = jnp.concatenate(dqs, axis=1).astype(BF16)
    dkv_acc[...] += jnp.concatenate(dks + dvs, axis=1)

    @pl.when(tile == pl.num_programs(0) - 1)
    def _():
        gout_ref[...] = gout_acc[...].astype(BF16)
        if len(dkv_refs) == 1:
            dkv_refs[0][...] = dkv_acc[...].astype(BF16)
        else:
            half = dkv_refs[0].shape[0]
            for at in range(2):
                part = dkv_acc[at * half : (at + 1) * half, :].astype(BF16)
                mine = scal[3] == at * half

                @pl.when(mine)
                def _():
                    dkv_refs[0][...] = part

                @pl.when(jnp.logical_not(mine))
                def _():
                    dkv_refs[1][...] = part


def project_back_kernel(scal, dq_ref, own_ref, got_ref, normed_ref, gout_ref, *refs, chunks):
    packs, halves, grads = refs[:4], refs[4 : 4 + 2 * chunks], refs[4 + 2 * chunks :]
    d_kv = (own_ref[...].astype(F32) + got_ref[...].astype(F32)).astype(BF16)
    d_q, normed = dq_ref[...], normed_ref[...]
    width = d_q.shape[1]
    weight = joined(packs)
    part = mm(d_kv, weight[:, KEYS:QUERY], NT) + mm(d_q, weight[:, QUERY : QUERY + width], NT)
    half = part.shape[0] // 2
    for at in range(2):
        put_halves(at, scal[1], part[at * half : (at + 1) * half], halves)
    g_kv, g_q, g_out = mm(normed, d_kv, TN), mm(normed, d_q, TN), gout_ref[...]
    rows = grads[0].shape[0]
    for at, ref in enumerate(grads):
        cut = slice(at * rows, (at + 1) * rows)
        ref[...] = jnp.zeros_like(ref)
        ref[:, KEYS:QUERY] = g_kv[cut].astype(BF16)
        ref[:, QUERY : QUERY + width] = g_q[cut].astype(BF16)
        ref[:, OUT : OUT + width] = g_out[cut]


def mix_kernel(scal, stream_ref, *refs, parts):
    mixed = stream_ref[...].astype(F32) + arrived(scal[1], refs[:parts])
    packs, (mixed_ref, in_ref) = refs[parts : parts + 4], refs[parts + 4 :]
    mixed_ref[...] = mixed
    in_ref[...] = normed_of(mixed, gain_row(packs, 1))[2].astype(BF16)


def shared_kernel(scal, in_ref, *refs):
    packs, (branch_ref, gate_ref, up_ref) = refs[:12], refs[12:]
    gate = mm(in_ref[...], joined(packs[:4]))
    up = mm(in_ref[...], joined(packs[4:8]))
    gate_ref[...] = gate
    up_ref[...] = up
    hidden = (gate / (1.0 + jnp.exp(-gate)) * up).astype(BF16)
    branch_ref[...] = mm(hidden, joined(packs[8:]), NT)


def glu_back(gate, up, d_hidden):
    sigmoid = 1.0 / (1.0 + jnp.exp(-gate))
    active = gate * sigmoid
    hidden = (active * up).astype(BF16)
    d_gate = (d_hidden * up * (sigmoid * (1.0 + gate * (1.0 - sigmoid)))).astype(BF16)
    return hidden, d_gate, (d_hidden * active).astype(BF16)


def shared_back_kernel(scal, d_ref, in_ref, gate_ref, up_ref, *refs):
    packs, (out_ref, *grad_refs) = refs[:12], refs[12:]
    hid = gate_ref.shape[1]
    cut = lambda at: joined(packs[4 * at : 4 * at + 4])
    d_branch, ffn_in = d_ref[...], in_ref[...]
    hidden, d_gate, d_up = glu_back(gate_ref[...], up_ref[...], mm(d_branch, cut(2)))
    out_ref[...] = mm(d_gate, cut(0), NT) + mm(d_up, cut(1), NT)
    grads = (mm(ffn_in, d_gate, TN), mm(ffn_in, d_up, TN), mm(d_branch, hidden, TN))
    rows = grad_refs[0].shape[0]
    for at, grad in enumerate(grads):
        for r, ref in enumerate(grad_refs):
            ref[:, at * hid : (at + 1) * hid] = grad[r * rows : (r + 1) * rows].astype(BF16)


def column(table_ref, rows, at):
    values = table_ref[rows, :]
    lane = lax.broadcasted_iota(jnp.int32, values.shape, 1)
    return jnp.sum(jnp.where(lane == at, values, 0.0), axis=1, keepdims=True)


def spread(first, second, places, weights):
    one, two = weights
    return jnp.where(places == first, one, jnp.where(places == second, two, 0.0)).astype(BF16)


def rows_of(lists_ref, half, tokens, slots, weighted):
    cut = slice(half * tokens, (half + 1) * tokens)
    first, second, one, two = [lists_ref[at : at + 1, cut] for at in range(4)]
    places = lax.broadcasted_iota(jnp.int32, (slots, tokens), 0)
    weights = (one, two) if weighted else (1.0, 1.0)
    return spread(first.astype(jnp.int32), second.astype(jnp.int32), places, weights)


def cols_of(table_ref, half, tokens, slots, weighted):
    cut = slice(half * tokens, (half + 1) * tokens)
    first, second = [column(table_ref, cut, at).astype(jnp.int32) for at in range(2)]
    weights = [column(table_ref, cut, at) for at in (2, 3)] if weighted else (1.0, 1.0)
    places = lax.broadcasted_iota(jnp.int32, (tokens, slots), 1)
    return spread(first, second, places, weights)


def to_slots(own_ref, sib_ref, lists_ref, slot_ref, block, weighted):
    @pl.when(pl.program_id(0) == 0)
    def _():
        tokens, slots = own_ref.shape[0], slot_ref.shape[1]
        sib = swap_pairs(sib_ref[...].astype(F32), block).astype(BF16)
        for half, values in enumerate((own_ref[...], sib)):
            picks = rows_of(lists_ref, half, tokens, slots, weighted)
            slot_ref[half] = mm(picks, values).astype(BF16)


def from_slots(slot_ref, table_ref, own_out, sib_out, weighted):
    @pl.when(pl.program_id(0) == pl.num_programs(0) - 1)
    def _():
        tokens, slots = own_out.shape[0], slot_ref.shape[1]
        for half, ref in enumerate((own_out, sib_out)):
            picks = cols_of(table_ref, half, tokens, slots, weighted)
            ref[...] = mm(picks, slot_ref[half]).astype(ref.dtype)


def of_expert(slot_ref):
    count = slot_ref.shape[1] // pl.num_programs(0)
    rows = pl.ds(pl.multiple_of(pl.program_id(0) * count, count), count)
    return jnp.concatenate([slot_ref[0, rows, :], slot_ref[1, rows, :]], axis=0)


def put_expert(slot_ref, values):
    count = slot_ref.shape[1] // pl.num_programs(0)
    rows = pl.ds(pl.multiple_of(pl.program_id(0) * count, count), count)
    slot_ref[0, rows, :] = values[:count]
    slot_ref[1, rows, :] = values[count:]


def pack_kernel(scal, in_ref, out_ref, own_ref, first_ref, last_ref):
    third = first_ref.shape[2]
    own_ref[0, :2] = pltpu.einshape("dkf->kdf", in_ref[0, 0])
    own_ref[0, 2] = out_ref[0, 0]
    first_ref[0] = own_ref[0, :, pl.ds(pl.multiple_of(scal[4] * third, third), third), :]
    last_ref[0] = own_ref[0, :, 2 * third :, :]


def expert_weights(scal, refs):
    def far(refs, part):
        straight, around, last = [ref[0, part] for ref in refs]
        low = jnp.where(scal[4] == 0, straight, around)
        middle = jnp.where(scal[4] == 0, around, straight)
        return [low, middle, last]

    return [
        jnp.concatenate(
            [refs[0][0, part], refs[1][0, part]] + far(refs[2:5], part) + far(refs[5:8], part), axis=0
        )
        for part in range(3)
    ]


def expert_kernel(scal, own_ref, sib_ref, lists_ref, table_ref, *refs, block, sources):
    weights, (own_out, sib_out, x_ref, gate_ref, up_ref, x_all, y_all) = refs[:sources], refs[sources:]
    to_slots(own_ref, sib_ref, lists_ref, x_all, block, False)
    w_gate, w_up, w_out = expert_weights(scal, weights)
    chosen = of_expert(x_all)
    gate = mm(chosen, w_gate)
    up = mm(chosen, w_up)
    x_ref[0], gate_ref[0], up_ref[0] = chosen, gate.astype(BF16), up.astype(BF16)
    hidden = (gate / (1.0 + jnp.exp(-gate)) * up).astype(BF16)
    put_expert(y_all, mm(hidden, w_out, NT).astype(BF16))
    from_slots(y_all, table_ref, own_out, sib_out, True)


def expert_back_kernel(
    scal, own_ref, sib_ref, lists_ref, table_ref, a_ref, b_ref, *refs, block, sizes, sources, fresh
):
    given, refs = ((), refs) if fresh else (refs[:1], refs[1:])
    weights, refs = refs[:sources], refs[sources:]
    (own_out, sib_out), grads, refs = refs[:2], refs[2 : 2 + 2 * len(sizes)], refs[2 + 2 * len(sizes) :]
    to_slots(own_ref, sib_ref, lists_ref, refs[-1], block, True)
    w_gate, w_up, w_out = expert_weights(scal, weights)
    d_rows = of_expert(refs[-1])
    if fresh:
        own_next, sib_next, x_all, y_all = refs[:4]
        to_slots(a_ref, b_ref, lists_ref, x_all, block, False)
        chosen = of_expert(x_all)
        gate, up = mm(chosen, w_gate), mm(chosen, w_up)
    else:
        chosen, gate, up = a_ref[0], b_ref[0].astype(F32), given[0][0].astype(F32)
    hidden, d_gate, d_up = glu_back(gate, up, mm(d_rows, w_out))
    if fresh:
        put_expert(y_all, mm(hidden, w_out, NT).astype(BF16))
        from_slots(y_all, table_ref, own_next, sib_next, True)
    step = pl.program_id(0)
    parts = (mm(chosen, d_gate, TN), mm(chosen, d_up, TN), mm(d_rows, hidden, TN))
    parts = [p.astype(BF16) for p in parts]
    for chunk, size in enumerate(sizes):
        first = sum(sizes[:chunk])

        @pl.when((step >= first) & (step < first + size))
        def _():
            for at in range(3):
                grads[2 * chunk][0, at] = parts[at][: 2 * block]
                grads[2 * chunk + 1][0, at] = parts[at][2 * block :]

    d_x = mm(d_gate, w_gate, NT) + mm(d_up, w_up, NT)
    put_expert(refs[-1], d_x.astype(BF16))
    from_slots(refs[-1], table_ref, own_out, sib_out, False)


def join_kernel(scal, own_ref, got_ref, shared_ref, *halves, block):
    part = own_ref[...] + shared_ref[...] + swap_pairs(got_ref[...].astype(F32), block)
    put_halves(pl.program_id(0), scal[1], part, halves)


def mix_back_kernel(scal, mixed_ref, next_ref, *refs, parts):
    packs, (d_ref, attn_ref, gain_ref) = refs[parts : parts + 4], refs[parts + 4 :]
    back, gain_grad = norm_back(arrived(scal[1], refs[:parts]), mixed_ref[...], gain_row(packs, 1))
    d_mixed = back + next_ref[...].astype(F32)
    d_ref[...] = d_mixed
    attn_ref[...] = d_mixed.astype(BF16)
    sum_tiles(gain_ref, gain_grad)


def sum_tiles(ref, value):
    value = jnp.broadcast_to(value, ref.shape)

    @pl.when(pl.program_id(0) == 0)
    def _():
        ref[...] = value

    @pl.when(pl.program_id(0) > 0)
    def _():
        ref[...] += value


def input_back_kernel(scal, stream_ref, mixed_ref, *refs, parts, block, final):
    packs, outs = refs[parts : parts + 4], refs[parts + 4 :]
    stream = stream_ref[...].astype(F32)
    back, gain_grad = norm_back(arrived(scal[1], refs[:parts]), stream, gain_row(packs, 0))
    d_stream = back + mixed_ref[...]
    if final:
        outs[0][...] = relative(d_stream, scal[0], block)
    else:
        outs[0][...] = d_stream
        outs[1][...] = d_stream.astype(BF16)
    sum_tiles(outs[-1], gain_grad)


def store_expert(in_ref, out_ref, gate, up, out):
    blocks = gate.shape[1] // 128
    for at, part in enumerate((gate, up)):
        for col in range(blocks):
            rows = pl.ds(col * 2 + at, part.shape[0], stride=2 * blocks)
            in_ref[0, 0, rows, :] = part[:, col * 128 : (col + 1) * 128]
    out_ref[0, 0] = out


def own_kernel(scal, part_ref, got_ref, *refs):
    give_ref, in_ref, out_ref = refs[-3:]
    half = give_ref.shape[2]
    total = [part_ref[0, at].astype(F32) + got_ref[0, at].astype(F32) for at in range(3)]
    for at in range(3):
        give_ref[0, at] = total[at][half:].astype(BF16)
    store_expert(in_ref, out_ref, *[t[:half] for t in total])


def other_kernel(scal, got_ref, *refs):
    store_expert(*refs[-2:], *[got_ref[0, at].astype(F32) for at in range(3)])


def packed_kernel(scal, part_ref, got_ref, *refs, first, shared, blocks):
    total = part_ref[...].astype(F32) + got_ref[...].astype(F32)
    if first is not None:
        refs, (qkv_ref, out_ref) = refs[:-2], refs[-2:]
        width = qkv_ref.shape[3]
        for at, col in enumerate((QUERY, KEYS, KEYS + width)):
            qkv_ref[0, at] = total[:, first + col : first + col + width]
        out_ref[0] = total[:, first + OUT : first + OUT + width].T
    if shared:
        sin_ref, sout_ref = refs[-2:]
        hid = sout_ref.shape[2]
        for at in range(2):
            for col in range(blocks):
                rows = pl.ds(col * 2 + at, total.shape[0], stride=2 * blocks)
                lanes = at * hid + col * 128
                sin_ref[0, rows, :] = total[:, lanes : lanes + 128]
        sout_ref[0] = total[:, 2 * hid : 3 * hid]

CHUNKS, PARTS = 2, ((1, 1, 2), (1, 1, 2))
SLOTS = {
    "start": ["pack 0", ("experts", 0)],
    ("attend", 0): ["slots"],
    ("attend half", 0): [("experts", 0), "pack 1"],
    ("attend sum", 0): ["pack 2", ("experts", 1)],
    ("mixed", 0): [("experts", 0), "pack 1"],
    ("experts", 0): ["pack 1", "pack 2", ("experts", 1)],
    ("branch sum", 0): ["pack 2", ("experts", 1)],
    ("attend", 1): [("experts", 1)],
    ("mixed", 1): [("experts", 1)],
    (1, "experts"): [(1, 0)],
    (1, "ffn half"): [(1, 1)],
    (1, "ffn sum"): [(1, 0), (1, 2)],
    (1, "attention"): [(1, 1)],
    (1, "project"): [(1, "packs")],
    (1, "attention half"): [(1, 0), (1, 2)],
    (1, "attention sum"): [(1, "packs")],
    (1, "input"): [(1, 0), (1, 1)],
    (0, "experts"): [(1, 2), (1, "packs"), (0, 0)],
    (0, "ffn half"): [(1, 1), "result", (0, 0), (0, 1)],
    (0, "ffn sum"): [(1, 2), (1, "packs"), "result", (0, 0), (0, 2), (0, "shared")],
    (0, "project"): [(0, 0), (0, 1), (0, "attention"), "result"],
    (0, "attention half"): [(0, 2), (0, "shared")],
    (0, "attention sum"): [(0, 1)],
    (0, "input"): [(0, 1), (0, 2), (0, "shared"), (0, "attention")],
}
TAIL = (
    ["gains", (0, 2), (0, "shared"), (0, "attention")],
    ["gains", (0, "attention")],
    ["gains"],
)


class Packs:
    def __init__(self, scal, layers, block, hid, width):
        self.scal, self.blocks = scal, hid // 128
        self.shapes = (
            sds((layers, block * 2 * self.blocks, 128), F32),
            sds((layers, block, hid), F32),
            sds((layers, 3, block, width), F32),
            sds((layers, width, block), F32),
        )
        self.held = [None] * 4

    def put(self, layer, first, shared, part, got):
        used = [0, 1] * shared + [2, 3] * (first is not None)
        before = [at for at in used if self.held[at] is not None]
        slot = lambda s: (s, (1,) + s.shape[1:], lambda *_: (layer,) + (0,) * (len(s.shape) - 1))
        results = call(
            functools.partial(packed_kernel, first=first, shared=shared, blocks=self.blocks),
            self.scal,
            (1,),
            [whole(part), whole(got)] + [(self.held[at], "any", None) for at in before],
            [slot(self.shapes[at]) for at in used],
            alias={3 + n: used.index(at) for n, at in enumerate(before)},
            limit=10,
        )
        for at, result in zip(used, results):
            self.held[at] = result


class Outs:
    def __init__(self, scal, layers, experts, block, hid):
        self.scal, self.per_core = scal, experts // 2
        self.shapes = (
            sds((layers, experts, block * 2 * hid // 128, 128), F32),
            sds((layers, experts, block, hid), F32),
        )
        self.held = None

    def put(self, kernel, ins, extra, layer, first, other):
        count = ins[0].shape[0]
        lead = lambda a: (a, (1,) + a.shape[1:], lambda e, s: (e, 0, 0, 0))
        place = lambda e, s: (layer, (s[2] ^ other) * self.per_core + first + e, 0, 0)
        moved = lambda s: count * s.size * 4 // (s.shape[0] * s.shape[1])
        slot = lambda s: (s, (1, 1) + s.shape[2:], place, moved(s))
        held = [] if self.held is None else [(h, "any", None) for h in self.held]
        base = 1 + len(ins)
        *rest, gin, gout = call(
            kernel,
            self.scal,
            (count,),
            [lead(i) for i in ins] + held,
            [lead(x) for x in extra] + [slot(s) for s in self.shapes],
            alias={base + at: len(extra) + at for at in range(len(held))},
            limit=10,
        )
        self.held = (gin, gout)
        return rest


def expert_flow(outs, near, far, layer, first):
    near, far = yield [near, far]
    near, got = yield [near, swap(far, "fsdp", 2)]
    part, got = yield list(ctx_last(add(near, got)))
    block = near.shape[2] // 2
    give = sds(near.shape[:2] + (block,) + near.shape[3:], BF16)
    (give,) = outs.put(own_kernel, (part, got), (give,), layer, first, 0)
    (got,) = yield [swap(give, "fsdp", 1)]
    outs.put(other_kernel, (got,), (), layer, first, 1)
    yield []


def pack_flow(done, parts):
    parts = yield list(parts)
    own, far, got, far_got = yield [parts[0], parts[2], swap(parts[1], "fsdp", 1), swap(parts[3], "fsdp", 1)]
    own, far = add(own, got), add(far, far_got)
    own, got = yield [own, swap(far, "fsdp", 2)]
    part, got = yield list(ctx_last(add(own, got)))
    done(part, got)
    yield []


def weight_flow(place, at, own, first, last):
    own, first, last = yield [own, first, last]
    if at > 0:
        own, first, last = yield [own, first, last]
    own, sib, straight, last = yield [own, swap(own, "fsdp", 1), swap(first, "fsdp", 2), last]
    last = swap(last, "fsdp", 2)
    if at > 0:
        (straight,) = yield [straight]
    around, cross = swap(straight, "ctx", 1), swap(straight, "fsdp", 1)
    straight, around, last, cross = yield [straight, around, last, cross]
    place[at] = [own, sib, straight, around, last]
    place[at] += [cross, swap(around, "fsdp", 1), swap(last, "fsdp", 1)]
    yield []


def block_flow(place, at, own):
    (own,) = yield [own]
    (own,) = yield [own]
    own, far = yield [own, swap(own, "fsdp", 2)]
    place[at] = [own, swap(own, "fsdp", 1), far, swap(far, "fsdp", 1)]
    yield []


def ancestry(parent_row):
    count = parent_row.shape[0]
    block_ids = jnp.arange(count, dtype=jnp.int32)
    step_map = ((parent_row[:, None] == block_ids[None, :]) & (block_ids[:, None] > 0)).astype(F32)
    reach = on_path = jnp.eye(count, dtype=F32)
    for _ in range(count):
        reach = jnp.dot(reach, step_map, precision=lax.Precision.HIGHEST)
        on_path = on_path + reach
    return on_path


def shards(
    tokens,
    parents,
    routes,
    gates,
    attn_gain,
    ffn_gain,
    qkv_weight,
    out_weight,
    shared_in,
    shared_out,
    expert_in,
    expert_out,
    cotangent,
):
    rows, width = tokens.shape[1], tokens.shape[2]
    layers, experts = expert_in.shape[0], expert_in.shape[1]
    block, heads_width = qkv_weight.shape[1], qkv_weight.shape[3]
    hid = expert_in.shape[4]
    ctx = lax.axis_size("ctx")
    tree_len = rows * ctx
    me, here = lax.axis_index("fsdp"), lax.axis_index("ctx")
    core, bit = me & 1, lax.axis_index("tp") & 1
    half_at = here & 1
    per_core = experts // 2
    capacity = 2 * (3 * rows // 8)
    scal = jnp.stack([me, bit, core, here * rows, half_at]).astype(jnp.int32)

    def pack_attention(at):
        cols = [qkv_weight[at][:, part] for part in (1, 2, 0)]
        pad = jnp.zeros((block, OUT - QUERY - heads_width), BF16)
        gains = jnp.stack([attn_gain[at], ffn_gain[at]], axis=1)
        tail = jnp.zeros((block, PACK - GAINS - 2), BF16)
        return jnp.concatenate(cols + [pad, out_weight[at].T, gains, tail], axis=1)

    def pack_shared(at):
        return [shared_in[at].reshape(block, 2 * hid), shared_out[at].T]

    eout = expert_out.transpose(0, 1, 3, 2)

    def pack_experts(at):
        third = block // 3
        whole_pack = sds((experts, 3, block, hid), BF16)
        part = sds((experts, 3, third, hid), BF16)
        lead = lambda a: (a, (1,) + a.shape[1:], lambda e, s: (e, 0, 0, 0))
        return call(
            pack_kernel,
            scal,
            (experts,),
            [
                (expert_in, (1, 1) + expert_in.shape[2:], lambda e, s: (at, e, 0, 0, 0)),
                (eout, (1, 1) + eout.shape[2:], lambda e, s: (at, e, 0, 0)),
            ],
            [lead(whole_pack), lead(part), lead(part)],
            limit=10,
        )

    ancestors = ancestry(parents[0])
    segment = tree_len // ancestors.shape[0]
    anc_row = lax.dynamic_slice_in_dim(ancestors, here * rows // segment, 1, 0)
    path = jnp.repeat(anc_row, segment, axis=1)

    places = 3 * rows // 8
    info = jnp.concatenate([routes[0].astype(F32), gates[0]], axis=1)
    info = jnp.concatenate([info, swap(info, "fsdp", 1)], axis=0)
    local = info[:, :2].astype(jnp.int32) - core * per_core
    hits = local[:, :, None] == jnp.arange(per_core, dtype=jnp.int32)
    at = jnp.arange(2 * rows)
    earlier = (at[:, None] > at[None, :]) & (at[:, None] // rows == at[None, :] // rows)
    before = mm(earlier.astype(BF16), jnp.any(hits, axis=1).astype(BF16))
    slot = before[:, None, :] + places * jnp.arange(per_core, dtype=F32)
    slot = jnp.sum(jnp.where(hits, slot + 1.0, 0.0), axis=2) - 1.0
    table = jnp.concatenate([slot, info[:, 2:]], axis=1)

    lead = lambda a: (
        a,
        (1,) + tuple(a.shape[1:]),
        lambda e, s: (e,) + (0,) * (len(a.shape) - 1),
    )

    matrix = 2 * rows * width
    expert_flops = 2 * per_core * capacity * width * hid
    slot_scratch = [pltpu.VMEM((2, per_core * places, width), BF16)]
    halves = half_shapes(rows, width, CHUNKS)
    row_f32, row_bf16 = sds((rows, width), F32), sds((rows, width), BF16)

    flows, held = {}, {}

    def open_flow(name, flow):
        flows[name] = flow
        held[name] = next(flow)

    def slot(name, *values):
        names = SLOTS.get(name, ())
        if not names:
            return list(values)
        values, arrays = lax.optimization_barrier((list(values), [held[n] for n in names]))
        for n, a in zip(names, arrays):
            if n == "slots":
                tables.extend(a)
            else:
                held[n] = flows[n].send(a)
        return values

    tables = []

    def finish(*names):
        for name in names:
            held[name] = flows[name].send(held[name])

    small, routed = {}, {}
    open_flow("pack 0", block_flow(small, 0, pack_attention(0)))
    for at in range(layers):
        open_flow(("experts", at), weight_flow(routed, at, *pack_experts(at)))
    open_flow("pack 1", block_flow(small, 1, jnp.concatenate(pack_shared(0), axis=1)))
    rest = [pack_attention(at) for at in range(1, layers)]
    rest = [v for pack in rest for v in (pack, jnp.zeros((block, 128), BF16))]
    rest += [v for at in range(1, layers) for v in pack_shared(at)]
    open_flow("pack 2", block_flow(small, 2, jnp.concatenate(rest, axis=1)))

    held["slots"] = [table.T, table]

    def attention_ins(at):
        if at == 0:
            return [whole(p) for p in small[0]]
        return [(p, (block, 1024), lambda *_: (0, at - 1)) for p in small[2]]

    def shared_ins(at):
        packs, first = (small[1], 0) if at == 0 else (small[2], 1024 * (layers - 1) // hid + 3 * at - 3)
        index = lambda which: lambda *_: (0, first + which)
        return [(p, (block, hid), index(which)) for which in range(3) for p in packs]

    def expert_ins(at):
        index = lambda e, s: (s[2] * per_core + e, 0, 0, 0)
        return [(a, (1,) + a.shape[1:], index) for a in routed[at]]

    stream, cot = call(
        functools.partial(order_kernel, block=block),
        scal,
        (2,),
        [tiled(tokens[0]), tiled(cotangent[0])],
        [tiled(row_bf16)] * 2,
    )
    finish("pack 0")
    finish("pack 0")
    slot("start")

    def experts_forward(at, own_in, sib_in):
        kept = [lead(sds((per_core, capacity, width), BF16))]
        kept += [lead(sds((per_core, capacity, hid), BF16))] * 2
        return call(
            functools.partial(
                expert_kernel, block=block, sources=len(routed[at])
            ),
            scal,
            (per_core,),
            [whole(own_in), whole(sib_in), whole(tables[0]), whole(tables[1])] + expert_ins(at),
            [whole(row_f32), whole(row_bf16)] + kept,
            scratch=slot_scratch * 2,
            flops=5 * expert_flops,
            limit=32,
        )

    def join(own, sib, shared_part):
        return call(
            functools.partial(join_kernel, block=block),
            scal,
            (2,),
            [tiled(own), tiled(swap(sib, "fsdp", 1)), tiled(shared_part)],
            halves,
        )

    def result_flow(mixed, own, sib, branch):
        own, sib = yield [own, sib]
        part = yield list(join(own, sib, branch))
        arrivals = yield tp_sum(part, lambda *values: values)
        (result[0],) = call(
            functools.partial(last_kernel, block=block),
            scal,
            (2,),
            [tiled(mixed)] + [whole(a) for a in arrivals],
            [tiled(row_bf16)],
        )
        yield []

    result = [None]
    saved = []
    mixed = arrivals = None
    for at in range(layers):
        outs = [
            tiled(row_bf16),
            tiled(sds((rows, heads_width), BF16)),
            tiled(sds((rows, 2 * heads_width), BF16)),
        ]
        weights = attention_ins(at)
        if at == 0:
            normed, query, kv = call(
                first_kernel, scal, (2,), [tiled(stream)] + weights, outs, flops=matrix * 576
            )
        else:
            stream, normed, query, kv = call(
                functools.partial(next_kernel, parts=len(arrivals)),
                scal,
                (2,),
                [tiled(mixed)] + [whole(a) for a in arrivals] + weights,
                [tiled(row_f32)] + outs,
                flops=matrix * 576,
            )
        (kv,) = slot(("project", at), kv)
        if ctx == 2:
            kv = [kv, swap(kv, "ctx", 1)]
        else:
            kv = [lax.all_gather(kv, "ctx", axis=0, tiled=True)]
        heads, *part = call(
            functools.partial(attend_kernel, parts=len(kv)),
            scal,
            (2,),
            [whole(path), tiled(query)] + [whole(k) for k in kv] + weights,
            [tiled(sds((rows, heads_width), BF16))] + halves,
            flops=4 * rows * tree_len * heads_width + matrix * heads_width,
            exps=rows * tree_len * heads_width // HEAD_DIM,
            limit=24,
        )
        part = slot(("attend", at), *part)
        arrivals = tp_sum(part, functools.partial(slot, ("attend half", at)))
        arrivals = slot(("attend sum", at), *arrivals)
        mixed, ffn_in = call(
            functools.partial(mix_kernel, parts=len(arrivals)),
            scal,
            (2,),
            [tiled(stream)] + [whole(a) for a in arrivals] + weights,
            [tiled(row_f32), tiled(row_bf16)],
        )
        sib_in = swap(ffn_in, "fsdp", 1)
        ffn_in, sib_in = slot(("mixed", at), ffn_in, sib_in)
        if at + 1 < layers:
            own, sib, *hidden = experts_forward(at, ffn_in, sib_in)
            own, sib = slot(("experts", at), own, sib)
        branch, gate, up = call(
            shared_kernel,
            scal,
            (2,),
            [tiled(ffn_in)] + shared_ins(at),
            [tiled(row_f32)] + [tiled(sds((rows, hid), F32))] * 2,
            flops=3 * matrix * hid,
            exps=rows * hid,
        )
        if at + 1 < layers:
            part = join(own, sib, branch)
            part = slot(("join", at), *part)
            arrivals = tp_sum(part, functools.partial(slot, ("branch half", at)))
            arrivals = slot(("branch sum", at), *arrivals)
        else:
            hidden = [ffn_in, sib_in]
        saved.append((stream, normed, query, kv, heads, mixed, ffn_in, gate, up, hidden))

    outs = Outs(scal, layers, experts, block, hid)
    packed = Packs(scal, layers, block, hid, heads_width)
    gain_sums = []
    gain_grads = [None] * (2 * layers)
    d_next, d_branch = cot, cot
    for at in reversed(range(layers)):
        stream, normed, query, kv, heads, mixed, ffn_in, gate, up, hidden = saved[at]
        weights = attention_ins(at)
        sib_d = swap(d_branch, "fsdp", 1)
        d_ffn, *g_shared = call(
            shared_back_kernel,
            scal,
            (1,),
            [whole(a) for a in (d_branch, ffn_in, gate, up)] + shared_ins(at),
            [whole(row_f32)] + [whole(sds((block, 3 * hid), BF16))] * 4,
            flops=6 * matrix * hid,
            exps=rows * hid,
        )
        sizes = PARTS[at]
        fresh = len(hidden) == 2
        part_of = lambda first, size: (
            sds((size, 3, 2 * block, hid), BF16),
            (1, 3, 2 * block, hid),
            lambda e, s: (jnp.clip(e - first, 0, size - 1), 0, 0, 0),
        )
        own, sib, *grads = call(
            functools.partial(
                expert_back_kernel, block=block, sizes=sizes, fresh=fresh,
                sources=len(routed[at])
            ),
            scal,
            (per_core,),
            [whole(d_branch), whole(sib_d), whole(tables[0]), whole(tables[1])]
            + [whole(a) if fresh else lead(a) for a in hidden]
            + expert_ins(at),
            [whole(row_f32), whole(row_bf16)]
            + [part_of(sum(sizes[:n]), size) for n, size in enumerate(sizes) for _ in range(2)]
            + [whole(row_f32), whole(row_bf16)] * fresh,
            scratch=slot_scratch * (3 if fresh else 1),
            flops=8 * expert_flops,
            exps=per_core * capacity * hid,
            limit=44,
        )
        for chunk in range(len(sizes)):
            near, far = grads[2 * chunk : 2 * chunk + 2]
            open_flow((at, chunk), expert_flow(outs, near, far, at, sum(sizes[:chunk])))
        if fresh:
            open_flow("result", result_flow(mixed, *grads[-2:], branch))
        if at == 0:
            open_flow((0, "shared"), pack_flow(functools.partial(packed.put, 0, None, True), g_shared))
        own, sib = slot((at, "experts"), own, sib)
        part = join(own, sib, d_ffn)
        part = slot((at, "join"), *part)
        arrivals = tp_sum(part, functools.partial(slot, (at, "ffn half")))
        arrivals = slot((at, "ffn sum"), *arrivals)
        d_mixed, d_attn, gain = call(
            functools.partial(mix_back_kernel, parts=len(arrivals)),
            scal,
            (2,),
            [tiled(mixed), tiled(d_next)] + [whole(a) for a in arrivals] + weights,
            [tiled(row_f32), tiled(row_bf16), whole(sds((8, width), F32))],
        )
        gain_grads[layers + at] = gain[:1]
        kv_shape = sds((rows, 2 * heads_width), BF16)
        kv_outs = [kv_shape] * 2 if ctx == 2 else [sds((tree_len, 2 * heads_width), BF16)]
        dq, g_out, *dkv = call(
            functools.partial(attend_back_kernel, parts=len(kv)),
            scal,
            (2,),
            [whole(path), tiled(query), tiled(d_attn), tiled(heads)]
            + [whole(k) for k in kv]
            + weights,
            [tiled(sds((rows, heads_width), BF16)), whole(sds((width, heads_width), BF16))]
            + [whole(k) for k in kv_outs],
            scratch=[
                pltpu.VMEM((tree_len, 2 * heads_width), F32),
                pltpu.VMEM((width, heads_width), F32),
            ],
            flops=10 * rows * tree_len * heads_width + 2 * matrix * heads_width,
            exps=rows * tree_len * heads_width // HEAD_DIM,
            limit=34,
        )
        dq, *dkv = slot((at, "attention"), dq, *dkv)
        if ctx == 2:
            kv_own, kv_got = dkv[0], swap(dkv[1], "ctx", 1)
        else:
            parts = dkv[0].reshape((ctx, rows) + dkv[0].shape[1:])
            parts = lax.all_to_all(parts, "ctx", 0, 0, tiled=True)
            kv_own, kv_got = jnp.sum(parts.astype(F32), axis=0), jnp.zeros(kv_shape.shape, F32)
        *part, g0, g1, g2, g3 = call(
            functools.partial(project_back_kernel, chunks=CHUNKS),
            scal,
            (1,),
            [whole(a) for a in (dq, kv_own, kv_got, normed, g_out)] + weights,
            halves + [whole(sds((block, PACK), BF16))] * 4,
            flops=2 * matrix * 576,
        )
        g_attention = [g0, g1, g2, g3]
        if at == 0:
            open_flow((0, "attention"), pack_flow(functools.partial(packed.put, 0, 0, False), g_attention))
        else:
            both = [jnp.concatenate(g, axis=1) for g in zip(g_shared, g_attention)]
            open_flow((at, "packs"), pack_flow(functools.partial(packed.put, at, 3 * hid, True), both))
        part = slot((at, "project"), *part)
        arrivals = tp_sum(part, functools.partial(slot, (at, "attention half")))
        arrivals = slot((at, "attention sum"), *arrivals)
        final = at == 0
        *rest, gain = call(
            functools.partial(
                input_back_kernel, parts=len(arrivals), block=block, final=final
            ),
            scal,
            (2,),
            [tiled(stream), tiled(d_mixed)] + [whole(a) for a in arrivals] + weights,
            [tiled(row_f32)] + ([] if final else [tiled(row_bf16)]) + [whole(sds((8, width), F32))],
        )
        gain_grads[at] = gain[:1]
        d_next, *rest = slot((at, "input"), *rest)
        if not final:
            (d_branch,) = rest
    gains = jnp.concatenate(gain_grads, axis=0).astype(BF16)
    cuts = [gains[:, r * block : (r + 1) * block] for r in range(4)]
    open_flow("gains", pack_flow(lambda *v: gain_sums.extend(v), cuts))
    finish("gains")
    for step in TAIL:
        finish(*step)
    gains = gain_sums[0].astype(F32) + gain_sums[1].astype(F32)
    g_sin, g_sout, g_qkv, g_attention_out = packed.held
    g_in, g_out = outs.held
    blocks = hid // 128
    g_in = g_in.reshape(layers * experts * block, blocks, 2, 128).transpose(0, 2, 1, 3)
    g_sin = g_sin.reshape(layers * block, blocks, 2, 128).transpose(0, 2, 1, 3)
    return (
        result[0][None],
        d_next[None],
        gains[:layers],
        gains[layers:],
        g_qkv.transpose(0, 2, 1, 3),
        g_attention_out,
        g_sin.reshape(layers, block, 2, hid),
        g_sout.transpose(0, 2, 1),
        g_in.reshape(layers, experts, block, 2, hid),
        g_out.transpose(0, 1, 3, 2),
    )


def solution(mesh):
    return jax.shard_map(
        shards,
        mesh=mesh,
        in_specs=(
            P("fsdp", "ctx", None),
            P("fsdp", None),
            P("fsdp", "ctx", None),
            P("fsdp", "ctx", None),
            P(None, "fsdp"),
            P(None, "fsdp"),
            P(None, "fsdp", None, "tp"),
            P(None, "tp", "fsdp"),
            P(None, "fsdp", None, "tp"),
            P(None, "tp", "fsdp"),
            P(None, None, "fsdp", None, "tp"),
            P(None, None, "tp", "fsdp"),
            P("fsdp", "ctx", None),
        ),
        out_specs=(
            P("fsdp", "ctx", None),
            P("fsdp", "ctx", None),
            P(None, "fsdp"),
            P(None, "fsdp"),
            P(None, "fsdp", None, "tp"),
            P(None, "tp", "fsdp"),
            P(None, "fsdp", None, "tp"),
            P(None, "tp", "fsdp"),
            P(None, None, "fsdp", None, "tp"),
            P(None, None, "tp", "fsdp"),
        ),
        check_vma=False,
    )
```
